512 devices in a mesh: seq: 16 (over y_lo, z), clus: 32 (over x, y_hi, core).
Axes of the slice: x: 4, y: 8 (y_hi: 4, y_lo: 2; y = y_hi * 2 + y_lo), z: 8, core: 2. Of those that a mesh axis runs over, the one named last changes fastest.
Arguments:
- node_feats: bfloat16 [32, 2048, 1024], P('clus', 'seq'), may hold values from -24 to 24
- qkv_weight: bfloat16 [3072, 1024], P('seq'), may hold values from -1 to 1
- block_pairs: int32 [32, 128, 2], P('clus'), may hold values from 0 to 15, as said below
- grad_out: bfloat16 [32, 2048, 1024], P('clus', 'seq'), may hold values from -6 to 6
Outputs:
- attended: bfloat16 [32, 2048, 1024], P('clus', 'seq')
- node_grad: bfloat16 [32, 2048, 1024], P('clus', 'seq')
- weight_grad: float32 [3072, 1024], P('seq')
The draws below stay inside these ranges and needn't reach their ends.
Inputs may be any that keep to these rules, and one draw needn't show every extreme that they name: `block_pairs`: each cluster's list holds 128 distinct pairs, among them (b, b) for every block b.
All inputs are finite; a program needn't handle non-finite values.
Results may differ from the reference program's by a relative error of at most 0.023.
Values may be sent and summed in bfloat16 or wider, within the bound.
A program may use at most 64 MiB of HBM per device.

```python
import jax
import jax.numpy as jnp
from jax import lax

D = 1024
H = 16
HD = 64
BLOCK = 128
NODES = 2048
CLUSTERS = 32
NB = 16
PAIRS = 128
N_SEQ = 16
N_CLUS = 32


def draw_node_feats(key, part):
    key_base = jax.random.fold_in(key, 0)
    return jnp.clip(jax.random.normal(key_base, (CLUSTERS, NODES, D), jnp.float32), -5.0, 5.0).astype(jnp.bfloat16)


def draw_qkv_weight(key, part):
    key_query, key_keys, key_values = jax.random.split(key, 3)
    shape_one = (D, H, 1, HD)
    query_part = jnp.clip(jax.random.normal(key_query, shape_one, jnp.float32), -4.0, 4.0) / D ** 0.5
    keys_part = jnp.clip(jax.random.normal(key_keys, shape_one, jnp.float32), -4.0, 4.0) / D ** 0.5
    values_part = jnp.clip(jax.random.normal(key_values, shape_one, jnp.float32), -4.0, 4.0) / D ** 0.5
    return jnp.concatenate([query_part, keys_part, values_part], axis=2).reshape(D, 3 * D).T.astype(jnp.bfloat16)


def draw_block_pairs(key, part):

    def one_cluster(cluster_key):
        key_noise, key_skew, key_order = jax.random.split(cluster_key, 3)
        random_part = jax.random.randint(key_noise, (NB, NB), 0, 16384)
        skewed = jax.random.randint(key_skew, (NB, 1), 0, 4) * 8192
        position = jnp.arange(NB * NB, dtype=jnp.int32).reshape(NB, NB)
        ranking = (random_part + skewed) * 32768 + position
        diagonal = jnp.arange(NB)[:, None] == jnp.arange(NB)[None, :]
        ranking = jnp.where(diagonal, -1, ranking).reshape(-1)
        chosen = lax.top_k(ranking, PAIRS - NB)[1].astype(jnp.int32)
        rows_all = jnp.concatenate([jnp.arange(NB, dtype=jnp.int32), chosen // NB])
        cols_all = jnp.concatenate([jnp.arange(NB, dtype=jnp.int32), chosen % NB])
        listed = jnp.stack([rows_all, cols_all], axis=1)
        shuffle = jax.random.permutation(key_order, PAIRS)
        return listed[shuffle]
    return jax.vmap(one_cluster)(jax.random.split(key, CLUSTERS))


def steps_of(stream_key, extent, shards, low, high):
    def one(dim, parts):
        heights = jax.random.uniform(jax.random.fold_in(jax.random.fold_in(stream_key, 6), dim), (parts,), jnp.float32, low / len(shards), high / len(shards))
        return jnp.repeat(jnp.exp(heights), extent[dim] // parts).reshape((-1,) + (1,) * (len(extent) - dim - 1))

    loudness = one(*shards[0])
    for cut in shards[1:]:
        loudness = loudness * one(*cut)
    return loudness


def normal_values(key, dims, spread, limit, cuts=(), held_as=jnp.bfloat16):
    drawn = jax.random.normal(key, dims, jnp.float32) * spread
    if len(cuts) > 0:
        drawn = steps_of(key, dims, cuts, -0.22, 0.18) * drawn
    return jnp.clip(drawn, min=-limit, max=limit).astype(held_as)


def setup_inputs(seed: int = 0) -> dict:
    splits = jax.random.split(jax.random.key(seed), 5)
    node_feats = draw_node_feats(jax.random.fold_in(splits[4], 71), 0)
    qkv_weight = draw_qkv_weight(jax.random.fold_in(splits[4], 71), 0)
    block_pairs = draw_block_pairs(jax.random.fold_in(splits[4], 71), 0)
    grad_out = normal_values(splits[3], (CLUSTERS, NODES, D), 1.0, 6.0, ((0, 32), (1, 16)))
    return {"node_feats": node_feats, "qkv_weight": qkv_weight, "block_pairs": block_pairs, "grad_out": grad_out}


def block_allowed(listed, blocks):
    block_ids = jnp.arange(blocks, dtype=jnp.int32)[None, :]
    row_hot = (listed[:, 0:1] == block_ids).astype(jnp.float32)
    col_hot = (listed[:, 1:2] == block_ids).astype(jnp.float32)
    counts = jnp.dot(row_hot.T, col_hot, precision=lax.Precision.HIGHEST)
    return counts > 0.5


def one_head(projected, upstream, allowed, head_index):
    node_count = projected.shape[0]
    grouped = projected.reshape(node_count, H, 3, HD)
    chosen = lax.dynamic_index_in_dim(grouped, head_index, 1, keepdims=False)
    queries = chosen[:, 0]
    keys_all = chosen[:, 1]
    values_all = chosen[:, 2]
    grad_rows = lax.dynamic_index_in_dim(upstream.reshape(node_count, H, HD), head_index, 1, keepdims=False)
    scores = jnp.dot(queries, keys_all.T, preferred_element_type=jnp.float32) * (HD ** -0.5)
    scores = jnp.where(allowed, scores, -jnp.inf)
    row_max = jnp.max(scores, axis=-1, keepdims=True)
    unnorm = jnp.where(allowed, jnp.exp(scores - row_max), 0.0)
    weights = unnorm / jnp.sum(unnorm, axis=-1, keepdims=True)
    weights_low = weights.astype(jnp.bfloat16)
    head_out = jnp.dot(weights_low, values_all, preferred_element_type=jnp.float32).astype(jnp.bfloat16)
    grad_weights = jnp.dot(grad_rows, values_all.T, preferred_element_type=jnp.float32)
    row_delta = jnp.sum(weights * grad_weights, axis=-1, keepdims=True)
    grad_scores = (weights * (grad_weights - row_delta) * (HD ** -0.5)).astype(jnp.bfloat16)
    grad_query = jnp.dot(grad_scores, keys_all, preferred_element_type=jnp.float32).astype(jnp.bfloat16)
    grad_keys = jnp.dot(grad_scores.T, queries, preferred_element_type=jnp.float32).astype(jnp.bfloat16)
    grad_values = jnp.dot(weights_low.T, grad_rows, preferred_element_type=jnp.float32).astype(jnp.bfloat16)
    return head_out, jnp.stack([grad_query, grad_keys, grad_values], axis=1)


def reference(node_feats, qkv_weight, block_pairs, grad_out):
    def one_cluster(running, inputs):
        features, listed, upstream = inputs
        node_count = features.shape[0]
        projected = lax.dot_general(features, qkv_weight, (((1,), (1,)), ((), ())), preferred_element_type=jnp.float32).astype(jnp.bfloat16)
        allowed_blocks = block_allowed(listed, node_count // BLOCK)
        allowed = jnp.repeat(jnp.repeat(allowed_blocks, BLOCK, axis=0), BLOCK, axis=1)
        heads_out, head_grads = lax.map(lambda head_index: one_head(projected, upstream, allowed, head_index), jnp.arange(H))
        attended = jnp.transpose(heads_out, (1, 0, 2)).reshape(node_count, D)
        grad_proj = jnp.transpose(head_grads, (1, 0, 2, 3)).reshape(node_count, 3 * D)
        group_cols = 3 * D // N_SEQ
        summed = jnp.zeros((node_count, D), jnp.float32)
        for group_index in range(N_SEQ):
            lower = group_index * group_cols
            upper = lower + group_cols
            group_term = jnp.dot(grad_proj[:, lower:upper], qkv_weight[lower:upper, :], preferred_element_type=jnp.float32).astype(jnp.bfloat16)
            summed = summed + lax.optimization_barrier(group_term).astype(jnp.float32)
        node_grad = summed.astype(jnp.bfloat16)
        running = running + lax.dot_general(grad_proj, features, (((0,), (0,)), ((), ())), preferred_element_type=jnp.float32)
        return running, (attended, node_grad)

    initial = jnp.zeros((3 * D, D), jnp.float32)
    summed_w, outputs = lax.scan(one_cluster, initial, (node_feats, block_pairs, grad_out))
    return outputs[0], outputs[1], summed_w / N_CLUS
```

```python
import jax
import jax.numpy as jnp
from jax import lax
from jax.experimental import pallas as pl
from jax.experimental.pallas import tpu as pltpu
from jax.sharding import PartitionSpec as P

F32 = jnp.float32
BF = jnp.bfloat16
HD = 64
BLOCK = 128
NB = 16
CH = 4
ROWS = CH * BLOCK
PAD = -1e30


def attn_kernel(pairs, b1, b2, kv, kvt, ot, dproj, cols, cnt, s_scr, d_scr, acc):
    npairs = pairs.shape[0] // 2

    def clear(t, _):
        cols[t] = 0
        return 0

    lax.fori_loop(0, NB * NB, clear, 0)

    def clear_cnt(t, _):
        cnt[t] = 0
        return 0

    lax.fori_loop(0, NB, clear_cnt, 0)

    def put(t, _):
        r = pairs[2 * t]
        n = cnt[r]
        cols[r * NB + n] = pairs[2 * t + 1]
        cnt[r] = n + 1
        return 0

    lax.fori_loop(0, npairs, put, 0)
    acc[...] = jnp.zeros_like(acc)

    def row(i, _):
        n = cnt[i]
        nch = (n + CH - 1) // CH
        w1 = b1[i]
        w2 = b2[i]

        def pass1(c, m):
            for t in range(CH):
                slot = c * CH + t
                j = cols[i * NB + slot]
                blk = kv[pl.ds(pl.multiple_of(j * BLOCK, BLOCK), BLOCK), :]
                sd = jnp.dot(blk, w1, preferred_element_type=F32)
                bias = jnp.where(slot < n, 0.0, PAD).astype(F32)
                s = sd[:, :BLOCK] + bias
                at = pl.ds(pl.multiple_of(slot * BLOCK, BLOCK), BLOCK)
                s_scr[at, :] = s
                d_scr[at, :] = sd[:, BLOCK:]
                m = jnp.maximum(m, jnp.max(s.reshape(16, 8, BLOCK), axis=0))
            return m

        m = lax.fori_loop(0, nch, pass1, jnp.full((8, BLOCK), PAD, F32))
        m = jnp.max(m, axis=0, keepdims=True)

        def pass2(c, carry):
            l, d = carry
            at = pl.ds(pl.multiple_of(c * ROWS, ROWS), ROWS)
            e = jnp.exp((s_scr[at, :] - m) * 0.125)
            s_scr[at, :] = e
            l = l + jnp.sum(e.reshape(ROWS // 8, 8, BLOCK), axis=0)
            d = d + jnp.sum((e * d_scr[at, :]).reshape(ROWS // 8, 8, BLOCK), axis=0)
            return l, d

        zero = jnp.zeros((8, BLOCK), F32)
        l, d = lax.fori_loop(0, nch, pass2, (zero, zero))
        linv = 1.0 / jnp.sum(l, axis=0, keepdims=True)
        delta = jnp.sum(d, axis=0, keepdims=True) * linv
        lscale = linv * 0.125

        def pass3(c, oq):
            at = pl.ds(pl.multiple_of(c * ROWS, ROWS), ROWS)
            e = s_scr[at, :]
            p = (e * linv).astype(BF)
            ds = (e * lscale * (d_scr[at, :] - delta)).astype(BF)
            cat = jnp.concatenate([ds, p], axis=1)
            lhs = jnp.concatenate(
                [
                    kvt[:, pl.ds(pl.multiple_of(cols[i * NB + c * CH + t] * BLOCK, BLOCK), BLOCK)]
                    for t in range(CH)
                ],
                axis=1,
            )
            oq = oq + jnp.dot(lhs, cat, preferred_element_type=F32)
            g = jnp.dot(cat, w2, preferred_element_type=F32)
            for t in range(CH):
                j = cols[i * NB + c * CH + t]
                aj = pl.ds(pl.multiple_of(j * BLOCK, BLOCK), BLOCK)
                acc[aj, :] += g[t * BLOCK : (t + 1) * BLOCK]
            return oq

        oq = lax.fori_loop(0, nch, pass3, jnp.zeros((BLOCK, 2 * BLOCK), F32))
        here = pl.ds(pl.multiple_of(i * BLOCK, BLOCK), BLOCK)
        ot[i] = oq[HD:, BLOCK:].astype(BF)
        dproj[here, 0:BLOCK] = oq[:, :BLOCK].T.astype(BF)
        return 0

    lax.fori_loop(0, NB, row, 0)

    def fin(i, _):
        here = pl.ds(pl.multiple_of(i * BLOCK, BLOCK), BLOCK)
        a = acc[here, :].astype(BF)
        q = dproj[here, 0:BLOCK]
        dproj[here, :] = jnp.concatenate([q[:, :HD], a], axis=1)
        return 0

    lax.fori_loop(0, NB, fin, 0)


def attention(pairs, b1, b2, kv, kvt):
    vm = pl.BlockSpec(memory_space=pltpu.VMEM)
    n = kv.shape[0]
    return pl.pallas_call(
        attn_kernel,
        out_shape=(
            jax.ShapeDtypeStruct((NB, HD, BLOCK), BF),
            jax.ShapeDtypeStruct((n, 3 * HD), BF),
        ),
        in_specs=[pl.BlockSpec(memory_space=pltpu.SMEM), vm, vm, vm, vm],
        out_specs=(vm, vm),
        scratch_shapes=[
            pltpu.SMEM((NB * NB,), jnp.int32),
            pltpu.SMEM((NB,), jnp.int32),
            pltpu.VMEM((n, BLOCK), F32),
            pltpu.VMEM((n, BLOCK), F32),
            pltpu.VMEM((n, BLOCK), F32),
        ],
        compiler_params=pltpu.CompilerParams(vmem_limit_bytes=40 * 1024 * 1024),
        name="attention",
    )(pairs, b1, b2, kv, kvt)

MESH = pl.DeviceIdType.MESH
HD = 64
BLOCK = 128
NB = 16
NZ = 8
D = 1024
HALF = 64
QUART = 32
CORES = 2
NX = 4
NY = 4


def dot_t(a, b):
    return lax.dot_general(a, b, (((1,), (1,)), ((), ())), preferred_element_type=F32)


def ring_place():
    s = lax.axis_index("seq")
    y = lax.div(s, NZ)
    z = lax.rem(s, NZ)
    return s, y, z


def greet(peers):
    barrier = pltpu.get_barrier_semaphore()
    for peer in peers:
        pl.semaphore_signal(barrier, inc=1, device_id=peer, device_id_type=MESH)
    pl.semaphore_wait(barrier, len(peers))


def gather_kernel(
    x, w, g, xall, b1, b2, kv, kvt, xg, gsend, grecv, sz, rz, sy, ry, sg, rg, lx, ll
):
    s, y, z = ring_place()
    p = 1 - y
    up = {"seq": y * NZ + lax.rem(z + 1, NZ)}
    down = {"seq": y * NZ + lax.rem(z + NZ - 1, NZ)}
    across = {"seq": p * NZ + z}
    load = pltpu.make_async_copy(x.at[0], xg.at[s], ll)
    load.start()
    greet([{"seq": lax.rem(s + d, NB)} for d in range(1, NB)])
    load.wait()

    def block(col, off):
        return col * NZ + lax.rem(z + off + NZ, NZ)

    def zmsg(flow, k, off, do_start):
        col = p if flow >= 4 else y
        part = 0 if flow < 2 else HALF
        rows = HALF
        if k == 3:
            rows = QUART
            part = part + (QUART if flow % 2 else 0)
        ref = xg.at[block(col, off), pl.ds(part, rows)]
        c = pltpu.make_async_remote_copy(
            src_ref=ref,
            dst_ref=ref,
            send_sem=sz.at[flow, k],
            recv_sem=rz.at[flow, k],
            device_id=down if flow % 2 else up,
            device_id_type=MESH,
        )
        if do_start:
            c.start()
        return c

    def ymsg(idx, col, do_start):
        off = 0 if idx == 8 else idx
        ref = xg.at[block(col, off), pl.ds(HALF if idx == 8 else 0, HALF)]
        c = pltpu.make_async_remote_copy(
            src_ref=ref,
            dst_ref=ref,
            send_sem=sy.at[idx],
            recv_sem=ry.at[idx],
            device_id=across,
            device_id_type=MESH,
        )
        if do_start:
            c.start()
        return c

    sent = []
    outs = []
    sent.append(ymsg(8, y, True))
    for flow in (2, 3, 0, 1):
        sent.append(zmsg(flow, 0, 0, True))
    sent.append(ymsg(0, y, True))

    def compute(b, n):
        xb = xg[b]
        at = pl.ds(pl.multiple_of(b * BLOCK, BLOCK), BLOCK)
        kvf = dot_t(xb, w[HD:, :])
        qt = dot_t(w[:HD, :], xb)
        zero = jnp.zeros((HD, BLOCK), F32)
        kv[at, :] = kvf.astype(BF)
        kvt[:, at] = kvf.T.astype(BF)
        b1[b, :HD, :] = jnp.concatenate([qt, zero], axis=1).astype(BF)
        b2[b, :BLOCK, :] = jnp.concatenate([qt, zero], axis=0).T.astype(BF)
        c = pltpu.make_async_copy(xg.at[b], xall.at[b], lx.at[n])
        c.start()
        outs.append(c)

    for c in range(NB // 2):
        t = g[0, :, c * BLOCK : (c + 1) * BLOCK].astype(F32).T.astype(BF)
        gsend[2 * c] = t[:HD]
        gsend[2 * c + 1] = t[HD:]

    def gmsg(d):
        to = lax.rem(s + d, NB)
        return pltpu.make_async_remote_copy(
            src_ref=gsend.at[to],
            dst_ref=grecv.at[s],
            send_sem=sg.at[d - 1],
            recv_sem=rg.at[d - 1],
            device_id={"seq": to},
            device_id_type=MESH,
        )

    compute(s, 0)
    ymsg(8, p, False).wait_recv()
    for flow in (4, 5):
        sent.append(zmsg(flow, 0, 0, True))
    for d in range(1, NB):
        c = gmsg(d)
        c.start()
        sent.append(c)
    grecv[s] = gsend[s]

    n = 1
    for k in range(4):
        for flow in (2, 3, 0, 1, 4, 5):
            off = (k + 1) if flow % 2 else -(k + 1)
            zmsg(flow, k, off, False).wait_recv()
            if k < 3:
                sent.append(zmsg(flow, k + 1, off, True))
            if flow < 2 and k < 3:
                sent.append(ymsg(off % NZ, y, True))
            if flow == 1 and k == 3:
                sent.append(ymsg(4, y, True))
        for off in [-(k + 1), k + 1][: 2 if k < 3 else 1]:
            compute(block(y, off), n)
            n += 1
        for off in [-k, k][: 2 if k > 0 else 1]:
            ymsg(off % NZ, p, False).wait_recv()
            compute(block(p, off), n)
            n += 1
    ymsg(4, p, False).wait_recv()
    compute(block(p, 4), n)
    for d in range(1, NB):
        frm = lax.rem(s + NB - d, NB)
        pltpu.make_async_remote_copy(
            src_ref=gsend.at[s],
            dst_ref=grecv.at[frm],
            send_sem=sg.at[d - 1],
            recv_sem=rg.at[d - 1],
            device_id={"seq": frm},
            device_id_type=MESH,
        ).wait_recv()

    def place(t, _):
        gt = grecv[t].astype(F32)
        zero = jnp.zeros((HD, BLOCK), F32)
        b1[t, HD:, :] = jnp.concatenate([zero, gt], axis=1).astype(BF)
        b2[t, BLOCK:, :] = jnp.concatenate([zero, gt], axis=0).T.astype(BF)
        return 0

    lax.fori_loop(0, NB, place, 0)
    for c in sent:
        c.wait_send()
    for c in outs:
        c.wait()


def gather(x, w, g):
    vm = pl.BlockSpec(memory_space=pltpu.VMEM)
    anyw = pl.BlockSpec(memory_space=pl.ANY)
    n = NB * BLOCK
    sem = pltpu.SemaphoreType.DMA
    return pl.pallas_call(
        gather_kernel,
        out_shape=(
            jax.ShapeDtypeStruct((NB, BLOCK, D), BF),
            jax.ShapeDtypeStruct((NB, BLOCK, 2 * BLOCK), BF),
            jax.ShapeDtypeStruct((NB, 2 * BLOCK, BLOCK), BF),
            jax.ShapeDtypeStruct((n, BLOCK), BF),
            jax.ShapeDtypeStruct((BLOCK, n), BF),
        ),
        in_specs=[anyw, vm, vm],
        out_specs=(anyw, vm, vm, vm, vm),
        scratch_shapes=[
            pltpu.VMEM((NB, BLOCK, D), BF),
            pltpu.VMEM((NB, HD, BLOCK), BF),
            pltpu.VMEM((NB, HD, BLOCK), BF),
            sem((6, 4)),
            sem((6, 4)),
            sem((9,)),
            sem((9,)),
            sem((NB - 1,)),
            sem((NB - 1,)),
            sem((NB,)),
            sem,
        ],
        compiler_params=pltpu.CompilerParams(
            collective_id=0, has_side_effects=True, vmem_limit_bytes=40 * 1024 * 1024
        ),
        name="gather_project",
    )(x, w, g)


def scatter_kernel(
    dproj, w, ot, xall,
    att, ng, wg,
    xv, zs, zr, ysb, yrb, arecv, dt, dwf, cs, cr, xs, xr, hs, hr, fs, fo, fsib,
    sz, rz, sy, ry, sa, ra, sc, rc, sx, rx, sh, rh, sf, rf, lx,
):
    s, y, z = ring_place()
    p = 1 - y
    up = {"seq": y * NZ + lax.rem(z + 1, NZ)}
    down = {"seq": y * NZ + lax.rem(z + NZ - 1, NZ)}
    across = {"seq": p * NZ + z}
    q = lax.axis_index("clus")
    cx = lax.div(q, NY * CORES)
    ch = lax.rem(lax.div(q, CORES), NY)
    cc = lax.rem(q, CORES)
    sib = {"clus": q + 1 - 2 * cc}

    def xpeer(d):
        return {"clus": lax.rem(cx + d, NX) * (NY * CORES) + ch * CORES + cc}

    def hpeer(d):
        return {"clus": cx * (NY * CORES) + lax.rem(ch + d, NY) * CORES + cc}

    load = pltpu.make_async_copy(xall, xv, lx)
    load.start()
    greet(
        [{"seq": lax.rem(s + d, NB)} for d in range(1, NB)]
        + [sib]
        + [xpeer(d) for d in range(1, NX)]
        + [hpeer(d) for d in range(1, NY)]
    )

    def block(col, off):
        return col * NZ + lax.rem(z + off + NZ, NZ)

    def part(col, off, first, rows):
        b = block(col, off)
        at = pl.ds(pl.multiple_of(b * BLOCK + first, QUART), rows)
        return jnp.dot(dproj[at, :], w[...], preferred_element_type=F32)

    sent = []

    def rcopy(src, dst, ss, rs, dev):
        return pltpu.make_async_remote_copy(
            src_ref=src, dst_ref=dst, send_sem=ss, recv_sem=rs,
            device_id=dev, device_id_type=MESH,
        )

    def span(flow, k):
        if k == 0:
            return pl.ds(QUART if flow % 2 else 0, QUART)
        return pl.ds(0, HALF)

    def zmsg(flow, k):
        at = span(flow, k)
        return rcopy(
            zs.at[flow, k, at], zr.at[flow, k, at], sz.at[flow, k], rz.at[flow, k],
            down if flow % 2 else up,
        )

    def ymsg(idx):
        return rcopy(ysb.at[idx], yrb.at[idx], sy.at[idx], ry.at[idx], across)

    def go(c):
        c.start()
        sent.append(c)

    def zstep(flow, k):
        col = p if flow >= 4 else y
        base = 0 if flow < 2 else HALF
        off = (4 - k) * (-1 if flow % 2 else 1)
        if k == 0:
            lo = QUART if flow % 2 else 0
            val = part(col, off, base + lo, QUART)
            if flow < 2:
                val = val + yrb[off % NZ, lo : lo + QUART, :].astype(F32)
            zs[flow, 0, lo : lo + QUART, :] = val.astype(BF)
        else:
            val = part(col, off, base, HALF)
            if flow < 2:
                val = val + yrb[off % NZ].astype(F32)
            zmsg(flow, k - 1).wait_recv()
            if k == 1:
                lo = QUART if flow % 2 else 0
                zs[flow, 1, QUART - lo : HALF - lo, :] = val[QUART - lo : HALF - lo].astype(BF)
                zs[flow, 1, lo : lo + QUART, :] = (
                    val[lo : lo + QUART] + zr[flow, 0, lo : lo + QUART, :].astype(F32)
                ).astype(BF)
            else:
                zs[flow, k] = (val + zr[flow, k - 1].astype(F32)).astype(BF)
        go(zmsg(flow, k))

    def ysend(off):
        ysb[off % NZ] = part(p, off, 0, HALF).astype(BF)
        go(ymsg(off % NZ))

    for flow in (2, 3):
        zstep(flow, 0)
    ysend(4)
    for flow in (4, 5):
        zstep(flow, 0)
    ysend(3)
    ysend(-3)
    for d in range(1, NB):
        to = lax.rem(s + d, NB)
        go(rcopy(ot.at[to], arecv.at[s], sa.at[d - 1], ra.at[d - 1], {"seq": to}))
    arecv[s] = ot[s]

    def turn(t, _):
        at = pl.ds(pl.multiple_of(t * BLOCK, BLOCK), BLOCK)
        v = jnp.concatenate([dproj[at, :].astype(F32), jnp.zeros((BLOCK, HD), F32)], axis=1)
        dt[:, at] = v.T[: 3 * HD].astype(BF)
        return 0

    def wstep(t, _):
        at = pl.ds(pl.multiple_of(t * 256, 256), 256)
        dwf[:, at] = jnp.dot(dt[...], xv[:, at], preferred_element_type=F32)
        return 0

    hrow = 3 * HD // CORES
    mine = pl.ds(pl.multiple_of(cc * hrow, QUART), hrow)
    other = pl.ds(pl.multiple_of((1 - cc) * hrow, QUART), hrow)
    wide = D // NX

    def stage0():
        lax.fori_loop(0, NB, turn, 0)
        load.wait()
        lax.fori_loop(0, D // 256, wstep, 0)
        cs[...] = dwf[other, :].astype(BF)
        go(rcopy(cs, cr, sc.at[0], rc.at[0], sib))

    def stage1():
        rcopy(cs, cr, sc.at[0], rc.at[0], sib).wait_recv()
        v = dwf[mine, :] + cr[...].astype(F32)
        for t in range(NX):
            xs[t] = v[:, t * wide : (t + 1) * wide].astype(BF)
        xr[cx] = xs[cx]
        for d in range(1, NX):
            go(rcopy(xs.at[lax.rem(cx + d, NX)], xr.at[cx], sx.at[d - 1], rx.at[d - 1], xpeer(d)))

    def stage2():
        for d in range(1, NX):
            frm = lax.rem(cx + NX - d, NX)
            rcopy(xs.at[cx], xr.at[frm], sx.at[d - 1], rx.at[d - 1], xpeer(d)).wait_recv()
        v = xr[0].astype(F32) + xr[1].astype(F32) + xr[2].astype(F32) + xr[3].astype(F32)
        hs[...] = v.astype(BF)
        hr[ch] = v.astype(BF)
        for d in range(1, NY):
            go(rcopy(hs, hr.at[ch], sh.at[d - 1], rh.at[d - 1], hpeer(d)))

    def stage3():
        for d in range(1, NY):
            frm = lax.rem(ch + NY - d, NY)
            rcopy(hs, hr.at[frm], sh.at[d - 1], rh.at[d - 1], hpeer(d)).wait_recv()
        v = hr[0].astype(F32) + hr[1].astype(F32) + hr[2].astype(F32) + hr[3].astype(F32)
        fs[...] = v.astype(BF)
        fo[cx] = v.astype(BF)
        for d in range(1, NX):
            go(rcopy(fs, fo.at[cx], sf.at[d - 1], rf.at[d - 1], xpeer(d)))

    def stage4():
        for d in range(1, NX):
            frm = lax.rem(cx + NX - d, NX)
            rcopy(fs, fo.at[frm], sf.at[d - 1], rf.at[d - 1], xpeer(d)).wait_recv()
        go(rcopy(fo, fsib, sc.at[1], rc.at[1], sib))

    def stage5():
        rcopy(fo, fsib, sc.at[1], rc.at[1], sib).wait_recv()
        for t in range(NX):
            at = pl.ds(t * wide, wide)
            wg[mine, at] = fo[t].astype(F32) * (1.0 / (NX * NY * CORES))
            wg[other, at] = fsib[t].astype(F32) * (1.0 / (NX * NY * CORES))

    def asteps(k):
        if k == 0:
            ymsg(4).wait_recv()
        else:
            ymsg((4 - k) % NZ).wait_recv()
            ymsg((k - 4) % NZ).wait_recv()
        zstep(0, k)
        zstep(1, k)

    stage0()
    asteps(0)
    for flow in (2, 3, 4, 5):
        zstep(flow, 1)
    ysend(2)
    ysend(-2)
    asteps(1)
    stage1()
    for flow in (2, 3, 4, 5):
        zstep(flow, 2)
    ysend(1)
    ysend(-1)
    asteps(2)
    stage2()
    for flow in (4, 5, 2, 3):
        zstep(flow, 3)
    ysend(0)
    asteps(3)
    stage3()

    def total(flow, col, base):
        val = part(col, 0, base, HALF)
        for f in (flow, flow + 1):
            zmsg(f, 3).wait_recv()
            val = val + zr[f, 3].astype(F32)
        return val

    ysb[8] = total(4, p, HALF).astype(BF)
    go(ymsg(8))
    stage4()
    own_b = total(2, y, HALF)
    ymsg(0).wait_recv()
    ng[0, :HALF, :] = (total(0, y, 0) + yrb[0].astype(F32)).astype(BF)
    for d in range(1, NB):
        frm = lax.rem(s + NB - d, NB)
        rcopy(ot.at[s], arecv.at[frm], sa.at[d - 1], ra.at[d - 1], {"seq": frm}).wait_recv()
    for c in range(NB // 2):
        t = jnp.concatenate([arecv[2 * c], arecv[2 * c + 1]], axis=0).astype(F32)
        att[0, :, c * BLOCK : (c + 1) * BLOCK] = t.T.astype(BF)
    stage5()
    ymsg(8).wait_recv()
    ng[0, HALF:, :] = (own_b + yrb[8].astype(F32)).astype(BF)
    for c in sent:
        c.wait_send()


def scatter(dproj, w, ot, xall):
    vm = pl.BlockSpec(memory_space=pltpu.VMEM)
    anyw = pl.BlockSpec(memory_space=pl.ANY)
    n = NB * BLOCK
    sem = pltpu.SemaphoreType.DMA
    vmem = pltpu.VMEM
    hrow = 3 * HD // CORES
    wide = D // NX
    return pl.pallas_call(
        scatter_kernel,
        out_shape=(
            jax.ShapeDtypeStruct((1, BLOCK, D), BF),
            jax.ShapeDtypeStruct((1, BLOCK, D), BF),
            jax.ShapeDtypeStruct((3 * HD, D), F32),
        ),
        in_specs=[vm, vm, vm, anyw],
        out_specs=(vm, vm, vm),
        scratch_shapes=[
            vmem((n, D), BF),
            vmem((6, 4, HALF, D), BF),
            vmem((6, 4, HALF, D), BF),
            vmem((9, HALF, D), BF),
            vmem((9, HALF, D), BF),
            vmem((NB, HD, BLOCK), BF),
            vmem((3 * HD, n), BF),
            vmem((3 * HD, D), F32),
            vmem((hrow, D), BF),
            vmem((hrow, D), BF),
            vmem((NX, hrow, wide), BF),
            vmem((NX, hrow, wide), BF),
            vmem((hrow, wide), BF),
            vmem((NY, hrow, wide), BF),
            vmem((hrow, wide), BF),
            vmem((NX, hrow, wide), BF),
            vmem((NX, hrow, wide), BF),
            sem((6, 4)),
            sem((6, 4)),
            sem((9,)),
            sem((9,)),
            sem((NB - 1,)),
            sem((NB - 1,)),
            sem((2,)),
            sem((2,)),
            sem((NX - 1,)),
            sem((NX - 1,)),
            sem((NY - 1,)),
            sem((NY - 1,)),
            sem((NX - 1,)),
            sem((NX - 1,)),
            sem,
        ],
        compiler_params=pltpu.CompilerParams(
            collective_id=1, has_side_effects=True, vmem_limit_bytes=60 * 1024 * 1024
        ),
        name="scatter_reduce",
    )(dproj, w, ot, xall)


def local(node_feats, qkv_weight, block_pairs, grad_out):
    xall, b1, b2, kv, kvt = gather(node_feats, qkv_weight, grad_out)
    ot, dproj = attention(block_pairs.reshape(-1), b1, b2, kv, kvt)
    return scatter(dproj, qkv_weight, ot, xall.reshape(NB * BLOCK, D))


def solution(mesh):
    return jax.shard_map(
        local,
        mesh=mesh,
        in_specs=(
            P("clus", "seq", None),
            P("seq", None),
            P("clus", None, None),
            P("clus", "seq", None),
        ),
        out_specs=(P("clus", "seq", None), P("clus", "seq", None), P("seq", None)),
        check_vma=False,
    )
```

```python
import math

import jax
import jax.numpy as jnp
from jax import lax
from jax.experimental import pallas as pl
from jax.experimental.pallas import tpu as pltpu
from jax.sharding import PartitionSpec as P

F32 = jnp.float32
BF = jnp.bfloat16
HD = 64
BLOCK = 128
NB = 16
CH = 4
ROWS = CH * BLOCK
PAD = -1e30
COUNT = 16
ROWID = 17
SCALE = 0.125 * math.log2(math.e)


def attn_kernel(lst, b1, b2, kv, kvt, ot, dproj, s_scr, d_scr, acc):
    acc[...] = jnp.zeros_like(acc)

    def at_block(j):
        return pl.ds(pl.multiple_of(j * BLOCK, BLOCK), BLOCK)

    def at_chunk(c):
        return pl.ds(pl.multiple_of(c * ROWS, ROWS), ROWS)

    def chunks(r):
        return lax.div(lst[r, COUNT] + (CH - 1), CH)

    def scores(r, c, buf, w1, m):
        n = lst[r, COUNT]
        lhs = jnp.concatenate([kv[at_block(lst[r, c * CH + t]), :] for t in range(CH)], axis=0)
        sd = jnp.dot(lhs, w1, preferred_element_type=F32)
        s = jnp.concatenate(
            [
                sd[t * BLOCK : (t + 1) * BLOCK, :BLOCK]
                + jnp.where(c * CH + t < n, 0.0, PAD).astype(F32)
                for t in range(CH)
            ],
            axis=0,
        )
        s_scr[buf, at_chunk(c), :] = s
        d_scr[buf, at_chunk(c), :] = sd[:, BLOCK:]
        return jnp.maximum(m, jnp.max(s.reshape(ROWS // 8, 8, BLOCK), axis=0))

    def weigh(r, buf, m):
        m = jnp.max(m, axis=0, keepdims=True)

        def step(c, carry):
            l, d = carry
            e = jnp.exp2((s_scr[buf, at_chunk(c), :] - m) * SCALE)
            s_scr[buf, at_chunk(c), :] = e
            l = l + jnp.sum(e.reshape(ROWS // 8, 8, BLOCK), axis=0)
            ed = e * d_scr[buf, at_chunk(c), :]
            d = d + jnp.sum(ed.reshape(ROWS // 8, 8, BLOCK), axis=0)
            return l, d

        zero = jnp.zeros((8, BLOCK), F32)
        l, d = lax.fori_loop(0, chunks(r), step, (zero, zero))
        linv = 1.0 / jnp.sum(l, axis=0, keepdims=True)
        return linv, jnp.sum(d, axis=0, keepdims=True) * linv

    def gradients(r, c, buf, w2, linv, delta, oq):
        e = s_scr[buf, at_chunk(c), :]
        p = e * linv
        ds = p * ((d_scr[buf, at_chunk(c), :] - delta) * 0.125)
        cat = jnp.concatenate([ds.astype(BF), p.astype(BF)], axis=1)
        cols = [lst[r, c * CH + t] for t in range(CH)]
        lhs = jnp.concatenate([kvt[:, at_block(j)] for j in cols], axis=1)
        oq = oq + jnp.dot(lhs, cat, preferred_element_type=F32)
        g = jnp.dot(cat, w2, preferred_element_type=F32)
        for t in range(CH):
            acc[at_block(cols[t]), :] += g[t * BLOCK : (t + 1) * BLOCK]
        return oq

    low = jnp.full((8, BLOCK), PAD, F32)
    first = b1[lst[0, ROWID]]
    m0 = lax.fori_loop(0, chunks(0), lambda c, m: scores(0, c, 0, first, m), low)
    linv0, delta0 = weigh(0, 0, m0)

    def row(r, carry):
        linv, delta = carry
        i = lst[r, ROWID]
        buf = lax.rem(r, 2)
        nxt = jnp.minimum(r + 1, NB - 1)
        w1 = b1[lst[nxt, ROWID]]
        w2 = b2[i]

        def both(c, state):
            oq, m = state
            m = scores(nxt, c, 1 - buf, w1, m)
            oq = gradients(r, c, buf, w2, linv, delta, oq)
            return oq, m

        oq, m = lax.fori_loop(
            0, chunks(r), both, (jnp.zeros((BLOCK, 2 * BLOCK), F32), low)
        )
        ot[i] = oq[HD:, BLOCK:].astype(BF)
        dproj[at_block(i), 0:BLOCK] = oq[:, :BLOCK].T.astype(BF)
        return weigh(nxt, 1 - buf, m)

    lax.fori_loop(0, NB, row, (linv0, delta0))

    def fin(i, _):
        a = acc[at_block(i), :].astype(BF)
        q = dproj[at_block(i), 0:BLOCK]
        dproj[at_block(i), :] = jnp.concatenate([q[:, :HD], a], axis=1)
        return 0

    lax.fori_loop(0, NB, fin, 0, unroll=4)


def attention(lst, b1, b2, kv, kvt):
    vm = pl.BlockSpec(memory_space=pltpu.VMEM)
    n = NB * BLOCK
    return pl.pallas_call(
        attn_kernel,
        out_shape=(
            jax.ShapeDtypeStruct((NB, HD, BLOCK), BF),
            jax.ShapeDtypeStruct((n, 3 * HD), BF),
        ),
        in_specs=[pl.BlockSpec(memory_space=pltpu.SMEM), vm, vm, vm, vm],
        out_specs=(vm, vm),
        scratch_shapes=[
            pltpu.VMEM((2, n, BLOCK), F32),
            pltpu.VMEM((2, n, BLOCK), F32),
            pltpu.VMEM((n, BLOCK), F32),
        ],
        compiler_params=pltpu.CompilerParams(vmem_limit_bytes=12 * 1024 * 1024),
        name="attention",
    )(lst, b1, b2, kv, kvt)

MESH = pl.DeviceIdType.MESH
HD = 64
BLOCK = 128
NB = 16
NZ = 8
D = 1024
HALF = 64
QUART = 32
CORES = 2
NX = 4
NY = 4


def dot_t(a, b):
    return lax.dot_general(a, b, (((1,), (1,)), ((), ())), preferred_element_type=F32)


def ring_place():
    s = lax.axis_index("seq")
    y = lax.div(s, NZ)
    z = lax.rem(s, NZ)
    return s, y, z


def greet(peers):
    barrier = pltpu.get_barrier_semaphore()
    for peer in peers:
        pl.semaphore_signal(barrier, inc=1, device_id=peer, device_id_type=MESH)
    pl.semaphore_wait(barrier, len(peers))


RA = 80
SPLIT = {0: (0, 48), 1: (48, 32), 2: (80, 16), 3: (96, 32)}


def row_lists(pairs):
    one = jnp.float32(1)
    sub = lax.broadcasted_iota(jnp.int32, (BLOCK, BLOCK), 0)
    lane = lax.broadcasted_iota(jnp.int32, (BLOCK, BLOCK), 1)
    sub_nb, lane_nb = sub[:NB], lane[:NB]
    row_hot = jnp.where(sub == pairs[0:1, :], one, 0.0).astype(BF)
    col_hot = jnp.where(sub == pairs[1:2, :], one, 0.0).astype(BF)
    allowed = dot_t(row_hot[:NB], col_hot)
    n_col = jnp.sum(allowed, axis=1, keepdims=True)
    n_row = dot_t(jnp.ones((NB, BLOCK), BF), row_hot)[0:1]
    before = jnp.where(sub < lane, one, 0.0).astype(BF)
    pos = jnp.dot(allowed.astype(BF), before, preferred_element_type=F32)
    lists = jnp.zeros((NB, BLOCK), F32)
    lane_f = lane_nb.astype(F32)
    for t in range(NB):
        hit = jnp.where(pos == t, allowed, 0.0)
        col = jnp.sum(hit * lane_f, axis=1, keepdims=True)
        lists = jnp.where(lane_nb == t, col, lists)
    lists = jnp.where(lane_nb == NB, n_col, lists)
    lists = jnp.where(lane_nb == NB + 1, sub_nb.astype(F32), lists)
    ahead = jnp.logical_or(n_col > n_row, jnp.logical_and(n_col == n_row, sub_nb < lane_nb))
    rank = jnp.sum(jnp.where(ahead, one, 0.0), axis=0, keepdims=True)
    move = jnp.where(jnp.logical_and(sub_nb.astype(F32) == rank, lane_nb < NB), one, 0.0)
    full = jnp.concatenate([lists, jnp.zeros((BLOCK - NB, BLOCK), F32)], axis=0)
    out = jnp.dot(move.astype(BF), full.astype(BF), preferred_element_type=F32)
    return (out + 0.5).astype(jnp.int32)


def gather_kernel(
    x, w_hbm, g_hbm, pairs_hbm,
    xall, b1, b2, kv, kvt, lst,
    w, g, pairs, xg, gsend, grecv, sz, rz, sy, ry, sg, rg, lx, ll,
):
    s, y, z = ring_place()
    p = 1 - y
    up = {"seq": y * NZ + lax.rem(z + 1, NZ)}
    down = {"seq": y * NZ + lax.rem(z + NZ - 1, NZ)}
    across = {"seq": p * NZ + z}
    load = pltpu.make_async_copy(x.at[0], xg.at[s], ll.at[0])
    load_g = pltpu.make_async_copy(g_hbm.at[0], g, ll.at[1])
    load_w = pltpu.make_async_copy(w_hbm, w, ll.at[2])
    load_p = pltpu.make_async_copy(pairs_hbm, pairs, ll.at[3])
    load.start()
    load_g.start()
    load_w.start()
    load_p.start()
    greet([{"seq": lax.rem(s + d, NB)} for d in range(1, NB)])
    load.wait()

    def block(col, off):
        return col * NZ + lax.rem(z + off + NZ, NZ)

    def zmsg(flow, k, off, do_start):
        col = p if flow >= 4 else y
        first, rows = (0, RA) if flow < 2 else (RA, BLOCK - RA)
        if k == 3:
            first, rows = SPLIT[flow - 2 if flow >= 4 else flow]
        ref = xg.at[block(col, off), pl.ds(first, rows)]
        c = pltpu.make_async_remote_copy(
            src_ref=ref,
            dst_ref=ref,
            send_sem=sz.at[flow, k],
            recv_sem=rz.at[flow, k],
            device_id=down if flow % 2 else up,
            device_id_type=MESH,
        )
        if do_start:
            c.start()
        return c

    def ymsg(idx, col, do_start):
        off = 0 if idx == 8 else idx
        ref = xg.at[block(col, off), pl.ds(RA, BLOCK - RA) if idx == 8 else pl.ds(0, RA)]
        c = pltpu.make_async_remote_copy(
            src_ref=ref,
            dst_ref=ref,
            send_sem=sy.at[idx],
            recv_sem=ry.at[idx],
            device_id=across,
            device_id_type=MESH,
        )
        if do_start:
            c.start()
        return c

    sent = []
    outs = []
    sent.append(ymsg(8, y, True))
    for flow in (0, 1, 2, 3):
        sent.append(zmsg(flow, 0, 0, True))
    sent.append(ymsg(0, y, True))

    def compute(b, n):
        xb = xg[b]
        at = pl.ds(pl.multiple_of(b * BLOCK, BLOCK), BLOCK)
        kvf = dot_t(xb, w[HD:, :])
        qt = dot_t(w[:HD, :], xb)
        zero = jnp.zeros((HD, BLOCK), F32)
        kv[at, :] = kvf.astype(BF)
        kvt[:, at] = kvf.T.astype(BF)
        b1[b, :HD, :] = jnp.concatenate([qt, zero], axis=1).astype(BF)
        b2[b, :BLOCK, :] = jnp.concatenate([qt, zero], axis=0).T.astype(BF)
        c = pltpu.make_async_copy(xg.at[b], xall.at[b], lx.at[n])
        c.start()
        outs.append(c)

    load_g.wait()
    for c in range(NB // 2):
        t = g[:, c * BLOCK : (c + 1) * BLOCK].astype(F32).T.astype(BF)
        gsend[2 * c] = t[:HD]
        gsend[2 * c + 1] = t[HD:]

    def gmsg(d):
        to = lax.rem(s + d, NB)
        return pltpu.make_async_remote_copy(
            src_ref=gsend.at[to],
            dst_ref=grecv.at[s],
            send_sem=sg.at[d - 1],
            recv_sem=rg.at[d - 1],
            device_id={"seq": to},
            device_id_type=MESH,
        )

    load_w.wait()
    compute(s, 0)
    ymsg(8, p, False).wait_recv()
    for flow in (4, 5):
        sent.append(zmsg(flow, 0, 0, True))
    for d in range(1, NB):
        c = gmsg(d)
        c.start()
        sent.append(c)
    grecv[s] = gsend[s]
    load_p.wait()
    lst[...] = row_lists(pairs[...])

    def place(t, _):
        gt = grecv[t].astype(F32)
        zero = jnp.zeros((HD, BLOCK), F32)
        b1[t, HD:, :] = jnp.concatenate([zero, gt], axis=1).astype(BF)
        b2[t, BLOCK:, :] = jnp.concatenate([zero, gt], axis=0).T.astype(BF)
        return 0

    def place_all():
        for d in range(1, NB):
            frm = lax.rem(s + NB - d, NB)
            pltpu.make_async_remote_copy(
                src_ref=gsend.at[s],
                dst_ref=grecv.at[frm],
                send_sem=sg.at[d - 1],
                recv_sem=rg.at[d - 1],
                device_id={"seq": frm},
                device_id_type=MESH,
            ).wait_recv()
        lax.fori_loop(0, NB, place, 0)

    n = 1
    for k in range(4):
        for flow in (0, 1, 2, 3, 4, 5):
            off = (k + 1) if flow % 2 else -(k + 1)
            zmsg(flow, k, off, False).wait_recv()
            if k < 3:
                sent.append(zmsg(flow, k + 1, off, True))
            if flow < 2 and k < 3:
                sent.append(ymsg(off % NZ, y, True))
            if flow == 1 and k == 3:
                sent.append(ymsg(4, y, True))
        for off in [-(k + 1), k + 1][: 2 if k < 3 else 1]:
            compute(block(y, off), n)
            n += 1
        for off in [-k, k][: 2 if k > 0 else 1]:
            ymsg(off % NZ, p, False).wait_recv()
            compute(block(p, off), n)
            n += 1
        if k == 2:
            place_all()
    for c in outs:
        c.wait()
    outs.clear()
    ymsg(4, p, False).wait_recv()
    compute(block(p, 4), n)
    for c in sent:
        c.wait_send()
    for c in outs:
        c.wait()


def gather(x, w, g, pairs):
    vm = pl.BlockSpec(memory_space=pltpu.VMEM)
    anyw = pl.BlockSpec(memory_space=pl.ANY)
    hbm = pl.BlockSpec(memory_space=pltpu.HBM)
    n = NB * BLOCK
    sem = pltpu.SemaphoreType.DMA
    return pl.pallas_call(
        gather_kernel,
        out_shape=(
            jax.ShapeDtypeStruct((NB, BLOCK, D), BF),
            jax.ShapeDtypeStruct((NB, BLOCK, 2 * BLOCK), BF),
            jax.ShapeDtypeStruct((NB, 2 * BLOCK, BLOCK), BF),
            jax.ShapeDtypeStruct((n, BLOCK), BF),
            jax.ShapeDtypeStruct((BLOCK, n), BF),
            jax.ShapeDtypeStruct((NB, BLOCK), jnp.int32),
        ),
        in_specs=[hbm, hbm, hbm, hbm],
        out_specs=(anyw, vm, vm, vm, vm, vm),
        scratch_shapes=[
            pltpu.VMEM((3 * HD, D), BF),
            pltpu.VMEM((BLOCK, D), BF),
            pltpu.VMEM((2, BLOCK), jnp.int32),
            pltpu.VMEM((NB, BLOCK, D), BF),
            pltpu.VMEM((NB, HD, BLOCK), BF),
            pltpu.VMEM((NB, HD, BLOCK), BF),
            sem((6, 4)),
            sem((6, 4)),
            sem((9,)),
            sem((9,)),
            sem((NB - 1,)),
            sem((NB - 1,)),
            sem((NB,)),
            sem((4,)),
        ],
        compiler_params=pltpu.CompilerParams(
            collective_id=0, has_side_effects=True, vmem_limit_bytes=20 * 1024 * 1024
        ),
        name="gather_project",
    )(x, w, g, pairs)


def scatter_kernel(
    dproj, w_hbm, ot, xv,
    att, ng, wg,
    w, zs, zr, ysb, yrb, arecv, dt, dwf, cs, cr, xs, xr, hs, hr, fs, fo, fsib,
    sz, rz, sy, ry, sa, ra, sc, rc, sx, rx, sh, rh, sf, rf, lx,
):
    s, y, z = ring_place()
    p = 1 - y
    up = {"seq": y * NZ + lax.rem(z + 1, NZ)}
    down = {"seq": y * NZ + lax.rem(z + NZ - 1, NZ)}
    across = {"seq": p * NZ + z}
    q = lax.axis_index("clus")
    cx = lax.div(q, NY * CORES)
    ch = lax.rem(lax.div(q, CORES), NY)
    cc = lax.rem(q, CORES)
    sib = {"clus": q + 1 - 2 * cc}

    def xpeer(d):
        return {"clus": lax.rem(cx + d, NX) * (NY * CORES) + ch * CORES + cc}

    def hpeer(d):
        return {"clus": cx * (NY * CORES) + lax.rem(ch + d, NY) * CORES + cc}

    load = pltpu.make_async_copy(w_hbm, w, lx)
    load.start()
    greet(
        [{"seq": lax.rem(s + d, NB)} for d in range(1, NB)]
        + [sib]
        + [xpeer(d) for d in range(1, NX)]
        + [hpeer(d) for d in range(1, NY)]
    )

    def block(col, off):
        return col * NZ + lax.rem(z + off + NZ, NZ)

    def part(col, off, first, rows):
        b = block(col, off)
        at = pl.ds(pl.multiple_of(b * BLOCK + first, QUART), rows)
        return jnp.dot(dproj[at, :], w[...], preferred_element_type=F32)

    sent = []

    def rcopy(src, dst, ss, rs, dev):
        return pltpu.make_async_remote_copy(
            src_ref=src, dst_ref=dst, send_sem=ss, recv_sem=rs,
            device_id=dev, device_id_type=MESH,
        )

    def span(flow, k):
        if k == 0:
            return pl.ds(QUART if flow % 2 else 0, QUART)
        return pl.ds(0, HALF)

    def zmsg(flow, k):
        at = span(flow, k)
        return rcopy(
            zs.at[flow, k, at], zr.at[flow, k, at], sz.at[flow, k], rz.at[flow, k],
            down if flow % 2 else up,
        )

    def ymsg(idx):
        return rcopy(ysb.at[idx], yrb.at[idx], sy.at[idx], ry.at[idx], across)

    def go(c):
        c.start()
        sent.append(c)

    def zstep(flow, k):
        col = p if flow >= 4 else y
        base = 0 if flow < 2 else HALF
        off = (4 - k) * (-1 if flow % 2 else 1)
        if k == 0:
            lo = QUART if flow % 2 else 0
            val = part(col, off, base + lo, QUART)
            if flow < 2:
                val = val + yrb[off % NZ, lo : lo + QUART, :].astype(F32)
            zs[flow, 0, lo : lo + QUART, :] = val.astype(BF)
        else:
            val = part(col, off, base, HALF)
            if flow < 2:
                val = val + yrb[off % NZ].astype(F32)
            zmsg(flow, k - 1).wait_recv()
            if k == 1:
                lo = QUART if flow % 2 else 0
                zs[flow, 1, QUART - lo : HALF - lo, :] = val[QUART - lo : HALF - lo].astype(BF)
                zs[flow, 1, lo : lo + QUART, :] = (
                    val[lo : lo + QUART] + zr[flow, 0, lo : lo + QUART, :].astype(F32)
                ).astype(BF)
            else:
                zs[flow, k] = (val + zr[flow, k - 1].astype(F32)).astype(BF)
        go(zmsg(flow, k))

    def ysend(off):
        ysb[off % NZ] = part(p, off, 0, HALF).astype(BF)
        go(ymsg(off % NZ))

    load.wait()
    for flow in (4, 5):
        zstep(flow, 0)
    ysend(4)
    for flow in (2, 3):
        zstep(flow, 0)
    ysend(3)
    ysend(-3)
    for d in range(1, NB):
        to = lax.rem(s + d, NB)
        go(rcopy(ot.at[to], arecv.at[s], sa.at[d - 1], ra.at[d - 1], {"seq": to}))
    arecv[s] = ot[s]

    def turn(t, _):
        at = pl.ds(pl.multiple_of(t * BLOCK, BLOCK), BLOCK)
        v = jnp.concatenate([dproj[at, :].astype(F32), jnp.zeros((BLOCK, HD), F32)], axis=1)
        dt[:, at] = v.T[: 3 * HD].astype(BF)
        return 0

    def wstep(t, _):
        at = pl.ds(pl.multiple_of(t * 256, 256), 256)
        dwf[:, at] = jnp.dot(dt[...], xv[:, at], preferred_element_type=F32)
        return 0

    hrow = 3 * HD // CORES
    mine = pl.ds(pl.multiple_of(cc * hrow, QUART), hrow)
    other = pl.ds(pl.multiple_of((1 - cc) * hrow, QUART), hrow)
    wide = D // NX

    def stage0a():
        lax.fori_loop(0, NB, turn, 0)
        lax.fori_loop(0, 2, wstep, 0)

    def stage0b():
        lax.fori_loop(2, D // 256, wstep, 0)
        cs[...] = dwf[other, :].astype(BF)
        go(rcopy(cs, cr, sc.at[0], rc.at[0], sib))

    def stage1():
        rcopy(cs, cr, sc.at[0], rc.at[0], sib).wait_recv()
        v = dwf[mine, :] + cr[...].astype(F32)
        for t in range(NX):
            xs[t] = v[:, t * wide : (t + 1) * wide].astype(BF)
        xr[cx] = xs[cx]
        for d in range(1, NX):
            go(rcopy(xs.at[lax.rem(cx + d, NX)], xr.at[cx], sx.at[d - 1], rx.at[d - 1], xpeer(d)))

    def stage2():
        for d in range(1, NX):
            frm = lax.rem(cx + NX - d, NX)
            rcopy(xs.at[cx], xr.at[frm], sx.at[d - 1], rx.at[d - 1], xpeer(d)).wait_recv()
        v = xr[0].astype(F32) + xr[1].astype(F32) + xr[2].astype(F32) + xr[3].astype(F32)
        hs[...] = v.astype(BF)
        hr[ch] = v.astype(BF)
        for d in range(1, NY):
            go(rcopy(hs, hr.at[ch], sh.at[d - 1], rh.at[d - 1], hpeer(d)))

    def stage3():
        for d in range(1, NY):
            frm = lax.rem(ch + NY - d, NY)
            rcopy(hs, hr.at[frm], sh.at[d - 1], rh.at[d - 1], hpeer(d)).wait_recv()
        v = hr[0].astype(F32) + hr[1].astype(F32) + hr[2].astype(F32) + hr[3].astype(F32)
        fs[...] = v.astype(BF)
        fo[cx] = v.astype(BF)
        for d in range(1, NX):
            go(rcopy(fs, fo.at[cx], sf.at[d - 1], rf.at[d - 1], xpeer(d)))

    def stage4():
        for d in range(1, NX):
            frm = lax.rem(cx + NX - d, NX)
            rcopy(fs, fo.at[frm], sf.at[d - 1], rf.at[d - 1], xpeer(d)).wait_recv()
        go(rcopy(fo, fsib, sc.at[1], rc.at[1], sib))

    def stage5():
        rcopy(fo, fsib, sc.at[1], rc.at[1], sib).wait_recv()
        for t in range(NX):
            at = pl.ds(t * wide, wide)
            wg[mine, at] = fo[t].astype(F32) * (1.0 / (NX * NY * CORES))
            wg[other, at] = fsib[t].astype(F32) * (1.0 / (NX * NY * CORES))

    def asteps(k):
        if k == 0:
            ymsg(4).wait_recv()
        else:
            ymsg((4 - k) % NZ).wait_recv()
            ymsg((k - 4) % NZ).wait_recv()
        zstep(0, k)
        zstep(1, k)

    def total(flow, col, base):
        val = part(col, 0, base, HALF)
        for f in (flow, flow + 1):
            zmsg(f, 3).wait_recv()
            val = val + zr[f, 3].astype(F32)
        return val

    asteps(0)
    for flow in (4, 5, 2, 3):
        zstep(flow, 1)
    ysend(2)
    ysend(-2)
    stage0a()
    asteps(1)
    for flow in (4, 5, 2, 3):
        zstep(flow, 2)
    ysend(1)
    ysend(-1)
    stage0b()
    asteps(2)
    stage1()
    for flow in (4, 5, 2, 3):
        zstep(flow, 3)
    ysend(0)
    stage2()
    asteps(3)
    ysb[8] = total(4, p, HALF).astype(BF)
    go(ymsg(8))
    stage3()
    own_b = total(2, y, HALF)
    stage4()
    ymsg(0).wait_recv()
    ng[0, :HALF, :] = (total(0, y, 0) + yrb[0].astype(F32)).astype(BF)
    for d in range(1, NB):
        frm = lax.rem(s + NB - d, NB)
        rcopy(ot.at[s], arecv.at[frm], sa.at[d - 1], ra.at[d - 1], {"seq": frm}).wait_recv()
    for c in range(NB // 2):
        t = jnp.concatenate([arecv[2 * c], arecv[2 * c + 1]], axis=0).astype(F32)
        att[0, :, c * BLOCK : (c + 1) * BLOCK] = t.T.astype(BF)
    stage5()
    ymsg(8).wait_recv()
    ng[0, HALF:, :] = (own_b + yrb[8].astype(F32)).astype(BF)
    for c in sent:
        c.wait_send()


def scatter(dproj, w, ot, xall):
    vm = pl.BlockSpec(memory_space=pltpu.VMEM)
    hbm = pl.BlockSpec(memory_space=pltpu.HBM)
    n = NB * BLOCK
    sem = pltpu.SemaphoreType.DMA
    vmem = pltpu.VMEM
    hrow = 3 * HD // CORES
    wide = D // NX
    return pl.pallas_call(
        scatter_kernel,
        out_shape=(
            jax.ShapeDtypeStruct((1, BLOCK, D), BF),
            jax.ShapeDtypeStruct((1, BLOCK, D), BF),
            jax.ShapeDtypeStruct((3 * HD, D), F32),
        ),
        in_specs=[vm, hbm, vm, vm],
        out_specs=(vm, vm, vm),
        scratch_shapes=[
            vmem((3 * HD, D), BF),
            vmem((6, 4, HALF, D), BF),
            vmem((6, 4, HALF, D), BF),
            vmem((9, HALF, D), BF),
            vmem((9, HALF, D), BF),
            vmem((NB, HD, BLOCK), BF),
            vmem((3 * HD, n), BF),
            vmem((3 * HD, D), F32),
            vmem((hrow, D), BF),
            vmem((hrow, D), BF),
            vmem((NX, hrow, wide), BF),
            vmem((NX, hrow, wide), BF),
            vmem((hrow, wide), BF),
            vmem((NY, hrow, wide), BF),
            vmem((hrow, wide), BF),
            vmem((NX, hrow, wide), BF),
            vmem((NX, hrow, wide), BF),
            sem((6, 4)),
            sem((6, 4)),
            sem((9,)),
            sem((9,)),
            sem((NB - 1,)),
            sem((NB - 1,)),
            sem((2,)),
            sem((2,)),
            sem((NX - 1,)),
            sem((NX - 1,)),
            sem((NY - 1,)),
            sem((NY - 1,)),
            sem((NX - 1,)),
            sem((NX - 1,)),
            sem,
        ],
        compiler_params=pltpu.CompilerParams(
            collective_id=1, has_side_effects=True, vmem_limit_bytes=22 * 1024 * 1024
        ),
        name="scatter_reduce",
    )(dproj, w, ot, xall)


def put_kernel(a, b, c, ao, bo, co, sems):
    copies = [
        pltpu.make_async_copy(src, dst, sems.at[t])
        for t, (src, dst) in enumerate(((c, co), (a, ao), (b, bo)))
    ]
    for copy in copies:
        copy.start()
    for copy in copies:
        copy.wait()


def put(a, b, c):
    vm = pl.BlockSpec(memory_space=pltpu.VMEM)
    hbm = pl.BlockSpec(memory_space=pltpu.HBM)
    return pl.pallas_call(
        put_kernel,
        out_shape=tuple(jax.ShapeDtypeStruct(t.shape, t.dtype) for t in (a, b, c)),
        in_specs=[vm, vm, vm],
        out_specs=(hbm, hbm, hbm),
        scratch_shapes=[pltpu.SemaphoreType.DMA((3,))],
        compiler_params=pltpu.CompilerParams(vmem_limit_bytes=4 * 1024 * 1024),
        name="put",
    )(a, b, c)


def local(node_feats, qkv_weight, block_pairs, grad_out):
    operands = (node_feats, qkv_weight, grad_out, jnp.transpose(block_pairs[0]))
    held = [pltpu.with_memory_space_constraint(t, pltpu.HBM) for t in operands]
    xall, b1, b2, kv, kvt, lst = gather(*held)
    ot, dproj = attention(lst, b1, b2, kv, kvt)
    return put(*scatter(dproj, qkv_weight, ot, xall.reshape(NB * BLOCK, D)))


def solution(mesh):
    return jax.shard_map(
        local,
        mesh=mesh,
        in_specs=(
            P("clus", "seq", None),
            P("seq", None),
            P("clus", None, None),
            P("clus", "seq", None),
        ),
        out_specs=(P("clus", "seq", None), P("clus", "seq", None), P("seq", None)),
        check_vma=False,
    )
```

```python
import math

import jax
import jax.numpy as jnp
from jax import lax
from jax.experimental import pallas as pl
from jax.experimental.pallas import tpu as pltpu
from jax.sharding import PartitionSpec as P

F32 = jnp.float32
BF = jnp.bfloat16
HD = 64
BLOCK = 128
NB = 16
BIG = True
PAD = -1e30
COUNT = 16
ROWID = 17
SCALE = 0.125 * math.log2(math.e)


def attn_kernel(lst, b1, b2, kv, kvt, ot, dproj, s_scr, d_scr, acc):
    acc[...] = jnp.zeros_like(acc)

    def at_block(j):
        return pl.ds(pl.multiple_of(j * BLOCK, BLOCK), BLOCK)

    def at_rows(base, ch):
        return pl.ds(pl.multiple_of(base * BLOCK, BLOCK), ch * BLOCK)

    def fold(v):
        return v.reshape(v.shape[0] // 8, 8, BLOCK)

    def scores(r, base, ch, buf, w1, m):
        n = lst[r, COUNT]
        lhs = jnp.concatenate([kv[at_block(lst[r, base + t]), :] for t in range(ch)], axis=0)
        sd = jnp.dot(lhs, w1, preferred_element_type=F32)
        s = jnp.concatenate(
            [
                sd[t * BLOCK : (t + 1) * BLOCK, :BLOCK]
                + jnp.where(base + t < n, 0.0, PAD).astype(F32)
                for t in range(ch)
            ],
            axis=0,
        )
        s_scr[buf, at_rows(base, ch), :] = s
        d_scr[buf, at_rows(base, ch), :] = sd[:, BLOCK:]
        return jnp.maximum(m, jnp.max(fold(s), axis=0))

    def weigh(base, ch, buf, m, l, d):
        e = jnp.exp2((s_scr[buf, at_rows(base, ch), :] - m) * SCALE)
        s_scr[buf, at_rows(base, ch), :] = e
        l = l + jnp.sum(fold(e), axis=0)
        d = d + jnp.sum(fold(e * d_scr[buf, at_rows(base, ch), :]), axis=0)
        return l, d

    def gradients(r, base, ch, buf, w2, linv, delta, oq):
        p = s_scr[buf, at_rows(base, ch), :] * linv
        ds = p * ((d_scr[buf, at_rows(base, ch), :] - delta) * 0.125)
        cat = jnp.concatenate([ds.astype(BF), p.astype(BF)], axis=1)
        cols = [lst[r, base + t] for t in range(ch)]
        lhs = jnp.concatenate([kvt[:, at_block(j)] for j in cols], axis=1)
        oq = oq + jnp.dot(lhs, cat, preferred_element_type=F32)
        g = jnp.dot(cat, w2, preferred_element_type=F32)
        for t in range(ch):
            acc[at_block(cols[t]), :] += g[t * BLOCK : (t + 1) * BLOCK]
        return oq

    def sweep(r, body, state):
        n = lst[r, COUNT]
        n8 = lax.div(n + 3, 8)
        n4 = lax.div(n + 3, 4) - 2 * n8
        if BIG:
            state = lax.fori_loop(0, n8, lambda c, st: body(c * 8, 8, st), state)
            return lax.fori_loop(0, n4, lambda c, st: body(n8 * 8, 4, st), state)
        return lax.fori_loop(0, lax.div(n + 3, 4), lambda c, st: body(c * 4, 4, st), state)

    def rows_max(m):
        return jnp.max(m, axis=0, keepdims=True)

    def close(l, d):
        linv = 1.0 / jnp.sum(l, axis=0, keepdims=True)
        return linv, jnp.sum(d, axis=0, keepdims=True) * linv

    low = jnp.full((8, BLOCK), PAD, F32)
    zero = jnp.zeros((8, BLOCK), F32)
    w1_0 = b1[lst[0, ROWID]]
    w1_1 = b1[lst[1, ROWID]]
    m0 = rows_max(sweep(0, lambda b, ch, m: scores(0, b, ch, 0, w1_0, m), low))

    def second(b, ch, st):
        m, l, d = st
        m = scores(1, b, ch, 1, w1_1, m)
        l, d = weigh(b, ch, 0, m0, l, d)
        return m, l, d

    m1, l0, d0 = sweep(0, second, (low, zero, zero))

    def row(r, carry):
        linv, delta, m = carry
        m = rows_max(m)
        i = lst[r, ROWID]
        far = jnp.minimum(r + 2, NB - 1)
        w1 = b1[lst[far, ROWID]]
        w2 = b2[i]
        buf, buf1, buf2 = lax.rem(r, 3), lax.rem(r + 1, 3), lax.rem(r + 2, 3)

        def body(b, ch, st):
            oq, l, d, mf = st
            mf = scores(far, b, ch, buf2, w1, mf)
            l, d = weigh(b, ch, buf1, m, l, d)
            oq = gradients(r, b, ch, buf, w2, linv, delta, oq)
            return oq, l, d, mf

        oq, l, d, mf = sweep(r, body, (jnp.zeros((BLOCK, 2 * BLOCK), F32), zero, zero, low))
        ot[i] = oq[HD:, BLOCK:].astype(BF)
        dproj[at_block(i), 0:BLOCK] = oq[:, :BLOCK].T.astype(BF)
        linv, delta = close(l, d)
        return linv, delta, mf

    lax.fori_loop(0, NB, row, (*close(l0, d0), m1))

    def fin(i, _):
        a = acc[at_block(i), :].astype(BF)
        q = dproj[at_block(i), 0:BLOCK]
        dproj[at_block(i), :] = jnp.concatenate([q[:, :HD], a], axis=1)
        return 0

    lax.fori_loop(0, NB, fin, 0, unroll=4)


def attention(lst, b1, b2, kv, kvt):
    vm = pl.BlockSpec(memory_space=pltpu.VMEM)
    n = NB * BLOCK
    return pl.pallas_call(
        attn_kernel,
        out_shape=(
            jax.ShapeDtypeStruct((NB, HD, BLOCK), BF),
            jax.ShapeDtypeStruct((n, 3 * HD), BF),
        ),
        in_specs=[pl.BlockSpec(memory_space=pltpu.SMEM), vm, vm, vm, vm],
        out_specs=(vm, vm),
        scratch_shapes=[
            pltpu.VMEM((3, n, BLOCK), F32),
            pltpu.VMEM((3, n, BLOCK), F32),
            pltpu.VMEM((n, BLOCK), F32),
        ],
        compiler_params=pltpu.CompilerParams(vmem_limit_bytes=14 * 1024 * 1024),
        name="attention",
    )(lst, b1, b2, kv, kvt)

MESH = pl.DeviceIdType.MESH
HD = 64
BLOCK = 128
NB = 16
NZ = 8
D = 1024
HALF = 64
QUART = 32
CORES = 2
NX = 4
NY = 4


def dot_t(a, b):
    return lax.dot_general(a, b, (((1,), (1,)), ((), ())), preferred_element_type=F32)


def ring_place():
    s = lax.axis_index("seq")
    y = lax.div(s, NZ)
    z = lax.rem(s, NZ)
    return s, y, z


def greet(peers):
    barrier = pltpu.get_barrier_semaphore()
    for peer in peers:
        pl.semaphore_signal(barrier, inc=1, device_id=peer, device_id_type=MESH)
    pl.semaphore_wait(barrier, len(peers))


RA = 80
SPLIT = {0: (0, 48), 1: (48, 32), 2: (80, 16), 3: (96, 32)}


def row_lists(pairs):
    one = jnp.float32(1)
    sub = lax.broadcasted_iota(jnp.int32, (BLOCK, BLOCK), 0)
    lane = lax.broadcasted_iota(jnp.int32, (BLOCK, BLOCK), 1)
    sub_nb, lane_nb = sub[:NB], lane[:NB]
    row_hot = jnp.where(sub == pairs[0:1, :], one, 0.0).astype(BF)
    col_hot = jnp.where(sub == pairs[1:2, :], one, 0.0).astype(BF)
    allowed = dot_t(row_hot[:NB], col_hot)
    n_col = jnp.sum(allowed, axis=1, keepdims=True)
    n_row = dot_t(jnp.ones((NB, BLOCK), BF), row_hot)[0:1]
    before = jnp.where(sub < lane, one, 0.0).astype(BF)
    pos = jnp.dot(allowed.astype(BF), before, preferred_element_type=F32)
    lists = jnp.zeros((NB, BLOCK), F32)
    lane_f = lane_nb.astype(F32)
    for t in range(NB):
        hit = jnp.where(pos == t, allowed, 0.0)
        col = jnp.sum(hit * lane_f, axis=1, keepdims=True)
        lists = jnp.where(lane_nb == t, col, lists)
    lists = jnp.where(lane_nb == NB, n_col, lists)
    lists = jnp.where(lane_nb == NB + 1, sub_nb.astype(F32), lists)
    ahead = jnp.logical_or(n_col > n_row, jnp.logical_and(n_col == n_row, sub_nb < lane_nb))
    rank = jnp.sum(jnp.where(ahead, one, 0.0), axis=0, keepdims=True)
    move = jnp.where(jnp.logical_and(sub_nb.astype(F32) == rank, lane_nb < NB), one, 0.0)
    full = jnp.concatenate([lists, jnp.zeros((BLOCK - NB, BLOCK), F32)], axis=0)
    out = jnp.dot(move.astype(BF), full.astype(BF), preferred_element_type=F32)
    return (out + 0.5).astype(jnp.int32)


def gather_kernel(
    x, w_hbm, g_hbm, pairs_hbm,
    xall, b1, b2, kv, kvt, lst,
    w, g, pairs, xg, gsend, grecv, sz, rz, sy, ry, sg, rg, lx, ll,
):
    s, y, z = ring_place()
    p = 1 - y
    up = {"seq": y * NZ + lax.rem(z + 1, NZ)}
    down = {"seq": y * NZ + lax.rem(z + NZ - 1, NZ)}
    across = {"seq": p * NZ + z}
    load = pltpu.make_async_copy(x.at[0], xg.at[s], ll.at[0])
    load_g = pltpu.make_async_copy(g_hbm.at[0], g, ll.at[1])
    load_w = pltpu.make_async_copy(w_hbm, w, ll.at[2])
    load_p = pltpu.make_async_copy(pairs_hbm, pairs, ll.at[3])
    load.start()
    load_g.start()
    load_w.start()
    load_p.start()
    greet([{"seq": lax.rem(s + d, NB)} for d in range(1, NB)])
    load.wait()

    def block(col, off):
        return col * NZ + lax.rem(z + off + NZ, NZ)

    def zmsg(flow, k, off, do_start):
        col = p if flow >= 4 else y
        first, rows = (0, RA) if flow < 2 else (RA, BLOCK - RA)
        if k == 3:
            first, rows = SPLIT[flow - 2 if flow >= 4 else flow]
        ref = xg.at[block(col, off), pl.ds(first, rows)]
        c = pltpu.make_async_remote_copy(
            src_ref=ref,
            dst_ref=ref,
            send_sem=sz.at[flow, k],
            recv_sem=rz.at[flow, k],
            device_id=down if flow % 2 else up,
            device_id_type=MESH,
        )
        if do_start:
            c.start()
        return c

    def ymsg(idx, col, do_start):
        off = 0 if idx == 8 else idx
        ref = xg.at[block(col, off), pl.ds(RA, BLOCK - RA) if idx == 8 else pl.ds(0, RA)]
        c = pltpu.make_async_remote_copy(
            src_ref=ref,
            dst_ref=ref,
            send_sem=sy.at[idx],
            recv_sem=ry.at[idx],
            device_id=across,
            device_id_type=MESH,
        )
        if do_start:
            c.start()
        return c

    sent = []
    outs = []
    sent.append(ymsg(8, y, True))
    for flow in (0, 1, 2, 3):
        sent.append(zmsg(flow, 0, 0, True))
    sent.append(ymsg(0, y, True))

    def compute(b, n):
        xb = xg[b]
        at = pl.ds(pl.multiple_of(b * BLOCK, BLOCK), BLOCK)
        kvf = dot_t(xb, w[HD:, :])
        qt = dot_t(w[:HD, :], xb)
        zero = jnp.zeros((HD, BLOCK), F32)
        kv[at, :] = kvf.astype(BF)
        kvt[:, at] = kvf.T.astype(BF)
        b1[b, :HD, :] = jnp.concatenate([qt, zero], axis=1).astype(BF)
        b2[b, :BLOCK, :] = jnp.concatenate([qt, zero], axis=0).T.astype(BF)
        c = pltpu.make_async_copy(xg.at[b], xall.at[b], lx.at[n])
        c.start()
        outs.append(c)

    load_g.wait()
    for c in range(NB // 2):
        t = g[:, c * BLOCK : (c + 1) * BLOCK].astype(F32).T.astype(BF)
        gsend[2 * c] = t[:HD]
        gsend[2 * c + 1] = t[HD:]

    def gmsg(d):
        to = lax.rem(s + d, NB)
        return pltpu.make_async_remote_copy(
            src_ref=gsend.at[to],
            dst_ref=grecv.at[s],
            send_sem=sg.at[d - 1],
            recv_sem=rg.at[d - 1],
            device_id={"seq": to},
            device_id_type=MESH,
        )

    load_w.wait()
    compute(s, 0)
    ymsg(8, p, False).wait_recv()
    for flow in (4, 5):
        sent.append(zmsg(flow, 0, 0, True))
    for d in range(1, NB):
        c = gmsg(d)
        c.start()
        sent.append(c)
    grecv[s] = gsend[s]
    load_p.wait()
    lst[...] = row_lists(pairs[...])

    def place(t, _):
        gt = grecv[t].astype(F32)
        zero = jnp.zeros((HD, BLOCK), F32)
        b1[t, HD:, :] = jnp.concatenate([zero, gt], axis=1).astype(BF)
        b2[t, BLOCK:, :] = jnp.concatenate([zero, gt], axis=0).T.astype(BF)
        return 0

    def place_all():
        for d in range(1, NB):
            frm = lax.rem(s + NB - d, NB)
            pltpu.make_async_remote_copy(
                src_ref=gsend.at[s],
                dst_ref=grecv.at[frm],
                send_sem=sg.at[d - 1],
                recv_sem=rg.at[d - 1],
                device_id={"seq": frm},
                device_id_type=MESH,
            ).wait_recv()
        lax.fori_loop(0, NB, place, 0)

    n = 1
    for k in range(4):
        for flow in (0, 1, 2, 3, 4, 5):
            off = (k + 1) if flow % 2 else -(k + 1)
            zmsg(flow, k, off, False).wait_recv()
            if k < 3:
                sent.append(zmsg(flow, k + 1, off, True))
            if flow < 2 and k < 3:
                sent.append(ymsg(off % NZ, y, True))
            if flow == 1 and k == 3:
                sent.append(ymsg(4, y, True))
        for off in [-(k + 1), k + 1][: 2 if k < 3 else 1]:
            compute(block(y, off), n)
            n += 1
        for off in [-k, k][: 2 if k > 0 else 1]:
            ymsg(off % NZ, p, False).wait_recv()
            compute(block(p, off), n)
            n += 1
        if k == 2:
            place_all()
    for c in outs:
        c.wait()
    outs.clear()
    ymsg(4, p, False).wait_recv()
    compute(block(p, 4), n)
    for c in sent:
        c.wait_send()
    for c in outs:
        c.wait()


def gather(x, w, g, pairs):
    vm = pl.BlockSpec(memory_space=pltpu.VMEM)
    anyw = pl.BlockSpec(memory_space=pl.ANY)
    hbm = pl.BlockSpec(memory_space=pltpu.HBM)
    n = NB * BLOCK
    sem = pltpu.SemaphoreType.DMA
    return pl.pallas_call(
        gather_kernel,
        out_shape=(
            jax.ShapeDtypeStruct((NB, BLOCK, D), BF),
            jax.ShapeDtypeStruct((NB, BLOCK, 2 * BLOCK), BF),
            jax.ShapeDtypeStruct((NB, 2 * BLOCK, BLOCK), BF),
            jax.ShapeDtypeStruct((n, BLOCK), BF),
            jax.ShapeDtypeStruct((BLOCK, n), BF),
            jax.ShapeDtypeStruct((NB, BLOCK), jnp.int32),
        ),
        in_specs=[hbm, hbm, hbm, hbm],
        out_specs=(anyw, vm, vm, vm, vm, vm),
        scratch_shapes=[
            pltpu.VMEM((3 * HD, D), BF),
            pltpu.VMEM((BLOCK, D), BF),
            pltpu.VMEM((2, BLOCK), jnp.int32),
            pltpu.VMEM((NB, BLOCK, D), BF),
            pltpu.VMEM((NB, HD, BLOCK), BF),
            pltpu.VMEM((NB, HD, BLOCK), BF),
            sem((6, 4)),
            sem((6, 4)),
            sem((9,)),
            sem((9,)),
            sem((NB - 1,)),
            sem((NB - 1,)),
            sem((NB,)),
            sem((4,)),
        ],
        compiler_params=pltpu.CompilerParams(
            collective_id=0, has_side_effects=True, vmem_limit_bytes=20 * 1024 * 1024
        ),
        name="gather_project",
    )(x, w, g, pairs)


def scatter_kernel(
    dproj, w_hbm, ot, xv,
    att, ng, wg,
    w, zs, zr, ysb, yrb, arecv, dt, dwf, cs, cr, xs, xr, hs, hr, fs, fo, fsib,
    sz, rz, sy, ry, sa, ra, sc, rc, sx, rx, sh, rh, sf, rf, lx,
):
    s, y, z = ring_place()
    p = 1 - y
    up = {"seq": y * NZ + lax.rem(z + 1, NZ)}
    down = {"seq": y * NZ + lax.rem(z + NZ - 1, NZ)}
    across = {"seq": p * NZ + z}
    q = lax.axis_index("clus")
    cx = lax.div(q, NY * CORES)
    ch = lax.rem(lax.div(q, CORES), NY)
    cc = lax.rem(q, CORES)
    sib = {"clus": q + 1 - 2 * cc}

    def xpeer(d):
        return {"clus": lax.rem(cx + d, NX) * (NY * CORES) + ch * CORES + cc}

    def hpeer(d):
        return {"clus": cx * (NY * CORES) + lax.rem(ch + d, NY) * CORES + cc}

    load = pltpu.make_async_copy(w_hbm, w, lx)
    load.start()
    greet(
        [{"seq": lax.rem(s + d, NB)} for d in range(1, NB)]
        + [sib]
        + [xpeer(d) for d in range(1, NX)]
        + [hpeer(d) for d in range(1, NY)]
    )

    def block(col, off):
        return col * NZ + lax.rem(z + off + NZ, NZ)

    def part(col, off, first, rows):
        b = block(col, off)
        at = pl.ds(pl.multiple_of(b * BLOCK + first, QUART), rows)
        return jnp.dot(dproj[at, :], w[...], preferred_element_type=F32)

    sent = []

    def rcopy(src, dst, ss, rs, dev):
        return pltpu.make_async_remote_copy(
            src_ref=src, dst_ref=dst, send_sem=ss, recv_sem=rs,
            device_id=dev, device_id_type=MESH,
        )

    def span(flow, k):
        if k == 0:
            return pl.ds(QUART if flow % 2 else 0, QUART)
        return pl.ds(0, HALF)

    def zmsg(flow, k):
        at = span(flow, k)
        return rcopy(
            zs.at[flow, k, at], zr.at[flow, k, at], sz.at[flow, k], rz.at[flow, k],
            down if flow % 2 else up,
        )

    def ymsg(idx):
        return rcopy(ysb.at[idx], yrb.at[idx], sy.at[idx], ry.at[idx], across)

    def go(c):
        c.start()
        sent.append(c)

    def zstep(flow, k):
        col = p if flow >= 4 else y
        base = 0 if flow < 2 else HALF
        off = (4 - k) * (-1 if flow % 2 else 1)
        if k == 0:
            lo = QUART if flow % 2 else 0
            val = part(col, off, base + lo, QUART)
            if flow < 2:
                val = val + yrb[off % NZ, lo : lo + QUART, :].astype(F32)
            zs[flow, 0, lo : lo + QUART, :] = val.astype(BF)
        else:
            val = part(col, off, base, HALF)
            if flow < 2:
                val = val + yrb[off % NZ].astype(F32)
            zmsg(flow, k - 1).wait_recv()
            if k == 1:
                lo = QUART if flow % 2 else 0
                zs[flow, 1, QUART - lo : HALF - lo, :] = val[QUART - lo : HALF - lo].astype(BF)
                zs[flow, 1, lo : lo + QUART, :] = (
                    val[lo : lo + QUART] + zr[flow, 0, lo : lo + QUART, :].astype(F32)
                ).astype(BF)
            else:
                zs[flow, k] = (val + zr[flow, k - 1].astype(F32)).astype(BF)
        go(zmsg(flow, k))

    def ysend(off):
        ysb[off % NZ] = part(p, off, 0, HALF).astype(BF)
        go(ymsg(off % NZ))

    load.wait()
    for flow in (4, 5):
        zstep(flow, 0)
    ysend(4)
    for flow in (2, 3):
        zstep(flow, 0)
    ysend(3)
    ysend(-3)
    for d in range(1, NB):
        to = lax.rem(s + d, NB)
        go(rcopy(ot.at[to], arecv.at[s], sa.at[d - 1], ra.at[d - 1], {"seq": to}))
    arecv[s] = ot[s]

    def turn(t, _):
        at = pl.ds(pl.multiple_of(t * BLOCK, BLOCK), BLOCK)
        v = jnp.concatenate([dproj[at, :].astype(F32), jnp.zeros((BLOCK, HD), F32)], axis=1)
        dt[:, at] = v.T[: 3 * HD].astype(BF)
        return 0

    def wstep(t, _):
        at = pl.ds(pl.multiple_of(t * 256, 256), 256)
        dwf[:, at] = jnp.dot(dt[...], xv[:, at], preferred_element_type=F32)
        return 0

    hrow = 3 * HD // CORES
    mine = pl.ds(pl.multiple_of(cc * hrow, QUART), hrow)
    other = pl.ds(pl.multiple_of((1 - cc) * hrow, QUART), hrow)
    wide = D // NX

    def stage0():
        lax.fori_loop(0, NB, turn, 0)
        lax.fori_loop(0, D // 256, wstep, 0)
        cs[...] = dwf[other, :].astype(BF)
        go(rcopy(cs, cr, sc.at[0], rc.at[0], sib))

    def stage1():
        rcopy(cs, cr, sc.at[0], rc.at[0], sib).wait_recv()
        v = dwf[mine, :] + cr[...].astype(F32)
        for t in range(NX):
            xs[t] = v[:, t * wide : (t + 1) * wide].astype(BF)
        xr[cx] = xs[cx]
        for d in range(1, NX):
            go(rcopy(xs.at[lax.rem(cx + d, NX)], xr.at[cx], sx.at[d - 1], rx.at[d - 1], xpeer(d)))

    def stage2():
        for d in range(1, NX):
            frm = lax.rem(cx + NX - d, NX)
            rcopy(xs.at[cx], xr.at[frm], sx.at[d - 1], rx.at[d - 1], xpeer(d)).wait_recv()
        v = xr[0].astype(F32) + xr[1].astype(F32) + xr[2].astype(F32) + xr[3].astype(F32)
        hs[...] = v.astype(BF)
        hr[ch] = v.astype(BF)
        for d in range(1, NY):
            go(rcopy(hs, hr.at[ch], sh.at[d - 1], rh.at[d - 1], hpeer(d)))

    def stage3():
        for d in range(1, NY):
            frm = lax.rem(ch + NY - d, NY)
            rcopy(hs, hr.at[frm], sh.at[d - 1], rh.at[d - 1], hpeer(d)).wait_recv()
        v = hr[0].astype(F32) + hr[1].astype(F32) + hr[2].astype(F32) + hr[3].astype(F32)
        fs[...] = v.astype(BF)
        fo[cx] = v.astype(BF)
        for d in range(1, NX):
            go(rcopy(fs, fo.at[cx], sf.at[d - 1], rf.at[d - 1], xpeer(d)))

    def stage4():
        for d in range(1, NX):
            frm = lax.rem(cx + NX - d, NX)
            rcopy(fs, fo.at[frm], sf.at[d - 1], rf.at[d - 1], xpeer(d)).wait_recv()
        go(rcopy(fo, fsib, sc.at[1], rc.at[1], sib))

    def stage5():
        rcopy(fo, fsib, sc.at[1], rc.at[1], sib).wait_recv()
        for t in range(NX):
            at = pl.ds(t * wide, wide)
            wg[mine, at] = fo[t].astype(F32) * (1.0 / (NX * NY * CORES))
            wg[other, at] = fsib[t].astype(F32) * (1.0 / (NX * NY * CORES))

    def asteps(k):
        if k == 0:
            ymsg(4).wait_recv()
        else:
            ymsg((4 - k) % NZ).wait_recv()
            ymsg((k - 4) % NZ).wait_recv()
        zstep(0, k)
        zstep(1, k)

    def total(flow, col, base):
        val = part(col, 0, base, HALF)
        for f in (flow, flow + 1):
            zmsg(f, 3).wait_recv()
            val = val + zr[f, 3].astype(F32)
        return val

    asteps(0)
    for flow in (4, 5, 2, 3):
        zstep(flow, 1)
    stage0()
    ysend(2)
    ysend(-2)
    asteps(1)
    stage1()
    for flow in (4, 5, 2, 3):
        zstep(flow, 2)
    ysend(1)
    ysend(-1)
    stage2()
    asteps(2)
    for flow in (4, 5, 2, 3):
        zstep(flow, 3)
    ysend(0)
    for d in range(1, NB):
        frm = lax.rem(s + NB - d, NB)
        rcopy(ot.at[s], arecv.at[frm], sa.at[d - 1], ra.at[d - 1], {"seq": frm}).wait_recv()
    for c in range(NB // 2):
        t = jnp.concatenate([arecv[2 * c], arecv[2 * c + 1]], axis=0).astype(F32)
        att[0, :, c * BLOCK : (c + 1) * BLOCK] = t.T.astype(BF)
    stage3()
    asteps(3)
    stage4()
    ysb[8] = total(4, p, HALF).astype(BF)
    go(ymsg(8))
    own_b = total(2, y, HALF)
    ymsg(0).wait_recv()
    ng[0, :HALF, :] = (total(0, y, 0) + yrb[0].astype(F32)).astype(BF)
    stage5()
    ymsg(8).wait_recv()
    ng[0, HALF:, :] = (own_b + yrb[8].astype(F32)).astype(BF)
    for c in sent:
        c.wait_send()


def scatter(dproj, w, ot, xall):
    vm = pl.BlockSpec(memory_space=pltpu.VMEM)
    hbm = pl.BlockSpec(memory_space=pltpu.HBM)
    n = NB * BLOCK
    sem = pltpu.SemaphoreType.DMA
    vmem = pltpu.VMEM
    hrow = 3 * HD // CORES
    wide = D // NX
    return pl.pallas_call(
        scatter_kernel,
        out_shape=(
            jax.ShapeDtypeStruct((1, BLOCK, D), BF),
            jax.ShapeDtypeStruct((1, BLOCK, D), BF),
            jax.ShapeDtypeStruct((3 * HD, D), F32),
        ),
        in_specs=[vm, hbm, vm, vm],
        out_specs=(vm, vm, vm),
        scratch_shapes=[
            vmem((3 * HD, D), BF),
            vmem((6, 4, HALF, D), BF),
            vmem((6, 4, HALF, D), BF),
            vmem((9, HALF, D), BF),
            vmem((9, HALF, D), BF),
            vmem((NB, HD, BLOCK), BF),
            vmem((3 * HD, n), BF),
            vmem((3 * HD, D), F32),
            vmem((hrow, D), BF),
            vmem((hrow, D), BF),
            vmem((NX, hrow, wide), BF),
            vmem((NX, hrow, wide), BF),
            vmem((hrow, wide), BF),
            vmem((NY, hrow, wide), BF),
            vmem((hrow, wide), BF),
            vmem((NX, hrow, wide), BF),
            vmem((NX, hrow, wide), BF),
            sem((6, 4)),
            sem((6, 4)),
            sem((9,)),
            sem((9,)),
            sem((NB - 1,)),
            sem((NB - 1,)),
            sem((2,)),
            sem((2,)),
            sem((NX - 1,)),
            sem((NX - 1,)),
            sem((NY - 1,)),
            sem((NY - 1,)),
            sem((NX - 1,)),
            sem((NX - 1,)),
            sem,
        ],
        compiler_params=pltpu.CompilerParams(
            collective_id=1, has_side_effects=True, vmem_limit_bytes=22 * 1024 * 1024
        ),
        name="scatter_reduce",
    )(dproj, w, ot, xall)


def put_kernel(a, b, c, ao, bo, co, sems):
    copies = [
        pltpu.make_async_copy(src, dst, sems.at[t])
        for t, (src, dst) in enumerate(((c, co), (a, ao), (b, bo)))
    ]
    for copy in copies:
        copy.start()
    for copy in copies:
        copy.wait()


def put(a, b, c):
    vm = pl.BlockSpec(memory_space=pltpu.VMEM)
    hbm = pl.BlockSpec(memory_space=pltpu.HBM)
    return pl.pallas_call(
        put_kernel,
        out_shape=tuple(jax.ShapeDtypeStruct(t.shape, t.dtype) for t in (a, b, c)),
        in_specs=[vm, vm, vm],
        out_specs=(hbm, hbm, hbm),
        scratch_shapes=[pltpu.SemaphoreType.DMA((3,))],
        compiler_params=pltpu.CompilerParams(vmem_limit_bytes=4 * 1024 * 1024),
        name="put",
    )(a, b, c)


def local(node_feats, qkv_weight, block_pairs, grad_out):
    operands = (node_feats, qkv_weight, grad_out, jnp.transpose(block_pairs[0]))
    held = [pltpu.with_memory_space_constraint(t, pltpu.HBM) for t in operands]
    xall, b1, b2, kv, kvt, lst = gather(*held)
    ot, dproj = attention(lst, b1, b2, kv, kvt)
    return put(*scatter(dproj, qkv_weight, ot, xall.reshape(NB * BLOCK, D)))


def solution(mesh):
    return jax.shard_map(
        local,
        mesh=mesh,
        in_specs=(
            P("clus", "seq", None),
            P("seq", None),
            P("clus", None, None),
            P("clus", "seq", None),
        ),
        out_specs=(P("clus", "seq", None), P("clus", "seq", None), P("seq", None)),
        check_vma=False,
    )
```

```python
import math

import jax
import jax.numpy as jnp
from jax import lax
from jax.experimental import pallas as pl
from jax.experimental.pallas import tpu as pltpu
from jax.sharding import PartitionSpec as P

F32 = jnp.float32
BF = jnp.bfloat16
HD = 64
BLOCK = 128
NB = 16
BIG = True
PAD = -1e30
COUNT = 16
ROWID = 17
SCALE = 0.125 * math.log2(math.e)


def attn_kernel(lst, b1, b2, kv, kvt, ot, dproj, s_scr, d_scr, acc):
    acc[...] = jnp.zeros_like(acc)

    def at_block(j):
        return pl.ds(pl.multiple_of(j * BLOCK, BLOCK), BLOCK)

    def at_rows(base, ch):
        return pl.ds(pl.multiple_of(base * BLOCK, BLOCK), ch * BLOCK)

    def fold(v):
        return v.reshape(v.shape[0] // 8, 8, BLOCK)

    def scores(r, base, ch, buf, w1, m):
        n = lst[r, COUNT]
        lhs = jnp.concatenate([kv[at_block(lst[r, base + t]), :] for t in range(ch)], axis=0)
        sd = jnp.dot(lhs, w1, preferred_element_type=F32)
        s = jnp.concatenate(
            [
                sd[t * BLOCK : (t + 1) * BLOCK, :BLOCK]
                + jnp.where(base + t < n, 0.0, PAD).astype(F32)
                for t in range(ch)
            ],
            axis=0,
        )
        s_scr[buf, at_rows(base, ch), :] = s
        d_scr[buf, at_rows(base, ch), :] = sd[:, BLOCK:]
        return jnp.maximum(m, jnp.max(fold(s), axis=0))

    def weigh(base, ch, buf, m, l, d):
        e = jnp.exp2((s_scr[buf, at_rows(base, ch), :] - m) * SCALE)
        s_scr[buf, at_rows(base, ch), :] = e
        l = l + jnp.sum(fold(e), axis=0)
        d = d + jnp.sum(fold(e * d_scr[buf, at_rows(base, ch), :]), axis=0)
        return l, d

    def gradients(r, base, ch, buf, w2, linv, delta, oq):
        p = s_scr[buf, at_rows(base, ch), :] * linv
        ds = p * ((d_scr[buf, at_rows(base, ch), :] - delta) * 0.125)
        cat = jnp.concatenate([ds.astype(BF), p.astype(BF)], axis=1)
        cols = [lst[r, base + t] for t in range(ch)]
        lhs = jnp.concatenate([kvt[:, at_block(j)] for j in cols], axis=1)
        oq = oq + jnp.dot(lhs, cat, preferred_element_type=F32)
        g = jnp.dot(cat, w2, preferred_element_type=F32)
        for t in range(ch):
            acc[at_block(cols[t]), :] += g[t * BLOCK : (t + 1) * BLOCK]
        return oq

    def sweep(r, body, state):
        n = lst[r, COUNT]
        n8 = lax.div(n + 3, 8)
        n4 = lax.div(n + 3, 4) - 2 * n8
        if BIG:
            state = lax.fori_loop(0, n8, lambda c, st: body(c * 8, 8, st), state)
            return lax.fori_loop(0, n4, lambda c, st: body(n8 * 8, 4, st), state)
        return lax.fori_loop(0, lax.div(n + 3, 4), lambda c, st: body(c * 4, 4, st), state)

    def rows_max(m):
        return jnp.max(m, axis=0, keepdims=True)

    def close(l, d):
        linv = 1.0 / jnp.sum(l, axis=0, keepdims=True)
        return linv, jnp.sum(d, axis=0, keepdims=True) * linv

    low = jnp.full((8, BLOCK), PAD, F32)
    zero = jnp.zeros((8, BLOCK), F32)
    w1_0 = b1[lst[0, ROWID]]
    w1_1 = b1[lst[1, ROWID]]
    m0 = rows_max(sweep(0, lambda b, ch, m: scores(0, b, ch, 0, w1_0, m), low))

    def second(b, ch, st):
        m, l, d = st
        m = scores(1, b, ch, 1, w1_1, m)
        l, d = weigh(b, ch, 0, m0, l, d)
        return m, l, d

    m1, l0, d0 = sweep(0, second, (low, zero, zero))

    def row(r, carry):
        linv, delta, m = carry
        m = rows_max(m)
        i = lst[r, ROWID]
        far = jnp.minimum(r + 2, NB - 1)
        w1 = b1[lst[far, ROWID]]
        w2 = b2[i]
        buf, buf1, buf2 = lax.rem(r, 3), lax.rem(r + 1, 3), lax.rem(r + 2, 3)

        def body(b, ch, st):
            oq, l, d, mf = st
            mf = scores(far, b, ch, buf2, w1, mf)
            l, d = weigh(b, ch, buf1, m, l, d)
            oq = gradients(r, b, ch, buf, w2, linv, delta, oq)
            return oq, l, d, mf

        oq, l, d, mf = sweep(r, body, (jnp.zeros((BLOCK, 2 * BLOCK), F32), zero, zero, low))
        ot[i] = oq[HD:, BLOCK:].astype(BF)
        dproj[at_block(i), 0:BLOCK] = oq[:, :BLOCK].T.astype(BF)
        linv, delta = close(l, d)
        return linv, delta, mf

    lax.fori_loop(0, NB, row, (*close(l0, d0), m1))

    def fin(i, _):
        a = acc[at_block(i), :].astype(BF)
        q = dproj[at_block(i), 0:BLOCK]
        dproj[at_block(i), :] = jnp.concatenate([q[:, :HD], a], axis=1)
        return 0

    lax.fori_loop(0, NB, fin, 0, unroll=4)


def attention(lst, b1, b2, kv, kvt):
    vm = pl.BlockSpec(memory_space=pltpu.VMEM)
    n = NB * BLOCK
    return pl.pallas_call(
        attn_kernel,
        out_shape=(
            jax.ShapeDtypeStruct((NB, HD, BLOCK), BF),
            jax.ShapeDtypeStruct((n, 3 * HD), BF),
        ),
        in_specs=[pl.BlockSpec(memory_space=pltpu.SMEM), vm, vm, vm, vm],
        out_specs=(vm, vm),
        scratch_shapes=[
            pltpu.VMEM((3, n, BLOCK), F32),
            pltpu.VMEM((3, n, BLOCK), F32),
            pltpu.VMEM((n, BLOCK), F32),
        ],
        compiler_params=pltpu.CompilerParams(vmem_limit_bytes=14 * 1024 * 1024),
        name="attention",
    )(lst, b1, b2, kv, kvt)

MESH = pl.DeviceIdType.MESH
HD = 64
BLOCK = 128
NB = 16
NZ = 8
D = 1024
HALF = 64
QUART = 32
CORES = 2
NX = 4
NY = 4


def dot_t(a, b):
    return lax.dot_general(a, b, (((1,), (1,)), ((), ())), preferred_element_type=F32)


def ring_place():
    s = lax.axis_index("seq")
    y = lax.div(s, NZ)
    z = lax.rem(s, NZ)
    return s, y, z


def greet(peers, meanwhile=None):
    barrier = pltpu.get_barrier_semaphore()
    for peer in peers:
        pl.semaphore_signal(barrier, inc=1, device_id=peer, device_id_type=MESH)
    if meanwhile is not None:
        meanwhile()
    pl.semaphore_wait(barrier, len(peers))


RA = 80
SPLIT = {0: (0, 48), 1: (48, 32), 2: (80, 16), 3: (96, 32)}


def row_lists(pairs):
    one = jnp.float32(1)
    sub = lax.broadcasted_iota(jnp.int32, (BLOCK, BLOCK), 0)
    lane = lax.broadcasted_iota(jnp.int32, (BLOCK, BLOCK), 1)
    sub_nb, lane_nb = sub[:NB], lane[:NB]
    row_hot = jnp.where(sub == pairs[0:1, :], one, 0.0).astype(BF)
    col_hot = jnp.where(sub == pairs[1:2, :], one, 0.0).astype(BF)
    allowed = dot_t(row_hot[:NB], col_hot)
    n_col = jnp.sum(allowed, axis=1, keepdims=True)
    n_row = dot_t(jnp.ones((NB, BLOCK), BF), row_hot)[0:1]
    before = jnp.where(sub < lane, one, 0.0).astype(BF)
    pos = jnp.dot(allowed.astype(BF), before, preferred_element_type=F32)
    lists = jnp.zeros((NB, BLOCK), F32)
    lane_f = lane_nb.astype(F32)
    for t in range(NB):
        hit = jnp.where(pos == t, allowed, 0.0)
        col = jnp.sum(hit * lane_f, axis=1, keepdims=True)
        lists = jnp.where(lane_nb == t, col, lists)
    lists = jnp.where(lane_nb == NB, n_col, lists)
    lists = jnp.where(lane_nb == NB + 1, sub_nb.astype(F32), lists)
    ahead = jnp.logical_or(n_col > n_row, jnp.logical_and(n_col == n_row, sub_nb < lane_nb))
    rank = jnp.sum(jnp.where(ahead, one, 0.0), axis=0, keepdims=True)
    move = jnp.where(jnp.logical_and(sub_nb.astype(F32) == rank, lane_nb < NB), one, 0.0)
    full = jnp.concatenate([lists, jnp.zeros((BLOCK - NB, BLOCK), F32)], axis=0)
    out = jnp.dot(move.astype(BF), full.astype(BF), preferred_element_type=F32)
    return (out + 0.5).astype(jnp.int32)


def gather_kernel(
    x, w_hbm, g_hbm, pairs_hbm,
    xall, b1, b2, kv, kvt, lst,
    w, g, pairs, xg, gsend, grecv, sz, rz, sy, ry, sg, rg, lx, ll, hop,
):
    s, y, z = ring_place()
    p = 1 - y
    up = {"seq": y * NZ + lax.rem(z + 1, NZ)}
    down = {"seq": y * NZ + lax.rem(z + NZ - 1, NZ)}
    across = {"seq": p * NZ + z}
    load = pltpu.make_async_copy(x.at[0], xg.at[s], ll.at[0])
    load_g = pltpu.make_async_copy(g_hbm.at[0], g, ll.at[1])
    load_w = pltpu.make_async_copy(w_hbm, w, ll.at[2])
    load_p = pltpu.make_async_copy(pairs_hbm, pairs, ll.at[3])
    load.start()
    load_g.start()
    load_w.start()
    load_p.start()
    near = [up, down, across]
    greet(near)

    def relay(r):
        for peer in near:
            pl.semaphore_signal(hop.at[r], inc=1, device_id=peer, device_id_type=MESH)
        pl.semaphore_wait(hop.at[r], len(near))

    load.wait()

    def block(col, off):
        return col * NZ + lax.rem(z + off + NZ, NZ)

    def zmsg(flow, k, off, do_start):
        col = p if flow >= 4 else y
        first, rows = (0, RA) if flow < 2 else (RA, BLOCK - RA)
        if k == 3:
            first, rows = SPLIT[flow - 2 if flow >= 4 else flow]
        ref = xg.at[block(col, off), pl.ds(first, rows)]
        c = pltpu.make_async_remote_copy(
            src_ref=ref,
            dst_ref=ref,
            send_sem=sz.at[flow, k],
            recv_sem=rz.at[flow, k],
            device_id=down if flow % 2 else up,
            device_id_type=MESH,
        )
        if do_start:
            c.start()
        return c

    def ymsg(idx, col, do_start):
        off = 0 if idx == 8 else idx
        ref = xg.at[block(col, off), pl.ds(RA, BLOCK - RA) if idx == 8 else pl.ds(0, RA)]
        c = pltpu.make_async_remote_copy(
            src_ref=ref,
            dst_ref=ref,
            send_sem=sy.at[idx],
            recv_sem=ry.at[idx],
            device_id=across,
            device_id_type=MESH,
        )
        if do_start:
            c.start()
        return c

    sent = []
    outs = []
    sent.append(ymsg(8, y, True))
    for flow in (0, 1, 2, 3):
        sent.append(zmsg(flow, 0, 0, True))
    sent.append(ymsg(0, y, True))

    def compute(b, n):
        xb = xg[b]
        at = pl.ds(pl.multiple_of(b * BLOCK, BLOCK), BLOCK)
        kvf = dot_t(xb, w[HD:, :])
        qt = dot_t(w[:HD, :], xb)
        zero = jnp.zeros((HD, BLOCK), F32)
        kv[at, :] = kvf.astype(BF)
        kvt[:, at] = kvf.T.astype(BF)
        b1[b, :HD, :] = jnp.concatenate([qt, zero], axis=1).astype(BF)
        b2[b, :BLOCK, :] = jnp.concatenate([qt, zero], axis=0).T.astype(BF)
        c = pltpu.make_async_copy(xg.at[b], xall.at[b], lx.at[n])
        c.start()
        outs.append(c)

    relay(0)
    load_g.wait()
    for c in range(NB // 2):
        t = g[:, c * BLOCK : (c + 1) * BLOCK].astype(F32).T.astype(BF)
        gsend[2 * c] = t[:HD]
        gsend[2 * c + 1] = t[HD:]

    def gmsg(d):
        to = lax.rem(s + d, NB)
        return pltpu.make_async_remote_copy(
            src_ref=gsend.at[to],
            dst_ref=grecv.at[s],
            send_sem=sg.at[d - 1],
            recv_sem=rg.at[d - 1],
            device_id={"seq": to},
            device_id_type=MESH,
        )

    relay(1)
    load_w.wait()
    compute(s, 0)
    relay(2)
    ymsg(8, p, False).wait_recv()
    for flow in (4, 5):
        sent.append(zmsg(flow, 0, 0, True))
    relay(3)
    for d in range(1, NB):
        c = gmsg(d)
        c.start()
        sent.append(c)
    grecv[s] = gsend[s]
    load_p.wait()
    lst[...] = row_lists(pairs[...])

    def place(t, _):
        gt = grecv[t].astype(F32)
        zero = jnp.zeros((HD, BLOCK), F32)
        b1[t, HD:, :] = jnp.concatenate([zero, gt], axis=1).astype(BF)
        b2[t, BLOCK:, :] = jnp.concatenate([zero, gt], axis=0).T.astype(BF)
        return 0

    def place_all():
        for d in range(1, NB):
            frm = lax.rem(s + NB - d, NB)
            pltpu.make_async_remote_copy(
                src_ref=gsend.at[s],
                dst_ref=grecv.at[frm],
                send_sem=sg.at[d - 1],
                recv_sem=rg.at[d - 1],
                device_id={"seq": frm},
                device_id_type=MESH,
            ).wait_recv()
        lax.fori_loop(0, NB, place, 0)

    n = 1
    for k in range(4):
        for flow in (0, 1, 2, 3, 4, 5):
            off = (k + 1) if flow % 2 else -(k + 1)
            zmsg(flow, k, off, False).wait_recv()
            if k < 3:
                sent.append(zmsg(flow, k + 1, off, True))
            if flow < 2 and k < 3:
                sent.append(ymsg(off % NZ, y, True))
            if flow == 1 and k == 3:
                sent.append(ymsg(4, y, True))
        for off in [-(k + 1), k + 1][: 2 if k < 3 else 1]:
            compute(block(y, off), n)
            n += 1
        for off in [-k, k][: 2 if k > 0 else 1]:
            ymsg(off % NZ, p, False).wait_recv()
            compute(block(p, off), n)
            n += 1
        if k == 2:
            place_all()
    for c in outs:
        c.wait()
    outs.clear()
    ymsg(4, p, False).wait_recv()
    compute(block(p, 4), n)
    for c in sent:
        c.wait_send()
    for c in outs:
        c.wait()


def gather(x, w, g, pairs):
    vm = pl.BlockSpec(memory_space=pltpu.VMEM)
    anyw = pl.BlockSpec(memory_space=pl.ANY)
    hbm = pl.BlockSpec(memory_space=pltpu.HBM)
    n = NB * BLOCK
    sem = pltpu.SemaphoreType.DMA
    return pl.pallas_call(
        gather_kernel,
        out_shape=(
            jax.ShapeDtypeStruct((NB, BLOCK, D), BF),
            jax.ShapeDtypeStruct((NB, BLOCK, 2 * BLOCK), BF),
            jax.ShapeDtypeStruct((NB, 2 * BLOCK, BLOCK), BF),
            jax.ShapeDtypeStruct((n, BLOCK), BF),
            jax.ShapeDtypeStruct((BLOCK, n), BF),
            jax.ShapeDtypeStruct((NB, BLOCK), jnp.int32),
        ),
        in_specs=[hbm, hbm, hbm, hbm],
        out_specs=(anyw, vm, vm, vm, vm, vm),
        scratch_shapes=[
            pltpu.VMEM((3 * HD, D), BF),
            pltpu.VMEM((BLOCK, D), BF),
            pltpu.VMEM((2, BLOCK), jnp.int32),
            pltpu.VMEM((NB, BLOCK, D), BF),
            pltpu.VMEM((NB, HD, BLOCK), BF),
            pltpu.VMEM((NB, HD, BLOCK), BF),
            sem((6, 4)),
            sem((6, 4)),
            sem((9,)),
            sem((9,)),
            sem((NB - 1,)),
            sem((NB - 1,)),
            sem((NB,)),
            sem((4,)),
            pltpu.SemaphoreType.REGULAR((4,)),
        ],
        compiler_params=pltpu.CompilerParams(
            collective_id=0, has_side_effects=True, vmem_limit_bytes=20 * 1024 * 1024
        ),
        name="gather_project",
    )(x, w, g, pairs)


def scatter_kernel(
    dproj, w, ot, xv,
    att, ng, wg,
    px, zs, zr, ysb, yrb, arecv, dt, dwf, cs, cr, xs, xr, hs, hr, fs, fo, fsib,
    sz, rz, sy, ry, sa, ra, sc, rc, sx, rx, sh, rh, sf, rf,
):
    s, y, z = ring_place()
    p = 1 - y
    up = {"seq": y * NZ + lax.rem(z + 1, NZ)}
    down = {"seq": y * NZ + lax.rem(z + NZ - 1, NZ)}
    across = {"seq": p * NZ + z}
    q = lax.axis_index("clus")
    cx = lax.div(q, NY * CORES)
    ch = lax.rem(lax.div(q, CORES), NY)
    cc = lax.rem(q, CORES)
    sib = {"clus": q + 1 - 2 * cc}

    def xpeer(d):
        return {"clus": lax.rem(cx + d, NX) * (NY * CORES) + ch * CORES + cc}

    def hpeer(d):
        return {"clus": cx * (NY * CORES) + lax.rem(ch + d, NY) * CORES + cc}

    def terms():
        def step(t, _):
            at = pl.ds(pl.multiple_of(t * 256, 256), 256)
            px[:, at] = jnp.dot(dproj[...], w[:, at], preferred_element_type=F32).astype(BF)
            return 0

        lax.fori_loop(0, D // 256, step, 0)
        arecv[s] = ot[s]

    greet(
        [{"seq": lax.rem(s + d, NB)} for d in range(1, NB)]
        + [sib]
        + [xpeer(d) for d in range(1, NX)]
        + [hpeer(d) for d in range(1, NY)],
        terms,
    )

    def block(col, off):
        return col * NZ + lax.rem(z + off + NZ, NZ)

    def part(col, off, first, rows):
        b = block(col, off)
        return px.at[pl.ds(pl.multiple_of(b * BLOCK + first, QUART), rows), :]

    sent = []

    def rcopy(src, dst, ss, rs, dev):
        return pltpu.make_async_remote_copy(
            src_ref=src, dst_ref=dst, send_sem=ss, recv_sem=rs,
            device_id=dev, device_id_type=MESH,
        )

    def span(flow, k):
        if k == 0:
            return pl.ds(QUART if flow % 2 else 0, QUART)
        return pl.ds(0, HALF)

    def zmsg(flow, k):
        at = span(flow, k)
        src = zs.at[flow, k, at]
        if k == 0 and flow >= 2:
            lo = QUART if flow % 2 else 0
            src = part(p if flow >= 4 else y, 4, HALF + lo, QUART)
        return rcopy(
            src, zr.at[flow, k, at], sz.at[flow, k], rz.at[flow, k],
            down if flow % 2 else up,
        )

    def ymsg(idx):
        src = ysb if idx == 8 else part(p, idx, 0, HALF)
        return rcopy(src, yrb.at[idx], sy.at[idx], ry.at[idx], across)

    def go(c):
        c.start()
        sent.append(c)

    def zstep(flow, k):
        col = p if flow >= 4 else y
        base = 0 if flow < 2 else HALF
        off = (4 - k) * (-1 if flow % 2 else 1)
        lo = QUART if flow % 2 else 0
        if k == 0:
            if flow < 2:
                val = part(col, off, lo, QUART)[...].astype(F32)
                val = val + yrb[off % NZ, lo : lo + QUART, :].astype(F32)
                zs[flow, 0, lo : lo + QUART, :] = val.astype(BF)
        else:
            val = part(col, off, base, HALF)[...].astype(F32)
            if flow < 2:
                val = val + yrb[off % NZ].astype(F32)
            zmsg(flow, k - 1).wait_recv()
            if k == 1:
                zs[flow, 1, QUART - lo : HALF - lo, :] = val[QUART - lo : HALF - lo].astype(BF)
                zs[flow, 1, lo : lo + QUART, :] = (
                    val[lo : lo + QUART] + zr[flow, 0, lo : lo + QUART, :].astype(F32)
                ).astype(BF)
            else:
                zs[flow, k] = (val + zr[flow, k - 1].astype(F32)).astype(BF)
        go(zmsg(flow, k))

    def ysend(off):
        go(ymsg(off % NZ))

    for flow in (4, 5):
        zstep(flow, 0)
    ysend(4)
    for flow in (2, 3):
        zstep(flow, 0)
    ysend(3)
    ysend(-3)
    for d in range(1, NB):
        to = lax.rem(s + d, NB)
        go(rcopy(ot.at[to], arecv.at[s], sa.at[d - 1], ra.at[d - 1], {"seq": to}))

    def turn(t, _):
        at = pl.ds(pl.multiple_of(t * BLOCK, BLOCK), BLOCK)
        v = jnp.concatenate([dproj[at, :].astype(F32), jnp.zeros((BLOCK, HD), F32)], axis=1)
        dt[:, at] = v.T[: 3 * HD].astype(BF)
        return 0

    def wstep(t, _):
        at = pl.ds(pl.multiple_of(t * 256, 256), 256)
        dwf[:, at] = jnp.dot(dt[...], xv[:, at], preferred_element_type=F32)
        return 0

    hrow = 3 * HD // CORES
    mine = pl.ds(pl.multiple_of(cc * hrow, QUART), hrow)
    other = pl.ds(pl.multiple_of((1 - cc) * hrow, QUART), hrow)
    wide = D // NX

    def stage0():
        lax.fori_loop(0, NB, turn, 0)
        lax.fori_loop(0, D // 256, wstep, 0)
        cs[...] = dwf[other, :].astype(BF)
        go(rcopy(cs, cr, sc.at[0], rc.at[0], sib))

    def stage1():
        rcopy(cs, cr, sc.at[0], rc.at[0], sib).wait_recv()
        v = dwf[mine, :] + cr[...].astype(F32)
        for t in range(NX):
            xs[t] = v[:, t * wide : (t + 1) * wide].astype(BF)
        xr[cx] = xs[cx]
        for d in range(1, NX):
            go(rcopy(xs.at[lax.rem(cx + d, NX)], xr.at[cx], sx.at[d - 1], rx.at[d - 1], xpeer(d)))

    def stage2():
        for d in range(1, NX):
            frm = lax.rem(cx + NX - d, NX)
            rcopy(xs.at[cx], xr.at[frm], sx.at[d - 1], rx.at[d - 1], xpeer(d)).wait_recv()
        v = xr[0].astype(F32) + xr[1].astype(F32) + xr[2].astype(F32) + xr[3].astype(F32)
        hs[...] = v.astype(BF)
        hr[ch] = v.astype(BF)
        for d in range(1, NY):
            go(rcopy(hs, hr.at[ch], sh.at[d - 1], rh.at[d - 1], hpeer(d)))

    def stage3():
        for d in range(1, NY):
            frm = lax.rem(ch + NY - d, NY)
            rcopy(hs, hr.at[frm], sh.at[d - 1], rh.at[d - 1], hpeer(d)).wait_recv()
        v = hr[0].astype(F32) + hr[1].astype(F32) + hr[2].astype(F32) + hr[3].astype(F32)
        fs[...] = v.astype(BF)
        fo[cx] = v.astype(BF)
        for d in range(1, NX):
            go(rcopy(fs, fo.at[cx], sf.at[d - 1], rf.at[d - 1], xpeer(d)))

    def stage4():
        for d in range(1, NX):
            frm = lax.rem(cx + NX - d, NX)
            rcopy(fs, fo.at[frm], sf.at[d - 1], rf.at[d - 1], xpeer(d)).wait_recv()
        go(rcopy(fo, fsib, sc.at[1], rc.at[1], sib))

    def stage5():
        rcopy(fo, fsib, sc.at[1], rc.at[1], sib).wait_recv()
        for t in range(NX):
            at = pl.ds(t * wide, wide)
            wg[mine, at] = fo[t].astype(F32) * (1.0 / (NX * NY * CORES))
            wg[other, at] = fsib[t].astype(F32) * (1.0 / (NX * NY * CORES))

    def asteps(k):
        if k == 0:
            ymsg(4).wait_recv()
        else:
            ymsg((4 - k) % NZ).wait_recv()
            ymsg((k - 4) % NZ).wait_recv()
        zstep(0, k)
        zstep(1, k)

    def total(flow, col, base):
        val = part(col, 0, base, HALF)[...].astype(F32)
        for f in (flow, flow + 1):
            zmsg(f, 3).wait_recv()
            val = val + zr[f, 3].astype(F32)
        return val

    asteps(0)
    for flow in (4, 5, 2, 3):
        zstep(flow, 1)
    stage0()
    ysend(2)
    ysend(-2)
    asteps(1)
    stage1()
    for flow in (4, 5, 2, 3):
        zstep(flow, 2)
    ysend(1)
    ysend(-1)
    stage2()
    asteps(2)
    for flow in (4, 5, 2, 3):
        zstep(flow, 3)
    ysend(0)
    for d in range(1, NB):
        frm = lax.rem(s + NB - d, NB)
        rcopy(ot.at[s], arecv.at[frm], sa.at[d - 1], ra.at[d - 1], {"seq": frm}).wait_recv()
    for c in range(NB // 2):
        t = jnp.concatenate([arecv[2 * c], arecv[2 * c + 1]], axis=0).astype(F32)
        att[0, :, c * BLOCK : (c + 1) * BLOCK] = t.T.astype(BF)
    stage3()
    asteps(3)
    stage4()
    ysb[...] = total(4, p, HALF).astype(BF)
    go(ymsg(8))
    own_b = total(2, y, HALF)
    ymsg(0).wait_recv()
    ng[0, :HALF, :] = (total(0, y, 0) + yrb[0].astype(F32)).astype(BF)
    stage5()
    ymsg(8).wait_recv()
    ng[0, HALF:, :] = (own_b + yrb[8].astype(F32)).astype(BF)
    for c in sent:
        c.wait_send()


def scatter(dproj, w, ot, xall):
    vm = pl.BlockSpec(memory_space=pltpu.VMEM)
    n = NB * BLOCK
    sem = pltpu.SemaphoreType.DMA
    vmem = pltpu.VMEM
    hrow = 3 * HD // CORES
    wide = D // NX
    return pl.pallas_call(
        scatter_kernel,
        out_shape=(
            jax.ShapeDtypeStruct((1, BLOCK, D), BF),
            jax.ShapeDtypeStruct((1, BLOCK, D), BF),
            jax.ShapeDtypeStruct((3 * HD, D), F32),
        ),
        in_specs=[vm, vm, vm, vm],
        out_specs=(vm, vm, vm),
        scratch_shapes=[
            vmem((n, D), BF),
            vmem((6, 4, HALF, D), BF),
            vmem((6, 4, HALF, D), BF),
            vmem((HALF, D), BF),
            vmem((9, HALF, D), BF),
            vmem((NB, HD, BLOCK), BF),
            vmem((3 * HD, n), BF),
            vmem((3 * HD, D), F32),
            vmem((hrow, D), BF),
            vmem((hrow, D), BF),
            vmem((NX, hrow, wide), BF),
            vmem((NX, hrow, wide), BF),
            vmem((hrow, wide), BF),
            vmem((NY, hrow, wide), BF),
            vmem((hrow, wide), BF),
            vmem((NX, hrow, wide), BF),
            vmem((NX, hrow, wide), BF),
            sem((6, 4)),
            sem((6, 4)),
            sem((9,)),
            sem((9,)),
            sem((NB - 1,)),
            sem((NB - 1,)),
            sem((2,)),
            sem((2,)),
            sem((NX - 1,)),
            sem((NX - 1,)),
            sem((NY - 1,)),
            sem((NY - 1,)),
            sem((NX - 1,)),
            sem((NX - 1,)),
        ],
        compiler_params=pltpu.CompilerParams(
            collective_id=1, has_side_effects=True, vmem_limit_bytes=24 * 1024 * 1024
        ),
        name="scatter_reduce",
    )(dproj, w, ot, xall)


def put_kernel(a, b, c, ao, bo, co, sems):
    copies = [
        pltpu.make_async_copy(src, dst, sems.at[t])
        for t, (src, dst) in enumerate(((c, co), (a, ao), (b, bo)))
    ]
    for copy in copies:
        copy.start()
    for copy in copies:
        copy.wait()


def put(a, b, c):
    vm = pl.BlockSpec(memory_space=pltpu.VMEM)
    hbm = pl.BlockSpec(memory_space=pltpu.HBM)
    return pl.pallas_call(
        put_kernel,
        out_shape=tuple(jax.ShapeDtypeStruct(t.shape, t.dtype) for t in (a, b, c)),
        in_specs=[vm, vm, vm],
        out_specs=(hbm, hbm, hbm),
        scratch_shapes=[pltpu.SemaphoreType.DMA((3,))],
        compiler_params=pltpu.CompilerParams(vmem_limit_bytes=4 * 1024 * 1024),
        name="put",
    )(a, b, c)


def local(node_feats, qkv_weight, block_pairs, grad_out):
    operands = (node_feats, qkv_weight, grad_out, jnp.transpose(block_pairs[0]))
    held = [pltpu.with_memory_space_constraint(t, pltpu.HBM) for t in operands]
    xall, b1, b2, kv, kvt, lst = gather(*held)
    ot, dproj = attention(lst, b1, b2, kv, kvt)
    return put(*scatter(dproj, qkv_weight, ot, xall.reshape(NB * BLOCK, D)))


def solution(mesh):
    return jax.shard_map(
        local,
        mesh=mesh,
        in_specs=(
            P("clus", "seq", None),
            P("seq", None),
            P("clus", None, None),
            P("clus", "seq", None),
        ),
        out_specs=(P("clus", "seq", None), P("clus", "seq", None), P("seq", None)),
        check_vma=False,
    )
```

```python
import math

import jax
import jax.numpy as jnp
from jax import lax
from jax.experimental import pallas as pl
from jax.experimental.pallas import tpu as pltpu
from jax.sharding import PartitionSpec as P

F32 = jnp.float32
BF = jnp.bfloat16
HD = 64
BLOCK = 128
NB = 16
SIZES = (1, 2, 4, 6, 8, 10, 12, 14, 16)
PAD = -1e30
COUNT = 16
ROWID = 17
SCALE = 0.125 * math.log2(math.e)


def attn_kernel(lst, b1, b2, kv, ot, dproj, s_scr, d_scr, acc):
    acc[...] = jnp.zeros_like(acc)

    def at_block(j):
        return pl.ds(pl.multiple_of(j * BLOCK, BLOCK), BLOCK)

    def at_rows(base, ch):
        return pl.ds(pl.multiple_of(base * BLOCK, BLOCK), ch * BLOCK)

    def fold(v):
        return v.reshape(v.shape[0] // 8, 8, BLOCK)

    def scores(r, base, ch, buf, w1, m):
        n = lst[r, COUNT]
        lhs = jnp.concatenate([kv[at_block(lst[r, base + t]), :] for t in range(ch)], axis=0)
        sd = jnp.dot(lhs, w1, preferred_element_type=F32)
        s = jnp.concatenate(
            [
                sd[t * BLOCK : (t + 1) * BLOCK, :BLOCK]
                + jnp.where(base + t < n, 0.0, PAD).astype(F32)
                for t in range(ch)
            ],
            axis=0,
        )
        s_scr[buf, at_rows(base, ch), :] = s
        d_scr[buf, at_rows(base, ch), :] = sd[:, BLOCK:]
        return jnp.maximum(m, jnp.max(fold(s), axis=0))

    def weigh(base, ch, buf, m, l, d):
        e = jnp.exp2((s_scr[buf, at_rows(base, ch), :] - m) * SCALE)
        s_scr[buf, at_rows(base, ch), :] = e
        l = l + jnp.sum(fold(e), axis=0)
        d = d + jnp.sum(fold(e * d_scr[buf, at_rows(base, ch), :]), axis=0)
        return l, d

    def gradients(r, base, ch, buf, w2, linv, delta, oq):
        p = s_scr[buf, at_rows(base, ch), :] * linv
        ds = p * ((d_scr[buf, at_rows(base, ch), :] - delta) * 0.125)
        cat = jnp.concatenate([ds.astype(BF), p.astype(BF)], axis=1)
        cols = [lst[r, base + t] for t in range(ch)]
        rhs = jnp.concatenate([kv[at_block(j), :] for j in cols], axis=0)
        oq = oq + lax.dot_general(cat, rhs, (((0,), (0,)), ((), ())), preferred_element_type=F32)
        g = jnp.dot(cat, w2, preferred_element_type=F32)
        for t in range(ch):
            acc[at_block(cols[t]), :] += g[t * BLOCK : (t + 1) * BLOCK]
        return oq

    def sweep(r, body, state):
        n = lst[r, COUNT]
        which = 0
        for size in SIZES[:-1]:
            which = which + (n > size).astype(jnp.int32)
        arms = [lambda st, ch=ch: body(0, ch, st) for ch in SIZES]
        return lax.switch(which, arms, state)

    def rows_max(m):
        return jnp.max(m, axis=0, keepdims=True)

    def close(l, d):
        linv = 1.0 / jnp.sum(l, axis=0, keepdims=True)
        return linv, jnp.sum(d, axis=0, keepdims=True) * linv

    low = jnp.full((8, BLOCK), PAD, F32)
    zero = jnp.zeros((8, BLOCK), F32)
    w1_0 = b1[lst[0, ROWID]]
    w1_1 = b1[lst[1, ROWID]]
    m0 = rows_max(sweep(0, lambda b, ch, m: scores(0, b, ch, 0, w1_0, m), low))

    def second(b, ch, st):
        m, l, d = st
        m = scores(1, b, ch, 1, w1_1, m)
        l, d = weigh(b, ch, 0, m0, l, d)
        return m, l, d

    m1, l0, d0 = sweep(0, second, (low, zero, zero))

    def row(r, carry):
        linv, delta, m = carry
        m = rows_max(m)
        i = lst[r, ROWID]
        far = jnp.minimum(r + 2, NB - 1)
        w1 = b1[lst[far, ROWID]]
        w2 = b2[i]
        buf, buf1, buf2 = lax.rem(r, 3), lax.rem(r + 1, 3), lax.rem(r + 2, 3)

        def body(b, ch, st):
            oq, l, d, mf = st
            mf = scores(far, b, ch, buf2, w1, mf)
            l, d = weigh(b, ch, buf1, m, l, d)
            oq = gradients(r, b, ch, buf, w2, linv, delta, oq)
            return oq, l, d, mf

        oq, l, d, mf = sweep(r, body, (jnp.zeros((2 * BLOCK, BLOCK), F32), zero, zero, low))
        ot[i] = oq[BLOCK:, :].T[HD:].astype(BF)
        dproj[at_block(i), 0:BLOCK] = oq[:BLOCK, :].astype(BF)
        linv, delta = close(l, d)
        return linv, delta, mf

    lax.fori_loop(0, NB, row, (*close(l0, d0), m1))

    def fin(i, _):
        a = acc[at_block(i), :].astype(BF)
        q = dproj[at_block(i), 0:BLOCK]
        dproj[at_block(i), :] = jnp.concatenate([q[:, :HD], a], axis=1)
        return 0

    lax.fori_loop(0, NB, fin, 0, unroll=4)


def attention(lst, b1, b2, kv):
    vm = pl.BlockSpec(memory_space=pltpu.VMEM)
    n = NB * BLOCK
    return pl.pallas_call(
        attn_kernel,
        out_shape=(
            jax.ShapeDtypeStruct((NB, HD, BLOCK), BF),
            jax.ShapeDtypeStruct((n, 3 * HD), BF),
        ),
        in_specs=[pl.BlockSpec(memory_space=pltpu.SMEM), vm, vm, vm],
        out_specs=(vm, vm),
        scratch_shapes=[
            pltpu.VMEM((3, n, BLOCK), F32),
            pltpu.VMEM((3, n, BLOCK), F32),
            pltpu.VMEM((n, BLOCK), F32),
        ],
        compiler_params=pltpu.CompilerParams(vmem_limit_bytes=14 * 1024 * 1024),
        name="attention",
    )(lst, b1, b2, kv)

MESH = pl.DeviceIdType.MESH
HD = 64
BLOCK = 128
NB = 16
NZ = 8
D = 1024
HALF = 64
QUART = 32
CORES = 2
NX = 4
NY = 4


def dot_t(a, b):
    return lax.dot_general(a, b, (((1,), (1,)), ((), ())), preferred_element_type=F32)


def ring_place():
    s = lax.axis_index("seq")
    y = lax.div(s, NZ)
    z = lax.rem(s, NZ)
    return s, y, z


def greet(peers, meanwhile=None):
    barrier = pltpu.get_barrier_semaphore()
    for peer in peers:
        pl.semaphore_signal(barrier, inc=1, device_id=peer, device_id_type=MESH)
    if meanwhile is not None:
        meanwhile()
    pl.semaphore_wait(barrier, len(peers))


RA = 80
SPLIT = {0: (0, 48), 1: (48, 32), 2: (80, 16), 3: (96, 32)}


def row_lists(pairs):
    one = jnp.float32(1)
    sub = lax.broadcasted_iota(jnp.int32, (BLOCK, BLOCK), 0)
    lane = lax.broadcasted_iota(jnp.int32, (BLOCK, BLOCK), 1)
    sub_nb, lane_nb = sub[:NB], lane[:NB]
    row_hot = jnp.where(sub == pairs[0:1, :], one, 0.0).astype(BF)
    col_hot = jnp.where(sub == pairs[1:2, :], one, 0.0).astype(BF)
    allowed = dot_t(row_hot[:NB], col_hot)
    n_col = jnp.sum(allowed, axis=1, keepdims=True)
    n_row = dot_t(jnp.ones((NB, BLOCK), BF), row_hot)[0:1]
    before = jnp.where(sub < lane, one, 0.0).astype(BF)
    pos = jnp.dot(allowed.astype(BF), before, preferred_element_type=F32)
    lists = jnp.zeros((NB, BLOCK), F32)
    lane_f = lane_nb.astype(F32)
    for t in range(NB):
        hit = jnp.where(pos == t, allowed, 0.0)
        col = jnp.sum(hit * lane_f, axis=1, keepdims=True)
        lists = jnp.where(lane_nb == t, col, lists)
    lists = jnp.where(lane_nb == NB, n_col, lists)
    lists = jnp.where(lane_nb == NB + 1, sub_nb.astype(F32), lists)
    ahead = jnp.logical_or(n_col > n_row, jnp.logical_and(n_col == n_row, sub_nb < lane_nb))
    rank = jnp.sum(jnp.where(ahead, one, 0.0), axis=0, keepdims=True)
    move = jnp.where(jnp.logical_and(sub_nb.astype(F32) == rank, lane_nb < NB), one, 0.0)
    full = jnp.concatenate([lists, jnp.zeros((BLOCK - NB, BLOCK), F32)], axis=0)
    out = jnp.dot(move.astype(BF), full.astype(BF), preferred_element_type=F32)
    return (out + 0.5).astype(jnp.int32)


def gather_kernel(
    x, w_hbm, g_hbm, pairs_hbm,
    xall, b1, b2, kv, lst,
    w, g, pairs, xg, gsend, grecv, sz, rz, sy, ry, sg, rg, lx, ll, hop,
):
    s, y, z = ring_place()
    p = 1 - y
    up = {"seq": y * NZ + lax.rem(z + 1, NZ)}
    down = {"seq": y * NZ + lax.rem(z + NZ - 1, NZ)}
    across = {"seq": p * NZ + z}
    load = pltpu.make_async_copy(x.at[0], xg.at[s], ll.at[0])
    load_g = pltpu.make_async_copy(g_hbm.at[0], g, ll.at[1])
    load_w = pltpu.make_async_copy(w_hbm.at[pl.ds(HD, BLOCK)], w.at[pl.ds(0, BLOCK)], ll.at[2])
    load_q = pltpu.make_async_copy(w_hbm.at[pl.ds(0, HD)], w.at[pl.ds(BLOCK, HD)], ll.at[4])
    load_p = pltpu.make_async_copy(pairs_hbm, pairs, ll.at[3])
    load.start()
    load_g.start()
    load_w.start()
    load_q.start()
    load_p.start()
    near = [up, down, across]
    greet(near)

    def relay(r):
        for peer in near:
            pl.semaphore_signal(hop.at[r], inc=1, device_id=peer, device_id_type=MESH)
        pl.semaphore_wait(hop.at[r], len(near))

    load.wait()

    def block(col, off):
        return col * NZ + lax.rem(z + off + NZ, NZ)

    def zmsg(flow, k, off, do_start):
        col = p if flow >= 4 else y
        first, rows = (0, RA) if flow < 2 else (RA, BLOCK - RA)
        if k == 3:
            first, rows = SPLIT[flow - 2 if flow >= 4 else flow]
        ref = xg.at[block(col, off), pl.ds(first, rows)]
        c = pltpu.make_async_remote_copy(
            src_ref=ref,
            dst_ref=ref,
            send_sem=sz.at[flow, k],
            recv_sem=rz.at[flow, k],
            device_id=down if flow % 2 else up,
            device_id_type=MESH,
        )
        if do_start:
            c.start()
        return c

    def ymsg(idx, col, do_start):
        off = 0 if idx == 8 else idx
        ref = xg.at[block(col, off), pl.ds(RA, BLOCK - RA) if idx == 8 else pl.ds(0, RA)]
        c = pltpu.make_async_remote_copy(
            src_ref=ref,
            dst_ref=ref,
            send_sem=sy.at[idx],
            recv_sem=ry.at[idx],
            device_id=across,
            device_id_type=MESH,
        )
        if do_start:
            c.start()
        return c

    sent = []
    outs = []
    sent.append(ymsg(8, y, True))
    for flow in (0, 1, 2, 3):
        sent.append(zmsg(flow, 0, 0, True))
    sent.append(ymsg(0, y, True))

    def compute(b, n):
        xb = xg[b]
        at = pl.ds(pl.multiple_of(b * BLOCK, BLOCK), BLOCK)
        proj = dot_t(xb, w[...])
        q = jnp.concatenate([proj[:, BLOCK:], jnp.zeros((BLOCK, HD), F32)], axis=1)
        kv[at, :] = proj[:, :BLOCK].astype(BF)
        b1[b, :HD, :] = jnp.concatenate([q.T[:HD], jnp.zeros((HD, BLOCK), F32)], axis=1).astype(BF)
        b2[b, :BLOCK, :] = q.astype(BF)
        c = pltpu.make_async_copy(xg.at[b], xall.at[b], lx.at[n])
        c.start()
        outs.append(c)

    relay(0)
    load_g.wait()
    for c in range(NB // 2):
        t = g[:, c * BLOCK : (c + 1) * BLOCK].astype(F32).T.astype(BF)
        gsend[2 * c] = t[:HD]
        gsend[2 * c + 1] = t[HD:]

    def gmsg(d):
        to = lax.rem(s + d, NB)
        return pltpu.make_async_remote_copy(
            src_ref=gsend.at[to],
            dst_ref=grecv.at[s],
            send_sem=sg.at[d - 1],
            recv_sem=rg.at[d - 1],
            device_id={"seq": to},
            device_id_type=MESH,
        )

    relay(1)
    load_w.wait()
    load_q.wait()
    compute(s, 0)
    relay(2)
    ymsg(8, p, False).wait_recv()
    for flow in (4, 5):
        sent.append(zmsg(flow, 0, 0, True))
    relay(3)
    for d in range(1, NB):
        c = gmsg(d)
        c.start()
        sent.append(c)
    grecv[s] = gsend[s]
    load_p.wait()
    lst[...] = row_lists(pairs[...])

    def place(t, _):
        gt = grecv[t].astype(F32)
        zero = jnp.zeros((HD, BLOCK), F32)
        b1[t, HD:, :] = jnp.concatenate([zero, gt], axis=1).astype(BF)
        b2[t, BLOCK:, :] = jnp.concatenate([zero, gt], axis=0).T.astype(BF)
        return 0

    def place_all():
        for d in range(1, NB):
            frm = lax.rem(s + NB - d, NB)
            pltpu.make_async_remote_copy(
                src_ref=gsend.at[s],
                dst_ref=grecv.at[frm],
                send_sem=sg.at[d - 1],
                recv_sem=rg.at[d - 1],
                device_id={"seq": frm},
                device_id_type=MESH,
            ).wait_recv()
        lax.fori_loop(0, NB, place, 0)

    n = 1
    for k in range(4):
        for flow in (0, 1, 2, 3, 4, 5):
            off = (k + 1) if flow % 2 else -(k + 1)
            zmsg(flow, k, off, False).wait_recv()
            if k < 3:
                sent.append(zmsg(flow, k + 1, off, True))
            if flow < 2 and k < 3:
                sent.append(ymsg(off % NZ, y, True))
            if flow == 1 and k == 3:
                sent.append(ymsg(4, y, True))
        for off in [-(k + 1), k + 1][: 2 if k < 3 else 1]:
            compute(block(y, off), n)
            n += 1
        for off in [-k, k][: 2 if k > 0 else 1]:
            ymsg(off % NZ, p, False).wait_recv()
            compute(block(p, off), n)
            n += 1
        if k == 2:
            place_all()
    for c in outs:
        c.wait()
    outs.clear()
    ymsg(4, p, False).wait_recv()
    compute(block(p, 4), n)
    for c in sent:
        c.wait_send()
    for c in outs:
        c.wait()


def gather(x, w, g, pairs):
    vm = pl.BlockSpec(memory_space=pltpu.VMEM)
    anyw = pl.BlockSpec(memory_space=pl.ANY)
    hbm = pl.BlockSpec(memory_space=pltpu.HBM)
    n = NB * BLOCK
    sem = pltpu.SemaphoreType.DMA
    return pl.pallas_call(
        gather_kernel,
        out_shape=(
            jax.ShapeDtypeStruct((NB, BLOCK, D), BF),
            jax.ShapeDtypeStruct((NB, BLOCK, 2 * BLOCK), BF),
            jax.ShapeDtypeStruct((NB, 2 * BLOCK, BLOCK), BF),
            jax.ShapeDtypeStruct((n, BLOCK), BF),
            jax.ShapeDtypeStruct((NB, BLOCK), jnp.int32),
        ),
        in_specs=[hbm, hbm, hbm, hbm],
        out_specs=(anyw, vm, vm, vm, vm),
        scratch_shapes=[
            pltpu.VMEM((3 * HD, D), BF),
            pltpu.VMEM((BLOCK, D), BF),
            pltpu.VMEM((2, BLOCK), jnp.int32),
            pltpu.VMEM((NB, BLOCK, D), BF),
            pltpu.VMEM((NB, HD, BLOCK), BF),
            pltpu.VMEM((NB, HD, BLOCK), BF),
            sem((6, 4)),
            sem((6, 4)),
            sem((9,)),
            sem((9,)),
            sem((NB - 1,)),
            sem((NB - 1,)),
            sem((NB,)),
            sem((5,)),
            pltpu.SemaphoreType.REGULAR((4,)),
        ],
        compiler_params=pltpu.CompilerParams(
            collective_id=0, has_side_effects=True, vmem_limit_bytes=20 * 1024 * 1024
        ),
        name="gather_project",
    )(x, w, g, pairs)


def scatter_kernel(
    dproj, w, ot, xv,
    att, ng, wg,
    px, zs, zr, ysb, yrb, arecv, dt, dwf, cs, cr, xs, xr, hs, hr, fs, fo, fsib,
    sz, rz, sy, ry, sa, ra, sc, rc, sx, rx, sh, rh, sf, rf,
):
    s, y, z = ring_place()
    p = 1 - y
    up = {"seq": y * NZ + lax.rem(z + 1, NZ)}
    down = {"seq": y * NZ + lax.rem(z + NZ - 1, NZ)}
    across = {"seq": p * NZ + z}
    q = lax.axis_index("clus")
    cx = lax.div(q, NY * CORES)
    ch = lax.rem(lax.div(q, CORES), NY)
    cc = lax.rem(q, CORES)
    sib = {"clus": q + 1 - 2 * cc}

    def xpeer(d):
        return {"clus": lax.rem(cx + d, NX) * (NY * CORES) + ch * CORES + cc}

    def hpeer(d):
        return {"clus": cx * (NY * CORES) + lax.rem(ch + d, NY) * CORES + cc}

    def terms():
        def step(t, _):
            at = pl.ds(pl.multiple_of(t * 256, 256), 256)
            px[:, at] = jnp.dot(dproj[...], w[:, at], preferred_element_type=F32).astype(BF)
            return 0

        lax.fori_loop(0, D // 256, step, 0)
        arecv[s] = ot[s]

    greet(
        [{"seq": lax.rem(s + d, NB)} for d in range(1, NB)]
        + [sib]
        + [xpeer(d) for d in range(1, NX)]
        + [hpeer(d) for d in range(1, NY)],
        terms,
    )

    def block(col, off):
        return col * NZ + lax.rem(z + off + NZ, NZ)

    def part(col, off, first, rows):
        b = block(col, off)
        return px.at[pl.ds(pl.multiple_of(b * BLOCK + first, QUART), rows), :]

    sent = []

    def rcopy(src, dst, ss, rs, dev):
        return pltpu.make_async_remote_copy(
            src_ref=src, dst_ref=dst, send_sem=ss, recv_sem=rs,
            device_id=dev, device_id_type=MESH,
        )

    def span(flow, k):
        if k == 0:
            return pl.ds(QUART if flow % 2 else 0, QUART)
        return pl.ds(0, HALF)

    def zmsg(flow, k):
        at = span(flow, k)
        src = zs.at[flow, k, at]
        if k == 0 and flow >= 2:
            lo = QUART if flow % 2 else 0
            src = part(p if flow >= 4 else y, 4, HALF + lo, QUART)
        return rcopy(
            src, zr.at[flow, k, at], sz.at[flow, k], rz.at[flow, k],
            down if flow % 2 else up,
        )

    def ymsg(idx):
        src = ysb if idx == 8 else part(p, idx, 0, HALF)
        return rcopy(src, yrb.at[idx], sy.at[idx], ry.at[idx], across)

    def go(c):
        c.start()
        sent.append(c)

    def zstep(flow, k):
        col = p if flow >= 4 else y
        base = 0 if flow < 2 else HALF
        off = (4 - k) * (-1 if flow % 2 else 1)
        lo = QUART if flow % 2 else 0
        if k == 0:
            if flow < 2:
                val = part(col, off, lo, QUART)[...].astype(F32)
                val = val + yrb[off % NZ, lo : lo + QUART, :].astype(F32)
                zs[flow, 0, lo : lo + QUART, :] = val.astype(BF)
        else:
            val = part(col, off, base, HALF)[...].astype(F32)
            if flow < 2:
                val = val + yrb[off % NZ].astype(F32)
            zmsg(flow, k - 1).wait_recv()
            if k == 1:
                zs[flow, 1, QUART - lo : HALF - lo, :] = val[QUART - lo : HALF - lo].astype(BF)
                zs[flow, 1, lo : lo + QUART, :] = (
                    val[lo : lo + QUART] + zr[flow, 0, lo : lo + QUART, :].astype(F32)
                ).astype(BF)
            else:
                zs[flow, k] = (val + zr[flow, k - 1].astype(F32)).astype(BF)
        go(zmsg(flow, k))

    def ysend(off):
        go(ymsg(off % NZ))

    for flow in (4, 5):
        zstep(flow, 0)
    ysend(4)
    for flow in (2, 3):
        zstep(flow, 0)
    ysend(3)
    ysend(-3)
    for d in range(1, NB):
        to = lax.rem(s + d, NB)
        go(rcopy(ot.at[to], arecv.at[s], sa.at[d - 1], ra.at[d - 1], {"seq": to}))

    def turn(t, _):
        at = pl.ds(pl.multiple_of(t * BLOCK, BLOCK), BLOCK)
        v = jnp.concatenate([dproj[at, :].astype(F32), jnp.zeros((BLOCK, HD), F32)], axis=1)
        dt[:, at] = v.T[: 3 * HD].astype(BF)
        return 0

    def wstep(t, _):
        at = pl.ds(pl.multiple_of(t * 256, 256), 256)
        dwf[:, at] = jnp.dot(dt[...], xv[:, at], preferred_element_type=F32)
        return 0

    hrow = 3 * HD // CORES
    mine = pl.ds(pl.multiple_of(cc * hrow, QUART), hrow)
    other = pl.ds(pl.multiple_of((1 - cc) * hrow, QUART), hrow)
    wide = D // NX

    def stage0():
        lax.fori_loop(0, NB, turn, 0)
        lax.fori_loop(0, D // 256, wstep, 0)
        cs[...] = dwf[other, :].astype(BF)
        go(rcopy(cs, cr, sc.at[0], rc.at[0], sib))

    def stage1():
        rcopy(cs, cr, sc.at[0], rc.at[0], sib).wait_recv()
        v = dwf[mine, :] + cr[...].astype(F32)
        for t in range(NX):
            xs[t] = v[:, t * wide : (t + 1) * wide].astype(BF)
        xr[cx] = xs[cx]
        for d in range(1, NX):
            go(rcopy(xs.at[lax.rem(cx + d, NX)], xr.at[cx], sx.at[d - 1], rx.at[d - 1], xpeer(d)))

    def stage2():
        for d in range(1, NX):
            frm = lax.rem(cx + NX - d, NX)
            rcopy(xs.at[cx], xr.at[frm], sx.at[d - 1], rx.at[d - 1], xpeer(d)).wait_recv()
        v = xr[0].astype(F32) + xr[1].astype(F32) + xr[2].astype(F32) + xr[3].astype(F32)
        hs[...] = v.astype(BF)
        hr[ch] = v.astype(BF)
        for d in range(1, NY):
            go(rcopy(hs, hr.at[ch], sh.at[d - 1], rh.at[d - 1], hpeer(d)))

    def stage3():
        for d in range(1, NY):
            frm = lax.rem(ch + NY - d, NY)
            rcopy(hs, hr.at[frm], sh.at[d - 1], rh.at[d - 1], hpeer(d)).wait_recv()
        v = hr[0].astype(F32) + hr[1].astype(F32) + hr[2].astype(F32) + hr[3].astype(F32)
        fs[...] = v.astype(BF)
        fo[cx] = v.astype(BF)
        for d in range(1, NX):
            go(rcopy(fs, fo.at[cx], sf.at[d - 1], rf.at[d - 1], xpeer(d)))

    def stage4():
        for d in range(1, NX):
            frm = lax.rem(cx + NX - d, NX)
            rcopy(fs, fo.at[frm], sf.at[d - 1], rf.at[d - 1], xpeer(d)).wait_recv()
        go(rcopy(fo, fsib, sc.at[1], rc.at[1], sib))

    def stage5():
        rcopy(fo, fsib, sc.at[1], rc.at[1], sib).wait_recv()
        for t in range(NX):
            at = pl.ds(t * wide, wide)
            wg[mine, at] = fo[t].astype(F32) * (1.0 / (NX * NY * CORES))
            wg[other, at] = fsib[t].astype(F32) * (1.0 / (NX * NY * CORES))

    def asteps(k):
        if k == 0:
            ymsg(4).wait_recv()
        else:
            ymsg((4 - k) % NZ).wait_recv()
            ymsg((k - 4) % NZ).wait_recv()
        zstep(0, k)
        zstep(1, k)

    def total(flow, col, base):
        val = part(col, 0, base, HALF)[...].astype(F32)
        for f in (flow, flow + 1):
            zmsg(f, 3).wait_recv()
            val = val + zr[f, 3].astype(F32)
        return val

    asteps(0)
    for flow in (4, 5, 2, 3):
        zstep(flow, 1)
    stage0()
    ysend(2)
    ysend(-2)
    asteps(1)
    stage1()
    for flow in (4, 5, 2, 3):
        zstep(flow, 2)
    ysend(1)
    ysend(-1)
    stage2()
    asteps(2)
    for flow in (4, 5, 2, 3):
        zstep(flow, 3)
    ysend(0)
    for d in range(1, NB):
        frm = lax.rem(s + NB - d, NB)
        rcopy(ot.at[s], arecv.at[frm], sa.at[d - 1], ra.at[d - 1], {"seq": frm}).wait_recv()
    for c in range(NB // 2):
        t = jnp.concatenate([arecv[2 * c], arecv[2 * c + 1]], axis=0).astype(F32)
        att[0, :, c * BLOCK : (c + 1) * BLOCK] = t.T.astype(BF)
    stage3()
    asteps(3)
    stage4()
    ysb[...] = total(4, p, HALF).astype(BF)
    go(ymsg(8))
    own_b = total(2, y, HALF)
    ymsg(0).wait_recv()
    ng[0, :HALF, :] = (total(0, y, 0) + yrb[0].astype(F32)).astype(BF)
    stage5()
    ymsg(8).wait_recv()
    ng[0, HALF:, :] = (own_b + yrb[8].astype(F32)).astype(BF)
    for c in sent:
        c.wait_send()


def scatter(dproj, w, ot, xall):
    vm = pl.BlockSpec(memory_space=pltpu.VMEM)
    n = NB * BLOCK
    sem = pltpu.SemaphoreType.DMA
    vmem = pltpu.VMEM
    hrow = 3 * HD // CORES
    wide = D // NX
    return pl.pallas_call(
        scatter_kernel,
        out_shape=(
            jax.ShapeDtypeStruct((1, BLOCK, D), BF),
            jax.ShapeDtypeStruct((1, BLOCK, D), BF),
            jax.ShapeDtypeStruct((3 * HD, D), F32),
        ),
        in_specs=[vm, vm, vm, vm],
        out_specs=(vm, vm, vm),
        scratch_shapes=[
            vmem((n, D), BF),
            vmem((6, 4, HALF, D), BF),
            vmem((6, 4, HALF, D), BF),
            vmem((HALF, D), BF),
            vmem((9, HALF, D), BF),
            vmem((NB, HD, BLOCK), BF),
            vmem((3 * HD, n), BF),
            vmem((3 * HD, D), F32),
            vmem((hrow, D), BF),
            vmem((hrow, D), BF),
            vmem((NX, hrow, wide), BF),
            vmem((NX, hrow, wide), BF),
            vmem((hrow, wide), BF),
            vmem((NY, hrow, wide), BF),
            vmem((hrow, wide), BF),
            vmem((NX, hrow, wide), BF),
            vmem((NX, hrow, wide), BF),
            sem((6, 4)),
            sem((6, 4)),
            sem((9,)),
            sem((9,)),
            sem((NB - 1,)),
            sem((NB - 1,)),
            sem((2,)),
            sem((2,)),
            sem((NX - 1,)),
            sem((NX - 1,)),
            sem((NY - 1,)),
            sem((NY - 1,)),
            sem((NX - 1,)),
            sem((NX - 1,)),
        ],
        compiler_params=pltpu.CompilerParams(
            collective_id=1, has_side_effects=True, vmem_limit_bytes=24 * 1024 * 1024
        ),
        name="scatter_reduce",
    )(dproj, w, ot, xall)


def put_kernel(a, b, c, ao, bo, co, sems):
    copies = [
        pltpu.make_async_copy(src, dst, sems.at[t])
        for t, (src, dst) in enumerate(((c, co), (a, ao), (b, bo)))
    ]
    for copy in copies:
        copy.start()
    for copy in copies:
        copy.wait()


def put(a, b, c):
    vm = pl.BlockSpec(memory_space=pltpu.VMEM)
    hbm = pl.BlockSpec(memory_space=pltpu.HBM)
    return pl.pallas_call(
        put_kernel,
        out_shape=tuple(jax.ShapeDtypeStruct(t.shape, t.dtype) for t in (a, b, c)),
        in_specs=[vm, vm, vm],
        out_specs=(hbm, hbm, hbm),
        scratch_shapes=[pltpu.SemaphoreType.DMA((3,))],
        compiler_params=pltpu.CompilerParams(vmem_limit_bytes=4 * 1024 * 1024),
        name="put",
    )(a, b, c)


def local(node_feats, qkv_weight, block_pairs, grad_out):
    operands = (node_feats, qkv_weight, grad_out, jnp.transpose(block_pairs[0]))
    held = [pltpu.with_memory_space_constraint(t, pltpu.HBM) for t in operands]
    xall, b1, b2, kv, lst = gather(*held)
    ot, dproj = attention(lst, b1, b2, kv)
    return put(*scatter(dproj, qkv_weight, ot, xall.reshape(NB * BLOCK, D)))


def solution(mesh):
    return jax.shard_map(
        local,
        mesh=mesh,
        in_specs=(
            P("clus", "seq", None),
            P("seq", None),
            P("clus", None, None),
            P("clus", "seq", None),
        ),
        out_specs=(P("clus", "seq", None), P("clus", "seq", None), P("seq", None)),
        check_vma=False,
    )
```

```python
import math

import jax
import jax.numpy as jnp
from jax import lax
from jax.experimental import pallas as pl
from jax.experimental.pallas import tpu as pltpu
from jax.sharding import PartitionSpec as P

F32 = jnp.float32
BF = jnp.bfloat16
HD = 64
BLOCK = 128
NB = 16
SIZES = (1, 2, 4, 6, 8, 10, 12, 14, 16)
PAD = -1e30
COUNT = 16
ROWID = 17
SCALE = 0.125 * math.log2(math.e)


def attn_kernel(lst, b1, b2, kv, ot, dproj, s_scr, d_scr, acc):
    acc[...] = jnp.zeros_like(acc)

    def at_block(j):
        return pl.ds(pl.multiple_of(j * BLOCK, BLOCK), BLOCK)

    def at_rows(base, ch):
        return pl.ds(pl.multiple_of(base * BLOCK, BLOCK), ch * BLOCK)

    def fold(v):
        return v.reshape(v.shape[0] // 8, 8, BLOCK)

    def scores(r, base, ch, buf, w1, m):
        n = lst[r, COUNT]
        lhs = jnp.concatenate([kv[at_block(lst[r, base + t]), :] for t in range(ch)], axis=0)
        sd = jnp.dot(lhs, w1, preferred_element_type=F32)
        s = jnp.concatenate(
            [
                sd[t * BLOCK : (t + 1) * BLOCK, :BLOCK]
                + jnp.where(base + t < n, 0.0, PAD).astype(F32)
                for t in range(ch)
            ],
            axis=0,
        )
        s_scr[buf, at_rows(base, ch), :] = s
        d_scr[buf, at_rows(base, ch), :] = sd[:, BLOCK:]
        return jnp.maximum(m, jnp.max(fold(s), axis=0))

    def weigh(base, ch, buf, m, l, d):
        e = jnp.exp2((s_scr[buf, at_rows(base, ch), :] - m) * SCALE)
        s_scr[buf, at_rows(base, ch), :] = e
        l = l + jnp.sum(fold(e), axis=0)
        d = d + jnp.sum(fold(e * d_scr[buf, at_rows(base, ch), :]), axis=0)
        return l, d

    def gradients(r, base, ch, buf, w2, linv, delta, oq):
        p = s_scr[buf, at_rows(base, ch), :] * linv
        ds = p * (d_scr[buf, at_rows(base, ch), :] - delta)
        cat = jnp.concatenate([ds.astype(BF), p.astype(BF)], axis=1)
        cols = [lst[r, base + t] for t in range(ch)]
        rhs = jnp.concatenate([kv[at_block(j), :] for j in cols], axis=0)
        oq = oq + lax.dot_general(cat, rhs, (((0,), (0,)), ((), ())), preferred_element_type=F32)
        g = jnp.dot(cat, w2, preferred_element_type=F32)
        for t in range(ch):
            acc[at_block(cols[t]), :] += g[t * BLOCK : (t + 1) * BLOCK]
        return oq

    def sweep(r, body, state):
        n = lst[r, COUNT]
        which = 0
        for size in SIZES[:-1]:
            which = which + (n > size).astype(jnp.int32)
        arms = [lambda st, ch=ch: body(0, ch, st) for ch in SIZES]
        return lax.switch(which, arms, state)

    def rows_max(m):
        return jnp.max(m, axis=0, keepdims=True)

    def close(l, d):
        linv = 1.0 / jnp.sum(l, axis=0, keepdims=True)
        return linv, jnp.sum(d, axis=0, keepdims=True) * linv

    low = jnp.full((8, BLOCK), PAD, F32)
    zero = jnp.zeros((8, BLOCK), F32)
    w1_0 = b1[lst[0, ROWID]]
    w1_1 = b1[lst[1, ROWID]]
    m0 = rows_max(sweep(0, lambda b, ch, m: scores(0, b, ch, 0, w1_0, m), low))

    def second(b, ch, st):
        m, l, d = st
        m = scores(1, b, ch, 1, w1_1, m)
        l, d = weigh(b, ch, 0, m0, l, d)
        return m, l, d

    m1, l0, d0 = sweep(0, second, (low, zero, zero))

    def row(r, carry):
        linv, delta, m = carry
        m = rows_max(m)
        i = lst[r, ROWID]
        far = jnp.minimum(r + 2, NB - 1)
        w1 = b1[lst[far, ROWID]]
        w2 = b2[i]
        buf, buf1, buf2 = lax.rem(r, 3), lax.rem(r + 1, 3), lax.rem(r + 2, 3)

        def body(b, ch, st):
            oq, l, d, mf = st
            mf = scores(far, b, ch, buf2, w1, mf)
            l, d = weigh(b, ch, buf1, m, l, d)
            oq = gradients(r, b, ch, buf, w2, linv, delta, oq)
            return oq, l, d, mf

        oq, l, d, mf = sweep(r, body, (jnp.zeros((2 * BLOCK, BLOCK), F32), zero, zero, low))
        ot[i] = oq[BLOCK:, :].T[HD:].astype(BF)
        dproj[at_block(i), 0:BLOCK] = (oq[:BLOCK, :] * 0.125).astype(BF)
        linv, delta = close(l, d)
        return linv, delta, mf

    lax.fori_loop(0, NB, row, (*close(l0, d0), m1))

    lane = lax.broadcasted_iota(jnp.int32, (1, BLOCK), 1)
    key_scale = jnp.where(lane < HD, 0.125, 1.0).astype(F32)

    def fin(i, _):
        a = (acc[at_block(i), :] * key_scale).astype(BF)
        q = dproj[at_block(i), 0:BLOCK]
        dproj[at_block(i), :] = jnp.concatenate([q[:, :HD], a], axis=1)
        return 0

    lax.fori_loop(0, NB, fin, 0, unroll=4)


def attention(lst, b1, b2, kv):
    vm = pl.BlockSpec(memory_space=pltpu.VMEM)
    n = NB * BLOCK
    return pl.pallas_call(
        attn_kernel,
        out_shape=(
            jax.ShapeDtypeStruct((NB, HD, BLOCK), BF),
            jax.ShapeDtypeStruct((n, 3 * HD), BF),
        ),
        in_specs=[pl.BlockSpec(memory_space=pltpu.SMEM), vm, vm, vm],
        out_specs=(vm, vm),
        scratch_shapes=[
            pltpu.VMEM((3, n, BLOCK), F32),
            pltpu.VMEM((3, n, BLOCK), F32),
            pltpu.VMEM((n, BLOCK), F32),
        ],
        compiler_params=pltpu.CompilerParams(vmem_limit_bytes=14 * 1024 * 1024),
        name="attention",
    )(lst, b1, b2, kv)

MESH = pl.DeviceIdType.MESH
HD = 64
BLOCK = 128
NB = 16
NZ = 8
D = 1024
HALF = 64
QUART = 32
CORES = 2
NX = 4
NY = 4


def dot_t(a, b):
    return lax.dot_general(a, b, (((1,), (1,)), ((), ())), preferred_element_type=F32)


def ring_place():
    s = lax.axis_index("seq")
    y = lax.div(s, NZ)
    z = lax.rem(s, NZ)
    return s, y, z


def greet(peers, meanwhile=None):
    barrier = pltpu.get_barrier_semaphore()
    for peer in peers:
        pl.semaphore_signal(barrier, inc=1, device_id=peer, device_id_type=MESH)
    if meanwhile is not None:
        meanwhile()
    pl.semaphore_wait(barrier, len(peers))


RA = 80
SPLIT = {0: (0, 48), 1: (48, 32), 2: (80, 16), 3: (96, 32)}


def row_lists(pairs):
    one = jnp.float32(1)
    sub = lax.broadcasted_iota(jnp.int32, (BLOCK, BLOCK), 0)
    lane = lax.broadcasted_iota(jnp.int32, (BLOCK, BLOCK), 1)
    sub_nb, lane_nb = sub[:NB], lane[:NB]
    row_hot = jnp.where(sub == pairs[0:1, :], one, 0.0).astype(BF)
    col_hot = jnp.where(sub == pairs[1:2, :], one, 0.0).astype(BF)
    allowed = dot_t(row_hot[:NB], col_hot)
    n_col = jnp.sum(allowed, axis=1, keepdims=True)
    n_row = dot_t(jnp.ones((NB, BLOCK), BF), row_hot)[0:1]
    before = jnp.where(sub < lane, one, 0.0).astype(BF)
    pos = jnp.dot(allowed.astype(BF), before, preferred_element_type=F32)
    lists = jnp.zeros((NB, BLOCK), F32)
    lane_f = lane_nb.astype(F32)
    for t in range(NB):
        hit = jnp.where(pos == t, allowed, 0.0)
        col = jnp.sum(hit * lane_f, axis=1, keepdims=True)
        lists = jnp.where(lane_nb == t, col, lists)
    lists = jnp.where(lane_nb == NB, n_col, lists)
    lists = jnp.where(lane_nb == NB + 1, sub_nb.astype(F32), lists)
    ahead = jnp.logical_or(n_col > n_row, jnp.logical_and(n_col == n_row, sub_nb < lane_nb))
    rank = jnp.sum(jnp.where(ahead, one, 0.0), axis=0, keepdims=True)
    move = jnp.where(jnp.logical_and(sub_nb.astype(F32) == rank, lane_nb < NB), one, 0.0)
    full = jnp.concatenate([lists, jnp.zeros((BLOCK - NB, BLOCK), F32)], axis=0)
    out = jnp.dot(move.astype(BF), full.astype(BF), preferred_element_type=F32)
    return (out + 0.5).astype(jnp.int32)


def gather_kernel(
    x, w_hbm, g_hbm, pairs_hbm,
    xall, b1, b2, kv, lst, wout,
    w, g, pairs, xg, gsend, grecv, sz, rz, sy, ry, sg, rg, lx, ll, hop,
):
    s, y, z = ring_place()
    p = 1 - y
    up = {"seq": y * NZ + lax.rem(z + 1, NZ)}
    down = {"seq": y * NZ + lax.rem(z + NZ - 1, NZ)}
    across = {"seq": p * NZ + z}
    load = pltpu.make_async_copy(x.at[0], xg.at[s], ll.at[0])
    load_g = pltpu.make_async_copy(g_hbm.at[0], g, ll.at[1])
    load_w = pltpu.make_async_copy(w_hbm.at[pl.ds(HD, BLOCK)], w.at[pl.ds(0, BLOCK)], ll.at[2])
    load_q = pltpu.make_async_copy(w_hbm.at[pl.ds(0, HD)], w.at[pl.ds(BLOCK, HD)], ll.at[4])
    load_p = pltpu.make_async_copy(pairs_hbm, pairs, ll.at[3])
    pass_w = pltpu.make_async_copy(w_hbm, wout, ll.at[5])
    load.start()
    load_g.start()
    load_w.start()
    load_q.start()
    load_p.start()
    pass_w.start()
    near = [up, down, across]
    greet(near)

    def relay(r):
        for peer in near:
            pl.semaphore_signal(hop.at[r], inc=1, device_id=peer, device_id_type=MESH)
        pl.semaphore_wait(hop.at[r], len(near))

    load.wait()

    def block(col, off):
        return col * NZ + lax.rem(z + off + NZ, NZ)

    def zmsg(flow, k, off, do_start):
        col = p if flow >= 4 else y
        first, rows = (0, RA) if flow < 2 else (RA, BLOCK - RA)
        if k == 3:
            first, rows = SPLIT[flow - 2 if flow >= 4 else flow]
        ref = xg.at[block(col, off), pl.ds(first, rows)]
        c = pltpu.make_async_remote_copy(
            src_ref=ref,
            dst_ref=ref,
            send_sem=sz.at[flow, k],
            recv_sem=rz.at[flow, k],
            device_id=down if flow % 2 else up,
            device_id_type=MESH,
        )
        if do_start:
            c.start()
        return c

    def ymsg(idx, col, do_start):
        off = 0 if idx == 8 else idx
        ref = xg.at[block(col, off), pl.ds(RA, BLOCK - RA) if idx == 8 else pl.ds(0, RA)]
        c = pltpu.make_async_remote_copy(
            src_ref=ref,
            dst_ref=ref,
            send_sem=sy.at[idx],
            recv_sem=ry.at[idx],
            device_id=across,
            device_id_type=MESH,
        )
        if do_start:
            c.start()
        return c

    sent = []
    outs = []
    sent.append(ymsg(8, y, True))
    for flow in (0, 1, 2, 3):
        sent.append(zmsg(flow, 0, 0, True))
    sent.append(ymsg(0, y, True))

    def compute(b, n):
        xb = xg[b]
        at = pl.ds(pl.multiple_of(b * BLOCK, BLOCK), BLOCK)
        proj = dot_t(xb, w[...])
        q = jnp.concatenate([proj[:, BLOCK:], jnp.zeros((BLOCK, HD), F32)], axis=1)
        kv[at, :] = proj[:, :BLOCK].astype(BF)
        b1[b, :HD, :] = jnp.concatenate([q.T[:HD], jnp.zeros((HD, BLOCK), F32)], axis=1).astype(BF)
        b2[b, :BLOCK, :] = q.astype(BF)
        c = pltpu.make_async_copy(xg.at[b], xall.at[b], lx.at[n])
        c.start()
        outs.append(c)

    relay(0)
    load_g.wait()
    for c in range(NB // 2):
        t = g[:, c * BLOCK : (c + 1) * BLOCK].astype(F32).T.astype(BF)
        gsend[2 * c] = t[:HD]
        gsend[2 * c + 1] = t[HD:]

    def gmsg(d):
        to = lax.rem(s + d, NB)
        return pltpu.make_async_remote_copy(
            src_ref=gsend.at[to],
            dst_ref=grecv.at[s],
            send_sem=sg.at[d - 1],
            recv_sem=rg.at[d - 1],
            device_id={"seq": to},
            device_id_type=MESH,
        )

    relay(1)
    load_w.wait()
    load_q.wait()
    compute(s, 0)
    relay(2)
    ymsg(8, p, False).wait_recv()
    for flow in (4, 5):
        sent.append(zmsg(flow, 0, 0, True))
    relay(3)
    for d in range(1, NB):
        c = gmsg(d)
        c.start()
        sent.append(c)
    grecv[s] = gsend[s]
    load_p.wait()
    pass_w.wait()
    lst[...] = row_lists(pairs[...])

    def place(t, _):
        gt = grecv[t].astype(F32)
        zero = jnp.zeros((HD, BLOCK), F32)
        b1[t, HD:, :] = jnp.concatenate([zero, gt], axis=1).astype(BF)
        b2[t, BLOCK:, :] = jnp.concatenate([zero, gt], axis=0).T.astype(BF)
        return 0

    def place_all():
        for d in range(1, NB):
            frm = lax.rem(s + NB - d, NB)
            pltpu.make_async_remote_copy(
                src_ref=gsend.at[s],
                dst_ref=grecv.at[frm],
                send_sem=sg.at[d - 1],
                recv_sem=rg.at[d - 1],
                device_id={"seq": frm},
                device_id_type=MESH,
            ).wait_recv()
        lax.fori_loop(0, NB, place, 0)

    n = 1
    for k in range(4):
        for flow in (0, 1, 2, 3, 4, 5):
            off = (k + 1) if flow % 2 else -(k + 1)
            zmsg(flow, k, off, False).wait_recv()
            if k < 3:
                sent.append(zmsg(flow, k + 1, off, True))
            if flow < 2 and k < 3:
                sent.append(ymsg(off % NZ, y, True))
            if flow == 1 and k == 3:
                sent.append(ymsg(4, y, True))
        for off in [-(k + 1), k + 1][: 2 if k < 3 else 1]:
            compute(block(y, off), n)
            n += 1
        for off in [-k, k][: 2 if k > 0 else 1]:
            ymsg(off % NZ, p, False).wait_recv()
            compute(block(p, off), n)
            n += 1
        if k == 2:
            place_all()
    for c in outs:
        c.wait()
    outs.clear()
    ymsg(4, p, False).wait_recv()
    compute(block(p, 4), n)
    for c in sent:
        c.wait_send()
    for c in outs:
        c.wait()


def gather(x, w, g, pairs):
    vm = pl.BlockSpec(memory_space=pltpu.VMEM)
    anyw = pl.BlockSpec(memory_space=pl.ANY)
    hbm = pl.BlockSpec(memory_space=pltpu.HBM)
    n = NB * BLOCK
    sem = pltpu.SemaphoreType.DMA
    return pl.pallas_call(
        gather_kernel,
        out_shape=(
            jax.ShapeDtypeStruct((NB, BLOCK, D), BF),
            jax.ShapeDtypeStruct((NB, BLOCK, 2 * BLOCK), BF),
            jax.ShapeDtypeStruct((NB, 2 * BLOCK, BLOCK), BF),
            jax.ShapeDtypeStruct((n, BLOCK), BF),
            jax.ShapeDtypeStruct((NB, BLOCK), jnp.int32),
            jax.ShapeDtypeStruct((3 * HD, D), BF),
        ),
        in_specs=[hbm, hbm, hbm, hbm],
        out_specs=(anyw, vm, vm, vm, vm, vm),
        scratch_shapes=[
            pltpu.VMEM((3 * HD, D), BF),
            pltpu.VMEM((BLOCK, D), BF),
            pltpu.VMEM((2, BLOCK), jnp.int32),
            pltpu.VMEM((NB, BLOCK, D), BF),
            pltpu.VMEM((NB, HD, BLOCK), BF),
            pltpu.VMEM((NB, HD, BLOCK), BF),
            sem((6, 4)),
            sem((6, 4)),
            sem((9,)),
            sem((9,)),
            sem((NB - 1,)),
            sem((NB - 1,)),
            sem((NB,)),
            sem((6,)),
            pltpu.SemaphoreType.REGULAR((4,)),
        ],
        compiler_params=pltpu.CompilerParams(
            collective_id=0, has_side_effects=True, vmem_limit_bytes=20 * 1024 * 1024
        ),
        name="gather_project",
    )(x, w, g, pairs)


def scatter_kernel(
    dproj, w, ot, xv,
    att, ng, wg,
    px, zs, zr, ysb, yrb, arecv, dt, dwf, cs, cr, xs, xr, hs, hr, fs, fo, fsib,
    sz, rz, sy, ry, sa, ra, sc, rc, sx, rx, sh, rh, sf, rf,
):
    s, y, z = ring_place()
    p = 1 - y
    up = {"seq": y * NZ + lax.rem(z + 1, NZ)}
    down = {"seq": y * NZ + lax.rem(z + NZ - 1, NZ)}
    across = {"seq": p * NZ + z}
    q = lax.axis_index("clus")
    cx = lax.div(q, NY * CORES)
    ch = lax.rem(lax.div(q, CORES), NY)
    cc = lax.rem(q, CORES)
    sib = {"clus": q + 1 - 2 * cc}

    def xpeer(d):
        return {"clus": lax.rem(cx + d, NX) * (NY * CORES) + ch * CORES + cc}

    def hplace(h):
        return {"clus": cx * (NY * CORES) + h * CORES + cc}

    odd = lax.rem(ch, 2)
    hpair = [hplace(ch + 1 - 2 * odd), hplace(lax.rem(ch + NY - 1 + 2 * odd, NY))]

    def turn(t, _):
        at = pl.ds(pl.multiple_of(t * BLOCK, BLOCK), BLOCK)
        v = jnp.concatenate([dproj[at, :].astype(F32), jnp.zeros((BLOCK, HD), F32)], axis=1)
        dt[:, at] = v.T[: 3 * HD].astype(BF)
        return 0

    def terms():
        def step(t, _):
            at = pl.ds(pl.multiple_of(t * 256, 256), 256)
            px[:, at] = jnp.dot(dproj[...], w[:, at], preferred_element_type=F32).astype(BF)
            return 0

        lax.fori_loop(0, D // 256, step, 0)
        arecv[s] = ot[s]
        lax.fori_loop(0, NB, turn, 0)

    greet(
        [{"seq": lax.rem(s + d, NB)} for d in range(1, NB)]
        + [sib]
        + [xpeer(d) for d in range(1, NX)]
        + hpair,
        terms,
    )

    def block(col, off):
        return col * NZ + lax.rem(z + off + NZ, NZ)

    def part(col, off, first, rows):
        b = block(col, off)
        return px.at[pl.ds(pl.multiple_of(b * BLOCK + first, QUART), rows), :]

    sent = []

    def rcopy(src, dst, ss, rs, dev):
        return pltpu.make_async_remote_copy(
            src_ref=src, dst_ref=dst, send_sem=ss, recv_sem=rs,
            device_id=dev, device_id_type=MESH,
        )

    def span(flow, k):
        if k == 0:
            return pl.ds(QUART if flow % 2 else 0, QUART)
        return pl.ds(0, HALF)

    def zmsg(flow, k):
        at = span(flow, k)
        src = zs.at[flow, k, at]
        if k == 0 and flow >= 2:
            lo = QUART if flow % 2 else 0
            src = part(p if flow >= 4 else y, 4, HALF + lo, QUART)
        return rcopy(
            src, zr.at[flow, k, at], sz.at[flow, k], rz.at[flow, k],
            down if flow % 2 else up,
        )

    def ymsg(idx):
        src = ysb if idx == 8 else part(p, idx, 0, HALF)
        return rcopy(src, yrb.at[idx], sy.at[idx], ry.at[idx], across)

    def go(c):
        c.start()
        sent.append(c)

    def zstep(flow, k):
        col = p if flow >= 4 else y
        base = 0 if flow < 2 else HALF
        off = (4 - k) * (-1 if flow % 2 else 1)
        lo = QUART if flow % 2 else 0
        if k == 0:
            if flow < 2:
                val = part(col, off, lo, QUART)[...].astype(F32)
                val = val + yrb[off % NZ, lo : lo + QUART, :].astype(F32)
                zs[flow, 0, lo : lo + QUART, :] = val.astype(BF)
        else:
            val = part(col, off, base, HALF)[...].astype(F32)
            if flow < 2:
                val = val + yrb[off % NZ].astype(F32)
            zmsg(flow, k - 1).wait_recv()
            if k == 1:
                zs[flow, 1, QUART - lo : HALF - lo, :] = val[QUART - lo : HALF - lo].astype(BF)
                zs[flow, 1, lo : lo + QUART, :] = (
                    val[lo : lo + QUART] + zr[flow, 0, lo : lo + QUART, :].astype(F32)
                ).astype(BF)
            else:
                zs[flow, k] = (val + zr[flow, k - 1].astype(F32)).astype(BF)
        go(zmsg(flow, k))

    def ysend(off):
        go(ymsg(off % NZ))

    for flow in (4, 5):
        zstep(flow, 0)
    ysend(4)
    for flow in (2, 3):
        zstep(flow, 0)
    ysend(3)
    ysend(-3)
    for d in range(1, NB):
        to = lax.rem(s + d, NB)
        go(rcopy(ot.at[to], arecv.at[s], sa.at[d - 1], ra.at[d - 1], {"seq": to}))

    def wstep(t, _):
        at = pl.ds(pl.multiple_of(t * 256, 256), 256)
        dwf[:, at] = jnp.dot(dt[...], xv[:, at], preferred_element_type=F32)
        return 0

    hrow = 3 * HD // CORES
    mine = pl.ds(pl.multiple_of(cc * hrow, QUART), hrow)
    other = pl.ds(pl.multiple_of((1 - cc) * hrow, QUART), hrow)
    wide = D // NX

    def stage0():
        lax.fori_loop(0, D // 256, wstep, 0)
        cs[...] = dwf[other, :].astype(BF)
        go(rcopy(cs, cr, sc.at[0], rc.at[0], sib))

    def stage1():
        rcopy(cs, cr, sc.at[0], rc.at[0], sib).wait_recv()
        v = dwf[mine, :] + cr[...].astype(F32)
        for t in range(NX):
            xs[t] = v[:, t * wide : (t + 1) * wide].astype(BF)
        xr[cx] = xs[cx]
        for d in range(1, NX):
            go(rcopy(xs.at[lax.rem(cx + d, NX)], xr.at[cx], sx.at[d - 1], rx.at[d - 1], xpeer(d)))

    def stage2():
        for d in range(1, NX):
            frm = lax.rem(cx + NX - d, NX)
            rcopy(xs.at[cx], xr.at[frm], sx.at[d - 1], rx.at[d - 1], xpeer(d)).wait_recv()
        v = xr[0].astype(F32) + xr[1].astype(F32) + xr[2].astype(F32) + xr[3].astype(F32)
        hs[0] = v.astype(BF)
        go(hmsg(0))

    def hmsg(t):
        return rcopy(hs.at[t], hr.at[t], sh.at[t], rh.at[t], hpair[t])

    def stage3a():
        hmsg(0).wait_recv()
        hs[1] = (hs[0].astype(F32) + hr[0].astype(F32)).astype(BF)
        go(hmsg(1))

    def stage3():
        hmsg(1).wait_recv()
        v = hs[1].astype(F32) + hr[1].astype(F32)
        fs[...] = v.astype(BF)
        fo[cx] = v.astype(BF)
        for d in range(1, NX):
            go(rcopy(fs, fo.at[cx], sf.at[d - 1], rf.at[d - 1], xpeer(d)))

    def stage4():
        for d in range(1, NX):
            frm = lax.rem(cx + NX - d, NX)
            rcopy(fs, fo.at[frm], sf.at[d - 1], rf.at[d - 1], xpeer(d)).wait_recv()
        go(rcopy(fo, fsib, sc.at[1], rc.at[1], sib))

    def stage5():
        rcopy(fo, fsib, sc.at[1], rc.at[1], sib).wait_recv()
        for t in range(NX):
            at = pl.ds(t * wide, wide)
            wg[mine, at] = fo[t].astype(F32) * (1.0 / (NX * NY * CORES))
            wg[other, at] = fsib[t].astype(F32) * (1.0 / (NX * NY * CORES))

    def asteps(k):
        if k == 0:
            ymsg(4).wait_recv()
        else:
            ymsg((4 - k) % NZ).wait_recv()
            ymsg((k - 4) % NZ).wait_recv()
        zstep(0, k)
        zstep(1, k)

    def total(flow, col, base):
        val = part(col, 0, base, HALF)[...].astype(F32)
        for f in (flow, flow + 1):
            zmsg(f, 3).wait_recv()
            val = val + zr[f, 3].astype(F32)
        return val

    asteps(0)
    for flow in (4, 5, 2, 3):
        zstep(flow, 1)
    stage0()
    ysend(2)
    ysend(-2)
    asteps(1)
    stage1()
    for flow in (4, 5, 2, 3):
        zstep(flow, 2)
    ysend(1)
    ysend(-1)
    stage2()
    asteps(2)
    stage3a()
    for flow in (4, 5, 2, 3):
        zstep(flow, 3)
    ysend(0)
    for d in range(1, NB):
        frm = lax.rem(s + NB - d, NB)
        rcopy(ot.at[s], arecv.at[frm], sa.at[d - 1], ra.at[d - 1], {"seq": frm}).wait_recv()
    for c in range(NB // 2):
        t = jnp.concatenate([arecv[2 * c], arecv[2 * c + 1]], axis=0).astype(F32)
        att[0, :, c * BLOCK : (c + 1) * BLOCK] = t.T.astype(BF)
    stage3()
    asteps(3)
    stage4()
    ysb[...] = total(4, p, HALF).astype(BF)
    go(ymsg(8))
    own_b = total(2, y, HALF)
    ymsg(0).wait_recv()
    ng[0, :HALF, :] = (total(0, y, 0) + yrb[0].astype(F32)).astype(BF)
    stage5()
    ymsg(8).wait_recv()
    ng[0, HALF:, :] = (own_b + yrb[8].astype(F32)).astype(BF)
    for c in sent:
        c.wait_send()


def scatter(dproj, w, ot, xall):
    vm = pl.BlockSpec(memory_space=pltpu.VMEM)
    n = NB * BLOCK
    sem = pltpu.SemaphoreType.DMA
    vmem = pltpu.VMEM
    hrow = 3 * HD // CORES
    wide = D // NX
    return pl.pallas_call(
        scatter_kernel,
        out_shape=(
            jax.ShapeDtypeStruct((1, BLOCK, D), BF),
            jax.ShapeDtypeStruct((1, BLOCK, D), BF),
            jax.ShapeDtypeStruct((3 * HD, D), F32),
        ),
        in_specs=[vm, vm, vm, vm],
        out_specs=(vm, vm, vm),
        scratch_shapes=[
            vmem((n, D), BF),
            vmem((6, 4, HALF, D), BF),
            vmem((6, 4, HALF, D), BF),
            vmem((HALF, D), BF),
            vmem((9, HALF, D), BF),
            vmem((NB, HD, BLOCK), BF),
            vmem((3 * HD, n), BF),
            vmem((3 * HD, D), F32),
            vmem((hrow, D), BF),
            vmem((hrow, D), BF),
            vmem((NX, hrow, wide), BF),
            vmem((NX, hrow, wide), BF),
            vmem((2, hrow, wide), BF),
            vmem((2, hrow, wide), BF),
            vmem((hrow, wide), BF),
            vmem((NX, hrow, wide), BF),
            vmem((NX, hrow, wide), BF),
            sem((6, 4)),
            sem((6, 4)),
            sem((9,)),
            sem((9,)),
            sem((NB - 1,)),
            sem((NB - 1,)),
            sem((2,)),
            sem((2,)),
            sem((NX - 1,)),
            sem((NX - 1,)),
            sem((2,)),
            sem((2,)),
            sem((NX - 1,)),
            sem((NX - 1,)),
        ],
        compiler_params=pltpu.CompilerParams(
            collective_id=1, has_side_effects=True, vmem_limit_bytes=24 * 1024 * 1024
        ),
        name="scatter_reduce",
    )(dproj, w, ot, xall)


def put_kernel(a, b, c, ao, bo, co, sems):
    copies = [
        pltpu.make_async_copy(src, dst, sems.at[t])
        for t, (src, dst) in enumerate(((c, co), (a, ao), (b, bo)))
    ]
    for copy in copies:
        copy.start()
    for copy in copies:
        copy.wait()


def put(a, b, c):
    vm = pl.BlockSpec(memory_space=pltpu.VMEM)
    hbm = pl.BlockSpec(memory_space=pltpu.HBM)
    return pl.pallas_call(
        put_kernel,
        out_shape=tuple(jax.ShapeDtypeStruct(t.shape, t.dtype) for t in (a, b, c)),
        in_specs=[vm, vm, vm],
        out_specs=(hbm, hbm, hbm),
        scratch_shapes=[pltpu.SemaphoreType.DMA((3,))],
        compiler_params=pltpu.CompilerParams(vmem_limit_bytes=4 * 1024 * 1024),
        name="put",
    )(a, b, c)


def local(node_feats, qkv_weight, block_pairs, grad_out):
    operands = (node_feats, qkv_weight, grad_out, jnp.transpose(block_pairs[0]))
    held = [pltpu.with_memory_space_constraint(t, pltpu.HBM) for t in operands]
    xall, b1, b2, kv, lst, w = gather(*held)
    ot, dproj = attention(lst, b1, b2, kv)
    return put(*scatter(dproj, w, ot, xall.reshape(NB * BLOCK, D)))


def solution(mesh):
    return jax.shard_map(
        local,
        mesh=mesh,
        in_specs=(
            P("clus", "seq", None),
            P("seq", None),
            P("clus", None, None),
            P("clus", "seq", None),
        ),
        out_specs=(P("clus", "seq", None), P("clus", "seq", None), P("seq", None)),
        check_vma=False,
    )
```

```python
import math

import jax
import jax.numpy as jnp
from jax import lax
from jax.experimental import pallas as pl
from jax.experimental.pallas import tpu as pltpu
from jax.sharding import PartitionSpec as P

F32 = jnp.float32
BF = jnp.bfloat16
HD = 64
BLOCK = 128
NB = 16
SIZES = (1, 2, 4, 6, 8, 10, 12, 14, 16)
PAD = -1e30
COUNT = 16
ROWID = 17
SCALE = 0.125 * math.log2(math.e)


def attn_kernel(lst, b1, b2, kv, ot, dproj, s_scr, d_scr, acc):
    acc[...] = jnp.zeros_like(acc)

    def at_block(j):
        return pl.ds(pl.multiple_of(j * BLOCK, BLOCK), BLOCK)

    def at_rows(base, ch):
        return pl.ds(pl.multiple_of(base * BLOCK, BLOCK), ch * BLOCK)

    def fold(v):
        return v.reshape(v.shape[0] // 8, 8, BLOCK)

    def scores(r, base, ch, buf, w1, m):
        n = lst[r, COUNT]
        lhs = jnp.concatenate([kv[at_block(lst[r, base + t]), :] for t in range(ch)], axis=0)
        sd = jnp.dot(lhs, w1, preferred_element_type=F32)
        s = jnp.concatenate(
            [
                sd[t * BLOCK : (t + 1) * BLOCK, :BLOCK]
                + jnp.where(base + t < n, 0.0, PAD).astype(F32)
                for t in range(ch)
            ],
            axis=0,
        )
        s_scr[buf, at_rows(base, ch), :] = s
        d_scr[buf, at_rows(base, ch), :] = sd[:, BLOCK:]
        return jnp.maximum(m, jnp.max(fold(s), axis=0))

    def weigh(base, ch, buf, m, l, d):
        e = jnp.exp2((s_scr[buf, at_rows(base, ch), :] - m) * SCALE)
        s_scr[buf, at_rows(base, ch), :] = e
        l = l + jnp.sum(fold(e), axis=0)
        d = d + jnp.sum(fold(e * d_scr[buf, at_rows(base, ch), :]), axis=0)
        return l, d

    def gradients(r, base, ch, buf, w2, linv, delta, oq):
        p = s_scr[buf, at_rows(base, ch), :] * linv
        ds = p * (d_scr[buf, at_rows(base, ch), :] - delta)
        cat = jnp.concatenate([ds.astype(BF), p.astype(BF)], axis=1)
        cols = [lst[r, base + t] for t in range(ch)]
        rhs = jnp.concatenate([kv[at_block(j), :] for j in cols], axis=0)
        oq = oq + lax.dot_general(cat, rhs, (((0,), (0,)), ((), ())), preferred_element_type=F32)
        g = jnp.dot(cat, w2, preferred_element_type=F32)
        for t in range(ch):
            acc[at_block(cols[t]), :] += g[t * BLOCK : (t + 1) * BLOCK]
        return oq

    def sweep(r, body, state):
        n = lst[r, COUNT]
        which = 0
        for size in SIZES[:-1]:
            which = which + (n > size).astype(jnp.int32)
        arms = [lambda st, ch=ch: body(0, ch, st) for ch in SIZES]
        return lax.switch(which, arms, state)

    def rows_max(m):
        return jnp.max(m, axis=0, keepdims=True)

    def close(l, d):
        linv = 1.0 / jnp.sum(l, axis=0, keepdims=True)
        return linv, jnp.sum(d, axis=0, keepdims=True) * linv

    low = jnp.full((8, BLOCK), PAD, F32)
    zero = jnp.zeros((8, BLOCK), F32)
    w1_0 = b1[lst[0, ROWID]]
    w1_1 = b1[lst[1, ROWID]]
    m0 = rows_max(sweep(0, lambda b, ch, m: scores(0, b, ch, 0, w1_0, m), low))

    def second(b, ch, st):
        m, l, d = st
        m = scores(1, b, ch, 1, w1_1, m)
        l, d = weigh(b, ch, 0, m0, l, d)
        return m, l, d

    m1, l0, d0 = sweep(0, second, (low, zero, zero))

    def row(r, carry):
        linv, delta, m = carry
        m = rows_max(m)
        i = lst[r, ROWID]
        far = jnp.minimum(r + 2, NB - 1)
        w1 = b1[lst[far, ROWID]]
        w2 = b2[i]
        buf, buf1, buf2 = lax.rem(r, 3), lax.rem(r + 1, 3), lax.rem(r + 2, 3)

        def body(b, ch, st):
            oq, l, d, mf = st
            mf = scores(far, b, ch, buf2, w1, mf)
            l, d = weigh(b, ch, buf1, m, l, d)
            oq = gradients(r, b, ch, buf, w2, linv, delta, oq)
            return oq, l, d, mf

        oq, l, d, mf = sweep(r, body, (jnp.zeros((2 * BLOCK, BLOCK), F32), zero, zero, low))
        ot[i] = oq[BLOCK:, :].T[HD:].astype(BF)
        dproj[at_block(i), 0:BLOCK] = (oq[:BLOCK, :] * 0.125).astype(BF)
        linv, delta = close(l, d)
        return linv, delta, mf

    lax.fori_loop(0, NB, row, (*close(l0, d0), m1))

    lane = lax.broadcasted_iota(jnp.int32, (1, BLOCK), 1)
    key_scale = jnp.where(lane < HD, 0.125, 1.0).astype(F32)

    def fin(i, _):
        a = (acc[at_block(i), :] * key_scale).astype(BF)
        q = dproj[at_block(i), 0:BLOCK]
        dproj[at_block(i), :] = jnp.concatenate([q[:, :HD], a], axis=1)
        return 0

    lax.fori_loop(0, NB, fin, 0, unroll=4)


def attention(lst, b1, b2, kv):
    vm = pl.BlockSpec(memory_space=pltpu.VMEM)
    n = NB * BLOCK
    return pl.pallas_call(
        attn_kernel,
        out_shape=(
            jax.ShapeDtypeStruct((NB, HD, BLOCK), BF),
            jax.ShapeDtypeStruct((n, 3 * HD), BF),
        ),
        in_specs=[pl.BlockSpec(memory_space=pltpu.SMEM), vm, vm, vm],
        out_specs=(vm, vm),
        scratch_shapes=[
            pltpu.VMEM((3, n, BLOCK), F32),
            pltpu.VMEM((3, n, BLOCK), F32),
            pltpu.VMEM((n, BLOCK), F32),
        ],
        compiler_params=pltpu.CompilerParams(vmem_limit_bytes=14 * 1024 * 1024),
        name="attention",
    )(lst, b1, b2, kv)

MESH = pl.DeviceIdType.MESH
HD = 64
BLOCK = 128
NB = 16
NZ = 8
D = 1024
HALF = 64
QUART = 32
CORES = 2
NX = 4
NY = 4


def dot_t(a, b):
    return lax.dot_general(a, b, (((1,), (1,)), ((), ())), preferred_element_type=F32)


def ring_place():
    s = lax.axis_index("seq")
    y = lax.div(s, NZ)
    z = lax.rem(s, NZ)
    return s, y, z


def greet(peers, meanwhile=None):
    barrier = pltpu.get_barrier_semaphore()
    for peer in peers:
        pl.semaphore_signal(barrier, inc=1, device_id=peer, device_id_type=MESH)
    if meanwhile is not None:
        meanwhile()
    pl.semaphore_wait(barrier, len(peers))


RA = 80
SPLIT = {0: (0, 48), 1: (48, 32), 2: (80, 16), 3: (96, 32)}


def row_lists(pairs):
    one = jnp.float32(1)
    sub = lax.broadcasted_iota(jnp.int32, (BLOCK, BLOCK), 0)
    lane = lax.broadcasted_iota(jnp.int32, (BLOCK, BLOCK), 1)
    sub_nb, lane_nb = sub[:NB], lane[:NB]
    row_hot = jnp.where(sub == pairs[0:1, :], one, 0.0).astype(BF)
    col_hot = jnp.where(sub == pairs[1:2, :], one, 0.0).astype(BF)
    allowed = dot_t(row_hot[:NB], col_hot)
    n_col = jnp.sum(allowed, axis=1, keepdims=True)
    n_row = dot_t(jnp.ones((NB, BLOCK), BF), row_hot)[0:1]
    before = jnp.where(sub < lane, one, 0.0).astype(BF)
    pos = jnp.dot(allowed.astype(BF), before, preferred_element_type=F32)
    lists = jnp.zeros((NB, BLOCK), F32)
    lane_f = lane_nb.astype(F32)
    for t in range(NB):
        hit = jnp.where(pos == t, allowed, 0.0)
        col = jnp.sum(hit * lane_f, axis=1, keepdims=True)
        lists = jnp.where(lane_nb == t, col, lists)
    lists = jnp.where(lane_nb == NB, n_col, lists)
    lists = jnp.where(lane_nb == NB + 1, sub_nb.astype(F32), lists)
    ahead = jnp.logical_or(n_col > n_row, jnp.logical_and(n_col == n_row, sub_nb < lane_nb))
    rank = jnp.sum(jnp.where(ahead, one, 0.0), axis=0, keepdims=True)
    move = jnp.where(jnp.logical_and(sub_nb.astype(F32) == rank, lane_nb < NB), one, 0.0)
    full = jnp.concatenate([lists, jnp.zeros((BLOCK - NB, BLOCK), F32)], axis=0)
    out = jnp.dot(move.astype(BF), full.astype(BF), preferred_element_type=F32)
    return (out + 0.5).astype(jnp.int32)


def gather_kernel(
    x, w_hbm, g_hbm, pairs_hbm,
    xall, b1, b2, kv, lst, wout,
    w, g, pairs, xg, gsend, grecv, sz, rz, sy, ry, sg, rg, lx, ll, hop,
):
    s, y, z = ring_place()
    p = 1 - y
    up = {"seq": y * NZ + lax.rem(z + 1, NZ)}
    down = {"seq": y * NZ + lax.rem(z + NZ - 1, NZ)}
    across = {"seq": p * NZ + z}
    load = pltpu.make_async_copy(x.at[0], xg.at[s], ll.at[0])
    load_g = pltpu.make_async_copy(g_hbm.at[0], g, ll.at[1])
    load_w = pltpu.make_async_copy(w_hbm.at[pl.ds(HD, BLOCK)], w.at[pl.ds(0, BLOCK)], ll.at[2])
    load_q = pltpu.make_async_copy(w_hbm.at[pl.ds(0, HD)], w.at[pl.ds(BLOCK, HD)], ll.at[4])
    load_p = pltpu.make_async_copy(pairs_hbm, pairs, ll.at[3])
    pass_w = pltpu.make_async_copy(w_hbm, wout, ll.at[5])
    load.start()
    load_g.start()
    load_w.start()
    load_q.start()
    load_p.start()
    pass_w.start()
    near = [up, down, across]
    greet(near)

    def relay(r):
        for peer in near:
            pl.semaphore_signal(hop.at[r], inc=1, device_id=peer, device_id_type=MESH)
        pl.semaphore_wait(hop.at[r], len(near))

    load.wait()

    def block(col, off):
        return col * NZ + lax.rem(z + off + NZ, NZ)

    def zmsg(flow, k, off, do_start):
        col = p if flow >= 4 else y
        first, rows = (0, RA) if flow < 2 else (RA, BLOCK - RA)
        if k == 3:
            first, rows = SPLIT[flow - 2 if flow >= 4 else flow]
        ref = xg.at[block(col, off), pl.ds(first, rows)]
        c = pltpu.make_async_remote_copy(
            src_ref=ref,
            dst_ref=ref,
            send_sem=sz.at[flow, k],
            recv_sem=rz.at[flow, k],
            device_id=down if flow % 2 else up,
            device_id_type=MESH,
        )
        if do_start:
            c.start()
        return c

    def ymsg(idx, col, do_start):
        off = 0 if idx == 8 else idx
        ref = xg.at[block(col, off), pl.ds(RA, BLOCK - RA) if idx == 8 else pl.ds(0, RA)]
        c = pltpu.make_async_remote_copy(
            src_ref=ref,
            dst_ref=ref,
            send_sem=sy.at[idx],
            recv_sem=ry.at[idx],
            device_id=across,
            device_id_type=MESH,
        )
        if do_start:
            c.start()
        return c

    sent = []
    outs = []
    sent.append(ymsg(8, y, True))
    for flow in (0, 1, 2, 3):
        sent.append(zmsg(flow, 0, 0, True))
    sent.append(ymsg(0, y, True))

    def compute(b, n):
        xb = xg[b]
        at = pl.ds(pl.multiple_of(b * BLOCK, BLOCK), BLOCK)
        proj = dot_t(xb, w[...])
        q = jnp.concatenate([proj[:, BLOCK:], jnp.zeros((BLOCK, HD), F32)], axis=1)
        kv[at, :] = proj[:, :BLOCK].astype(BF)
        b1[b, :HD, :] = jnp.concatenate([q.T[:HD], jnp.zeros((HD, BLOCK), F32)], axis=1).astype(BF)
        b2[b, :BLOCK, :] = q.astype(BF)
        c = pltpu.make_async_copy(xg.at[b], xall.at[b], lx.at[n])
        c.start()
        outs.append(c)

    relay(0)
    load_g.wait()
    for c in range(NB // 2):
        t = g[:, c * BLOCK : (c + 1) * BLOCK].astype(F32).T.astype(BF)
        gsend[2 * c] = t[:HD]
        gsend[2 * c + 1] = t[HD:]

    def gmsg(d):
        to = lax.rem(s + d, NB)
        return pltpu.make_async_remote_copy(
            src_ref=gsend.at[to],
            dst_ref=grecv.at[s],
            send_sem=sg.at[d - 1],
            recv_sem=rg.at[d - 1],
            device_id={"seq": to},
            device_id_type=MESH,
        )

    relay(1)
    load_w.wait()
    load_q.wait()
    compute(s, 0)
    relay(2)
    ymsg(8, p, False).wait_recv()
    for flow in (4, 5):
        sent.append(zmsg(flow, 0, 0, True))
    relay(3)
    for d in range(1, NB):
        c = gmsg(d)
        c.start()
        sent.append(c)
    grecv[s] = gsend[s]
    load_p.wait()
    pass_w.wait()
    lst[...] = row_lists(pairs[...])

    def place(t, _):
        gt = grecv[t].astype(F32)
        zero = jnp.zeros((HD, BLOCK), F32)
        b1[t, HD:, :] = jnp.concatenate([zero, gt], axis=1).astype(BF)
        b2[t, BLOCK:, :] = jnp.concatenate([zero, gt], axis=0).T.astype(BF)
        return 0

    def place_all():
        for d in range(1, NB):
            frm = lax.rem(s + NB - d, NB)
            pltpu.make_async_remote_copy(
                src_ref=gsend.at[s],
                dst_ref=grecv.at[frm],
                send_sem=sg.at[d - 1],
                recv_sem=rg.at[d - 1],
                device_id={"seq": frm},
                device_id_type=MESH,
            ).wait_recv()
        lax.fori_loop(0, NB, place, 0)

    n = 1
    for k in range(4):
        for flow in (0, 1, 2, 3, 4, 5):
            off = (k + 1) if flow % 2 else -(k + 1)
            zmsg(flow, k, off, False).wait_recv()
            if k < 3:
                sent.append(zmsg(flow, k + 1, off, True))
            if flow < 2 and k < 3:
                sent.append(ymsg(off % NZ, y, True))
            if flow == 1 and k == 3:
                sent.append(ymsg(4, y, True))
        for off in [-(k + 1), k + 1][: 2 if k < 3 else 1]:
            compute(block(y, off), n)
            n += 1
        for off in [-k, k][: 2 if k > 0 else 1]:
            ymsg(off % NZ, p, False).wait_recv()
            compute(block(p, off), n)
            n += 1
        if k == 2:
            place_all()
    for c in outs:
        c.wait()
    outs.clear()
    ymsg(4, p, False).wait_recv()
    compute(block(p, 4), n)
    for c in sent:
        c.wait_send()
    for c in outs:
        c.wait()


def gather(x, w, g, pairs):
    vm = pl.BlockSpec(memory_space=pltpu.VMEM)
    anyw = pl.BlockSpec(memory_space=pl.ANY)
    hbm = pl.BlockSpec(memory_space=pltpu.HBM)
    n = NB * BLOCK
    sem = pltpu.SemaphoreType.DMA
    return pl.pallas_call(
        gather_kernel,
        out_shape=(
            jax.ShapeDtypeStruct((NB, BLOCK, D), BF),
            jax.ShapeDtypeStruct((NB, BLOCK, 2 * BLOCK), BF),
            jax.ShapeDtypeStruct((NB, 2 * BLOCK, BLOCK), BF),
            jax.ShapeDtypeStruct((n, BLOCK), BF),
            jax.ShapeDtypeStruct((NB, BLOCK), jnp.int32),
            jax.ShapeDtypeStruct((3 * HD, D), BF),
        ),
        in_specs=[hbm, hbm, hbm, hbm],
        out_specs=(anyw, vm, vm, vm, vm, vm),
        scratch_shapes=[
            pltpu.VMEM((3 * HD, D), BF),
            pltpu.VMEM((BLOCK, D), BF),
            pltpu.VMEM((2, BLOCK), jnp.int32),
            pltpu.VMEM((NB, BLOCK, D), BF),
            pltpu.VMEM((NB, HD, BLOCK), BF),
            pltpu.VMEM((NB, HD, BLOCK), BF),
            sem((6, 4)),
            sem((6, 4)),
            sem((9,)),
            sem((9,)),
            sem((NB - 1,)),
            sem((NB - 1,)),
            sem((NB,)),
            sem((6,)),
            pltpu.SemaphoreType.REGULAR((4,)),
        ],
        compiler_params=pltpu.CompilerParams(
            collective_id=0, has_side_effects=True, vmem_limit_bytes=20 * 1024 * 1024
        ),
        name="gather_project",
    )(x, w, g, pairs)


def scatter_kernel(
    dproj, w, ot, xv,
    att, ng, wg,
    px, zs, zr, ysb, yrb, arecv, dt, dwf, cs, cr, xs, xr, hs, hr, fs, fo, fsib,
    sz, rz, sy, ry, sa, ra, sc, rc, sx, rx, sh, rh, sf, rf,
):
    s, y, z = ring_place()
    p = 1 - y
    up = {"seq": y * NZ + lax.rem(z + 1, NZ)}
    down = {"seq": y * NZ + lax.rem(z + NZ - 1, NZ)}
    across = {"seq": p * NZ + z}
    q = lax.axis_index("clus")
    cx = lax.div(q, NY * CORES)
    ch = lax.rem(lax.div(q, CORES), NY)
    cc = lax.rem(q, CORES)
    sib = {"clus": q + 1 - 2 * cc}

    def xpeer(d):
        return {"clus": lax.rem(cx + d, NX) * (NY * CORES) + ch * CORES + cc}

    def hpeer(d):
        return {"clus": cx * (NY * CORES) + lax.rem(ch + d, NY) * CORES + cc}

    def turn(t, _):
        at = pl.ds(pl.multiple_of(t * BLOCK, BLOCK), BLOCK)
        v = jnp.concatenate([dproj[at, :].astype(F32), jnp.zeros((BLOCK, HD), F32)], axis=1)
        dt[:, at] = v.T[: 3 * HD].astype(BF)
        return 0

    def terms():
        def step(t, _):
            at = pl.ds(pl.multiple_of(t * 256, 256), 256)
            px[:, at] = jnp.dot(dproj[...], w[:, at], preferred_element_type=F32).astype(BF)
            return 0

        lax.fori_loop(0, D // 256, step, 0)
        arecv[s] = ot[s]
        lax.fori_loop(0, NB, turn, 0)

    greet(
        [{"seq": lax.rem(s + d, NB)} for d in range(1, NB)]
        + [sib]
        + [xpeer(d) for d in range(1, NX)]
        + [hpeer(d) for d in range(1, NY)],
        terms,
    )

    def block(col, off):
        return col * NZ + lax.rem(z + off + NZ, NZ)

    def part(col, off, first, rows):
        b = block(col, off)
        return px.at[pl.ds(pl.multiple_of(b * BLOCK + first, QUART), rows), :]

    sent = []

    def rcopy(src, dst, ss, rs, dev):
        return pltpu.make_async_remote_copy(
            src_ref=src, dst_ref=dst, send_sem=ss, recv_sem=rs,
            device_id=dev, device_id_type=MESH,
        )

    def span(flow, k):
        if k == 0:
            return pl.ds(QUART if flow % 2 else 0, QUART)
        return pl.ds(0, HALF)

    def zmsg(flow, k):
        at = span(flow, k)
        src = zs.at[flow, k, at]
        if k == 0 and flow >= 2:
            lo = QUART if flow % 2 else 0
            src = part(p if flow >= 4 else y, 4, HALF + lo, QUART)
        return rcopy(
            src, zr.at[flow, k, at], sz.at[flow, k], rz.at[flow, k],
            down if flow % 2 else up,
        )

    def ymsg(idx):
        src = ysb if idx == 8 else part(p, idx, 0, HALF)
        return rcopy(src, yrb.at[idx], sy.at[idx], ry.at[idx], across)

    def go(c):
        c.start()
        sent.append(c)

    def zstep(flow, k):
        col = p if flow >= 4 else y
        base = 0 if flow < 2 else HALF
        off = (4 - k) * (-1 if flow % 2 else 1)
        lo = QUART if flow % 2 else 0
        if k == 0:
            if flow < 2:
                val = part(col, off, lo, QUART)[...].astype(F32)
                val = val + yrb[off % NZ, lo : lo + QUART, :].astype(F32)
                zs[flow, 0, lo : lo + QUART, :] = val.astype(BF)
        else:
            val = part(col, off, base, HALF)[...].astype(F32)
            if flow < 2:
                val = val + yrb[off % NZ].astype(F32)
            zmsg(flow, k - 1).wait_recv()
            if k == 1:
                zs[flow, 1, QUART - lo : HALF - lo, :] = val[QUART - lo : HALF - lo].astype(BF)
                zs[flow, 1, lo : lo + QUART, :] = (
                    val[lo : lo + QUART] + zr[flow, 0, lo : lo + QUART, :].astype(F32)
                ).astype(BF)
            else:
                zs[flow, k] = (val + zr[flow, k - 1].astype(F32)).astype(BF)
        go(zmsg(flow, k))

    def ysend(off):
        go(ymsg(off % NZ))

    for flow in (4, 5):
        zstep(flow, 0)
    ysend(4)
    for flow in (2, 3):
        zstep(flow, 0)
    ysend(3)
    ysend(-3)
    for d in range(1, NB):
        to = lax.rem(s + d, NB)
        go(rcopy(ot.at[to], arecv.at[s], sa.at[d - 1], ra.at[d - 1], {"seq": to}))

    def wstep(t, _):
        at = pl.ds(pl.multiple_of(t * 256, 256), 256)
        dwf[:, at] = jnp.dot(dt[...], xv[:, at], preferred_element_type=F32)
        return 0

    hrow = 3 * HD // CORES
    mine = pl.ds(pl.multiple_of(cc * hrow, QUART), hrow)
    other = pl.ds(pl.multiple_of((1 - cc) * hrow, QUART), hrow)
    wide = D // NX

    def stage0():
        lax.fori_loop(0, D // 256, wstep, 0)
        cs[...] = dwf[other, :].astype(BF)
        go(rcopy(cs, cr, sc.at[0], rc.at[0], sib))

    def stage1():
        rcopy(cs, cr, sc.at[0], rc.at[0], sib).wait_recv()
        v = dwf[mine, :] + cr[...].astype(F32)
        for t in range(NX):
            xs[t] = v[:, t * wide : (t + 1) * wide].astype(BF)
        xr[cx] = xs[cx]
        for d in range(1, NX):
            go(rcopy(xs.at[lax.rem(cx + d, NX)], xr.at[cx], sx.at[d - 1], rx.at[d - 1], xpeer(d)))

    def stage2():
        for d in range(1, NX):
            frm = lax.rem(cx + NX - d, NX)
            rcopy(xs.at[cx], xr.at[frm], sx.at[d - 1], rx.at[d - 1], xpeer(d)).wait_recv()
        v = xr[0].astype(F32) + xr[1].astype(F32) + xr[2].astype(F32) + xr[3].astype(F32)
        hs[...] = v.astype(BF)
        hr[ch] = v.astype(BF)
        for d in range(1, NY):
            go(rcopy(hs, hr.at[ch], sh.at[d - 1], rh.at[d - 1], hpeer(d)))

    def stage3():
        for d in range(1, NY):
            frm = lax.rem(ch + NY - d, NY)
            rcopy(hs, hr.at[frm], sh.at[d - 1], rh.at[d - 1], hpeer(d)).wait_recv()
        v = hr[0].astype(F32) + hr[1].astype(F32) + hr[2].astype(F32) + hr[3].astype(F32)
        fs[...] = v.astype(BF)
        fo[cx] = v.astype(BF)
        for d in range(1, NX):
            go(rcopy(fs, fo.at[cx], sf.at[d - 1], rf.at[d - 1], xpeer(d)))

    def stage4():
        for d in range(1, NX):
            frm = lax.rem(cx + NX - d, NX)
            rcopy(fs, fo.at[frm], sf.at[d - 1], rf.at[d - 1], xpeer(d)).wait_recv()
        go(rcopy(fo, fsib, sc.at[1], rc.at[1], sib))

    def stage5():
        rcopy(fo, fsib, sc.at[1], rc.at[1], sib).wait_recv()
        for t in range(NX):
            at = pl.ds(t * wide, wide)
            wg[mine, at] = fo[t].astype(F32) * (1.0 / (NX * NY * CORES))
            wg[other, at] = fsib[t].astype(F32) * (1.0 / (NX * NY * CORES))

    def asteps(k):
        if k == 0:
            ymsg(4).wait_recv()
        else:
            ymsg((4 - k) % NZ).wait_recv()
            ymsg((k - 4) % NZ).wait_recv()
        zstep(0, k)
        zstep(1, k)

    def total(flow, col, base):
        val = part(col, 0, base, HALF)[...].astype(F32)
        for f in (flow, flow + 1):
            zmsg(f, 3).wait_recv()
            val = val + zr[f, 3].astype(F32)
        return val

    asteps(0)
    for flow in (4, 5, 2, 3):
        zstep(flow, 1)
    stage0()
    ysend(2)
    ysend(-2)
    asteps(1)
    stage1()
    for flow in (4, 5, 2, 3):
        zstep(flow, 2)
    ysend(1)
    ysend(-1)
    stage2()
    asteps(2)
    for flow in (4, 5, 2, 3):
        zstep(flow, 3)
    ysend(0)
    for d in range(1, NB):
        frm = lax.rem(s + NB - d, NB)
        rcopy(ot.at[s], arecv.at[frm], sa.at[d - 1], ra.at[d - 1], {"seq": frm}).wait_recv()
    for c in range(NB // 2):
        t = jnp.concatenate([arecv[2 * c], arecv[2 * c + 1]], axis=0).astype(F32)
        att[0, :, c * BLOCK : (c + 1) * BLOCK] = t.T.astype(BF)
    stage3()
    asteps(3)
    stage4()
    ysb[...] = total(4, p, HALF).astype(BF)
    go(ymsg(8))
    own_b = total(2, y, HALF)
    ymsg(0).wait_recv()
    ng[0, :HALF, :] = (total(0, y, 0) + yrb[0].astype(F32)).astype(BF)
    stage5()
    ymsg(8).wait_recv()
    ng[0, HALF:, :] = (own_b + yrb[8].astype(F32)).astype(BF)
    for c in sent:
        c.wait_send()


def scatter(dproj, w, ot, xall):
    vm = pl.BlockSpec(memory_space=pltpu.VMEM)
    n = NB * BLOCK
    sem = pltpu.SemaphoreType.DMA
    vmem = pltpu.VMEM
    hrow = 3 * HD // CORES
    wide = D // NX
    return pl.pallas_call(
        scatter_kernel,
        out_shape=(
            jax.ShapeDtypeStruct((1, BLOCK, D), BF),
            jax.ShapeDtypeStruct((1, BLOCK, D), BF),
            jax.ShapeDtypeStruct((3 * HD, D), F32),
        ),
        in_specs=[vm, vm, vm, vm],
        out_specs=(vm, vm, vm),
        scratch_shapes=[
            vmem((n, D), BF),
            vmem((6, 4, HALF, D), BF),
            vmem((6, 4, HALF, D), BF),
            vmem((HALF, D), BF),
            vmem((9, HALF, D), BF),
            vmem((NB, HD, BLOCK), BF),
            vmem((3 * HD, n), BF),
            vmem((3 * HD, D), F32),
            vmem((hrow, D), BF),
            vmem((hrow, D), BF),
            vmem((NX, hrow, wide), BF),
            vmem((NX, hrow, wide), BF),
            vmem((hrow, wide), BF),
            vmem((NY, hrow, wide), BF),
            vmem((hrow, wide), BF),
            vmem((NX, hrow, wide), BF),
            vmem((NX, hrow, wide), BF),
            sem((6, 4)),
            sem((6, 4)),
            sem((9,)),
            sem((9,)),
            sem((NB - 1,)),
            sem((NB - 1,)),
            sem((2,)),
            sem((2,)),
            sem((NX - 1,)),
            sem((NX - 1,)),
            sem((NY - 1,)),
            sem((NY - 1,)),
            sem((NX - 1,)),
            sem((NX - 1,)),
        ],
        compiler_params=pltpu.CompilerParams(
            collective_id=1, has_side_effects=True, vmem_limit_bytes=24 * 1024 * 1024
        ),
        name="scatter_reduce",
    )(dproj, w, ot, xall)


def put_kernel(a, b, c, ao, bo, co, sems):
    copies = [
        pltpu.make_async_copy(src, dst, sems.at[t])
        for t, (src, dst) in enumerate(((c, co), (a, ao), (b, bo)))
    ]
    for copy in copies:
        copy.start()
    for copy in copies:
        copy.wait()


def put(a, b, c):
    vm = pl.BlockSpec(memory_space=pltpu.VMEM)
    hbm = pl.BlockSpec(memory_space=pltpu.HBM)
    return pl.pallas_call(
        put_kernel,
        out_shape=tuple(jax.ShapeDtypeStruct(t.shape, t.dtype) for t in (a, b, c)),
        in_specs=[vm, vm, vm],
        out_specs=(hbm, hbm, hbm),
        scratch_shapes=[pltpu.SemaphoreType.DMA((3,))],
        compiler_params=pltpu.CompilerParams(vmem_limit_bytes=4 * 1024 * 1024),
        name="put",
    )(a, b, c)


def local(node_feats, qkv_weight, block_pairs, grad_out):
    operands = (node_feats, qkv_weight, grad_out, jnp.transpose(block_pairs[0]))
    held = [pltpu.with_memory_space_constraint(t, pltpu.HBM) for t in operands]
    xall, b1, b2, kv, lst, w = gather(*held)
    ot, dproj = attention(lst, b1, b2, kv)
    return put(*scatter(dproj, w, ot, xall.reshape(NB * BLOCK, D)))


def solution(mesh):
    return jax.shard_map(
        local,
        mesh=mesh,
        in_specs=(
            P("clus", "seq", None),
            P("seq", None),
            P("clus", None, None),
            P("clus", "seq", None),
        ),
        out_specs=(P("clus", "seq", None), P("clus", "seq", None), P("seq", None)),
        check_vma=False,
    )
```
